128 devices in a mesh: layer: 16 (over y, z_hi, core), feat: 8 (over x, z_lo).
Axes of the slice: x: 4, y: 4, z: 4 (z_hi: 2, z_lo: 2; z = z_hi * 2 + z_lo), core: 2. Of those that a mesh axis runs over, the one named last changes fastest.
Arguments:
- tokens_in: bfloat16 [512, 4096], P('feat', 'layer'), may hold values from -6 to 6
- targets: bfloat16 [512, 4096], P('feat', 'layer'), may hold values from -6 to 6
- enc_weight: bfloat16 [2048, 131072], P(None, ('layer', 'feat')), may hold values from -0.125 to 0.125
- enc_bias: float32 [131072], P(('layer', 'feat')), may hold values from -1 to 0.5
- dec_weight: bfloat16 [2, 131072, 2048], P(None, ('layer', 'feat')), may hold values from -0.0234375 to 0.0234375
Outputs:
- recon_error: float32 [512, 4096], P('feat', 'layer')
- mean_square: float32 [], replicated
- enc_grad: bfloat16 [2048, 131072], P(None, ('layer', 'feat'))
- bias_grad: float32 [131072], P(('layer', 'feat'))
- dec_grad: bfloat16 [2, 131072, 2048], P(None, ('layer', 'feat'))
The draws below stay inside these ranges and needn't reach their ends.
All inputs are finite; a program needn't handle non-finite values.
Results may differ from the reference program's by a relative error of at most 0.02.
Values may be sent and summed in bfloat16 or wider, within the bound.
A program may use at most 128 MiB of HBM per device.

```python
import jax
import jax.numpy as jnp

D = 2048
LAYERS = 2
TOK = 512
FEATS = 65536


def block_levels(key, dims, pieces, least, top_value):
    def one(axis_at, blocks):
        draws = jax.random.uniform(jax.random.fold_in(jax.random.fold_in(key, 6), axis_at), (blocks,), jnp.float32, least / len(pieces), top_value / len(pieces))
        return jnp.repeat(jnp.exp(draws), dims[axis_at] // blocks).reshape((-1,) + (1,) * (len(dims) - axis_at - 1))

    gain = one(*pieces[0])
    for cut in pieces[1:]:
        gain = gain * one(*cut)
    return gain


def bell_draw(own_key, dims, deviation, reach, split=(), dtype=jnp.bfloat16):
    values = jax.random.normal(own_key, dims, jnp.float32) * deviation
    if len(split) > 0:
        values = block_levels(own_key, dims, split, -0.22, 0.18) * values
    return jnp.clip(values, min=-reach, max=reach).astype(dtype)


def setup_inputs(seed: int = 0) -> dict:
    keys = jax.random.split(jax.random.key(seed), 6)
    tokens_in = bell_draw(keys[0], (TOK, LAYERS * D), 1.0, 6.0, ((0, 8), (1, 16)))
    targets = bell_draw(keys[1], (TOK, LAYERS * D), 1.0, 6.0, ((0, 8), (1, 16)))
    enc_weight = bell_draw(keys[2], (D, LAYERS * FEATS), D ** -0.5, 0.125, ((1, 128),))
    enc_bias = jnp.clip(-1.0 + 1.5 * jax.random.uniform(keys[3], (LAYERS * FEATS,), jnp.float32) ** block_levels(keys[3], (LAYERS * FEATS,), ((0, 128),), -0.2, 0.2), -1.0, 0.5)
    dec_weight = bell_draw(keys[4], (LAYERS, LAYERS * FEATS, D), FEATS ** -0.5, 0.0234375, ((1, 128),))
    return {"tokens_in": tokens_in, "targets": targets, "enc_weight": enc_weight, "enc_bias": enc_bias, "dec_weight": dec_weight}


loss_scale = 64.0


def reference(tokens_in, targets, enc_weight, enc_bias, dec_weight):
    layer_inputs, pre_acts, features = [], [], []
    for source in range(LAYERS):
        cols_in = tokens_in[:, source * D:(source + 1) * D]
        weights = enc_weight[:, source * FEATS:(source + 1) * FEATS]
        pre_act = jnp.dot(cols_in, weights, preferred_element_type=jnp.float32) + enc_bias[source * FEATS:(source + 1) * FEATS]
        layer_inputs.append(cols_in)
        pre_acts.append(pre_act)
        features.append(jnp.maximum(pre_act, 0.0).astype(jnp.bfloat16))
    errors = []
    for target in range(LAYERS):
        rebuilt = jnp.zeros((TOK, D), jnp.float32)
        for source in range(target + 1):
            rows = dec_weight[target - source, source * FEATS:(source + 1) * FEATS]
            rebuilt = rebuilt + jnp.dot(features[source], rows, preferred_element_type=jnp.float32)
        errors.append(rebuilt - targets[:, target * D:(target + 1) * D].astype(jnp.float32))
    recon_error = jnp.concatenate(errors, 1)
    mean_square = jnp.sum(recon_error * recon_error) / (LAYERS * TOK * D)
    scaled = ((loss_scale / TOK) * recon_error).astype(jnp.bfloat16)
    enc_parts, bias_parts = [], []
    dec_parts = [[] for offset in range(LAYERS)]
    for source in range(LAYERS):
        feature_grad = jnp.zeros((TOK, FEATS), jnp.float32)
        for offset in range(LAYERS):
            target = source + offset
            if target < LAYERS:
                grad_block = scaled[:, target * D:(target + 1) * D]
                rows = dec_weight[offset, source * FEATS:(source + 1) * FEATS]
                dec_parts[offset].append(jnp.dot(features[source].T, grad_block, preferred_element_type=jnp.float32).astype(jnp.bfloat16))
                feature_grad = feature_grad + jnp.dot(grad_block, rows.T, preferred_element_type=jnp.float32)
            else:
                dec_parts[offset].append(jnp.zeros((FEATS, D), jnp.bfloat16))
        preact_grad = jnp.where(pre_acts[source] > 0.0, feature_grad, 0.0).astype(jnp.bfloat16)
        enc_parts.append(jnp.dot(layer_inputs[source].T, preact_grad, preferred_element_type=jnp.float32).astype(jnp.bfloat16))
        bias_parts.append(jnp.sum(preact_grad.astype(jnp.float32), 0))
    enc_grad = jnp.concatenate(enc_parts, 1)
    bias_grad = jnp.concatenate(bias_parts, 0)
    dec_grad = jnp.stack([jnp.concatenate(dec_parts[offset], 0) for offset in range(LAYERS)], 0)
    return recon_error, mean_square, enc_grad, bias_grad, dec_grad
```

```python
import jax
import jax.numpy as jnp
from jax import lax
from jax.experimental import pallas as pl
from jax.experimental.pallas import tpu as pltpu
from jax.sharding import PartitionSpec as P

D = 2048
LAYERS = 2
TOK = 512
SHARD = 1024
ROWS = 64
COLS = 256
LOSS_SCALE = 64.0
MESH = pl.DeviceIdType.MESH
BF16 = jnp.bfloat16
F32 = jnp.float32


def place(x, y, z, core):
    return (y * 4 + lax.div(z, 2) * 2 + core, x * 2 + lax.rem(z, 2))


def block_at(core, z, x):
    return z * (1 - core) + x * core, x * (1 - core) + z * core


def column_block(ref, lead, y, z_high, core):
    pieces = []
    for x in range(4):
        for z_low in range(2):
            big, small = block_at(core, z_high * 2 + z_low, x)
            pieces.append(ref[(*lead, y, core, big, small)])
    return jnp.concatenate(pieces, 0)


def all_columns(ref, lead):
    return jnp.concatenate(
        [column_block(ref, lead, m // 4, m // 2 % 2, m % 2) for m in range(8)], 1
    )


def add_into(ref, other):
    ref[...] = (ref[...].astype(F32) + other[...].astype(F32)).astype(BF16)


K_TOK_Y = 0
K_TOK = 1
K_PART = 14
K_RS_BIG = 16
K_RS_SMALL = 28
K_RS_Y = 40
K_CROSS = 42
K_S_Y = 43
K_S_CROSS = 44
K_S_FWD = 45
K_S = 46
K_MS = 72
K_COUNT = 79


def step_kernel(
    tok, tgt, enc, bias, dec,
    rerr, msq, gt_out, ft_out, s_out, pg_out, bg,
    encv, decv, g, pre, feat, p, rc, big_in, r1, small_in, r2, y_in, cross_in, cross_out,
    total, s, fg, gt, ft, pg, ms_in, ms_own, send_sem, recv_sem, local_sem,
):
    me_layer = lax.axis_index("layer")
    me_feat = lax.axis_index("feat")
    core = lax.rem(me_layer, 2)
    y = lax.div(me_layer, 4)
    x = lax.div(me_feat, 2)
    z = lax.rem(lax.div(me_layer, 2), 2) * 2 + lax.rem(me_feat, 2)
    yb = lax.rem(y, 2)
    first_layer = y < 2
    second_layer = y >= 2

    partner = place(x, y, z, 1 - core)
    y_pair = place(x, y + 1 - 2 * yb, z, core)
    y_cross = place(x, 3 - y, z, core)
    x_right, x_left = lax.rem(x + 1, 4), lax.rem(x + 3, 4)
    z_right, z_left = lax.rem(z + 1, 4), lax.rem(z + 3, 4)

    def big_place(step):
        return place(
            lax.rem(x + core * step, 4), y, lax.rem(z + (1 - core) * step, 4), core
        )

    def small_place(step):
        return place(
            lax.rem(x + (1 - core) * step, 4), y, lax.rem(z + core * step, 4), core
        )

    big_pos, small_pos = block_at(core, z, x)
    big_ring = (big_pos, big_place(1), big_place(3))
    small_ring = (small_pos, small_place(1), small_place(3))

    pending = []

    def send(src, dst, number, device):
        return pltpu.make_async_remote_copy(
            src_ref=src,
            dst_ref=dst,
            send_sem=send_sem.at[number],
            recv_sem=recv_sem.at[number],
            device_id=device,
            device_id_type=MESH,
        )

    enc_copy = pltpu.make_async_copy(enc, encv, local_sem.at[0])
    dec_copy = pltpu.make_async_copy(dec, decv, local_sem.at[1])
    enc_copy.start()
    dec_copy.start()

    barrier = pltpu.get_barrier_semaphore()
    for device in (
        partner,
        y_pair,
        y_cross,
        place(x_right, y, z, core),
        place(x_left, y, z, core),
        place(x, y, z_right, core),
        place(x, y, z_left, core),
    ):
        pl.semaphore_signal(barrier, inc=1, device_id=device, device_id_type=MESH)
    pl.semaphore_wait(barrier, 7)

    def ring_copies(ref_of, ring, number):
        pos, right, left = ring
        own = ref_of(slice(None), pos)
        from_left = ref_of(0, lax.rem(pos + 3, 4))
        from_right = ref_of(1, lax.rem(pos + 1, 4))
        return (
            send(own, own, number, right),
            send(own, own, number + 1, left),
            send(from_left, from_left, number + 2, right),
            send(from_right, from_right, number + 3, left),
        )

    def gather_pieces(buf, t, number):
        small = ring_copies(
            lambda half, i: buf.at[t, half, core, big_pos, i], small_ring, number
        )
        large = ring_copies(lambda half, i: buf.at[t, half, core, i], big_ring, number + 4)
        whole = slice(None)
        opposite = lax.rem(big_pos + 2, 4)
        shared = []
        for half, i in (
            (whole, big_pos),
            (whole, lax.rem(big_pos + 3, 4)),
            (whole, lax.rem(big_pos + 1, 4)),
            (0, opposite),
            (1, opposite),
        ):
            ref = buf.at[t, half, core, i]
            shared.append(send(ref, ref, number + 8 + len(shared), partner))

        class Pieces:
            def small_start(self):
                small[0].start()
                small[1].start()

            def small_mid(self):
                small[0].wait_recv()
                small[2].start()
                small[1].wait_recv()
                small[3].start()

            def small_end(self):
                small[2].wait_recv()
                small[3].wait_recv()

            def big_start(self):
                large[0].start()
                large[1].start()
                shared[0].start()

            def big_mid(self):
                large[0].wait_recv()
                large[2].start()
                large[1].wait_recv()
                large[3].start()
                shared[1].start()
                shared[2].start()

            def big_end(self):
                large[2].wait_recv()
                shared[3].start()
                large[3].wait_recv()
                shared[4].start()

            def shared_end(self):
                for copy in shared:
                    copy.wait_recv()

            def drain(self):
                for copy in (*small, *large, *shared):
                    copy.wait_send()

        return Pieces()

    g[0, yb, core, big_pos, small_pos] = tok[...]
    own = g.at[0, yb, core, big_pos, small_pos]
    tok_y = send(own, own, K_TOK_Y, y_pair)
    tok_y.start()
    tok_y.wait_recv()
    tokens = gather_pieces(g, 0, K_TOK)
    tokens.small_start()
    tokens.small_mid()
    tokens.small_end()
    tokens.big_start()
    tokens.big_mid()
    tokens.big_end()
    tokens.shared_end()

    enc_copy.wait()

    @pl.loop(0, 4)
    def _(n):
        cols = pl.ds(pl.multiple_of(n * 256, 256), 256)
        act = (
            jnp.dot(all_columns(g, (0,)), encv[:, cols], preferred_element_type=F32)
            + bias[:, cols]
        )
        pre[:, cols] = act
        feat[:, cols] = jnp.maximum(act, 0.0).astype(BF16)

    dec_copy.wait()

    def decode(t, to_core):
        @pl.loop(0, 4)
        def _(i):
            to_y, z_high = lax.div(i, 2), lax.rem(i, 2)
            first = pl.multiple_of((to_y * 4 + z_high * 2 + to_core) * 256, 256)
            value = jnp.dot(
                feat[...], decv[t, :, pl.ds(first, 256)], preferred_element_type=F32
            ).astype(BF16)
            for to_x in range(4):
                for z_low in range(2):
                    big, small = block_at(to_core, z_high * 2 + z_low, to_x)
                    at = (to_x * 2 + z_low) * ROWS
                    p[t, to_y, to_core, big, small] = value[at : at + ROWS]

    def part_copy(t):
        return send(p.at[t, :, 1 - core], rc.at[t], K_PART + t, partner)

    def part_add(t):
        part_copy(t).wait_recv()

        @pl.loop(0, 8)
        def _(i):
            h, b = lax.div(i, 4), lax.rem(i, 4)
            add_into(p.at[t, h, core, b], rc.at[t, h, b])

    def scatter_pieces(q, bufs, ring, number):
        pos, right, left = ring
        at_right, at_left, opposite = (
            lax.rem(pos + 1, 4),
            lax.rem(pos + 3, 4),
            lax.rem(pos + 2, 4),
        )
        copies = (
            send(q(0, opposite), bufs(0), number, right),
            send(q(1, opposite), bufs(1), number + 1, left),
            send(q(1, at_right), bufs(2), number + 2, right),
            send(q(0, at_left), bufs(3), number + 3, left),
            send(q(0, at_right), bufs(4), number + 4, right),
            send(q(1, at_left), bufs(5), number + 5, left),
        )

        class Pieces:
            def start(self):
                for copy in copies[:4]:
                    copy.start()

            def mid(self):
                copies[0].wait_recv()
                add_into(q(0, at_right), bufs(0))
                copies[4].start()
                copies[1].wait_recv()
                add_into(q(1, at_left), bufs(1))
                copies[5].start()

            def end(self, out):
                copies[3].wait_recv()
                copies[4].wait_recv()
                out[0] = (
                    q(0, pos)[...].astype(F32)
                    + bufs(3)[...].astype(F32)
                    + bufs(4)[...].astype(F32)
                ).astype(BF16)
                copies[2].wait_recv()
                copies[5].wait_recv()
                out[1] = (
                    q(1, pos)[...].astype(F32)
                    + bufs(2)[...].astype(F32)
                    + bufs(5)[...].astype(F32)
                ).astype(BF16)

            def drain(self):
                for copy in copies:
                    copy.wait_send()

        return Pieces()

    def big_scatter(t):
        return scatter_pieces(
            lambda h, i: p.at[t, h, core, i],
            lambda k: big_in.at[t, k],
            big_ring,
            K_RS_BIG + 6 * t,
        )

    def small_scatter(t):
        return scatter_pieces(
            lambda h, i: r1.at[t, h, i],
            lambda k: small_in.at[t, k],
            small_ring,
            K_RS_SMALL + 6 * t,
        )

    def y_copy(t):
        away = 1 - yb if t == 0 else yb
        return send(r2.at[t, away], y_in.at[t], K_RS_Y + t, y_pair)

    def cross_copy():
        return send(cross_out, cross_in, K_CROSS, y_cross)

    def part(t):
        decode(t, 1 - core)
        part_copy(t).start()

    @pl.when(first_layer)
    def _():
        part(1)
        decode(1, core)
        part_add(1)
        big_scatter(1).start()

    part(0)

    @pl.when(first_layer)
    def _():
        big_scatter(1).mid()

    decode(0, core)
    part_add(0)
    big_scatter(0).start()

    @pl.when(first_layer)
    def _():
        big_scatter(1).end(r1.at[1])
        small_scatter(1).start()

    big_scatter(0).mid()

    @pl.when(first_layer)
    def _():
        small_scatter(1).mid()

    big_scatter(0).end(r1.at[0])
    small_scatter(0).start()

    @pl.when(first_layer)
    def _():
        small_scatter(1).end(r2.at[1])
        y_copy(1).start()

    small_scatter(0).mid()

    @pl.when(first_layer)
    def _():
        y_copy(1).wait_recv()
        cross_out[...] = (
            r2[1, 1 - yb].astype(F32) + y_in[1].astype(F32)
        ).astype(BF16)
        cross_copy().start()

    small_scatter(0).end(r2.at[0])
    y_copy(0).start()
    y_copy(0).wait_recv()
    total[...] = r2[0, yb].astype(F32) + y_in[0].astype(F32)

    @pl.when(second_layer)
    def _():
        cross_copy().wait_recv()
        total[...] = total[...] + cross_in[...].astype(F32)

    error = total[...] - tgt[...].astype(F32)
    rerr[...] = error
    s[0, yb, core, big_pos, small_pos] = (LOSS_SCALE / TOK * error).astype(BF16)
    own_s = s.at[0, yb, core, big_pos, small_pos]
    s_y = send(own_s, own_s, K_S_Y, y_pair)
    s_y.start()
    s_cross = send(own_s, s.at[1, yb, core, big_pos, small_pos], K_S_CROSS, y_cross)

    @pl.when(second_layer)
    def _():
        s_cross.start()

    squares = error * error
    tile = jnp.zeros((8, 128), F32)
    for i in range(8):
        for j in range(2):
            tile = tile + squares[i * 8 : i * 8 + 8, j * 128 : j * 128 + 128]
    ms_own[0] = tile

    ms_places = (
        partner,
        place(x + 1 - 2 * lax.rem(x, 2), y, z, core),
        place(3 - x, y, z, core),
        place(x, y, z + 1 - 2 * lax.rem(z, 2), core),
        place(x, y, 3 - z, core),
        y_pair,
        y_cross,
    )

    def ms_copy(i):
        return send(ms_own.at[i], ms_in.at[i], K_MS + i, ms_places[i])

    def ms_step(i):
        ms_copy(i).wait_recv()
        ms_own[i + 1] = ms_own[i] + ms_in[i]
        if i < 6:
            ms_copy(i + 1).start()

    ms_copy(0).start()

    def feature_grad(t, n):
        rows = pl.ds(pl.multiple_of(n * 256, 256), 256)
        value = lax.dot_general(
            all_columns(s, (t,)),
            decv[t, rows, :],
            (((1,), (1,)), ((), ())),
            preferred_element_type=F32,
        )
        if t == 0:
            fg[:, rows] = value
        else:
            fg[:, rows] = fg[:, rows] + value

    s0 = gather_pieces(s, 0, K_S)
    s1 = gather_pieces(s, 1, K_S + 13)
    got = s.at[1, 1 - yb, core, big_pos, small_pos]
    s_fwd = send(got, got, K_S_FWD, y_pair)

    s_y.wait_recv()
    s0.small_start()

    @pl.when(first_layer)
    def _():
        s_cross.wait_recv()
        s_fwd.start()

    ms_step(0)
    s0.small_mid()

    @pl.when(first_layer)
    def _():
        s_fwd.wait_recv()
        s1.small_start()

    ms_step(1)
    s0.small_end()
    s0.big_start()
    ms_step(2)

    @pl.when(first_layer)
    def _():
        s1.small_mid()

    ms_step(3)

    @pl.when(first_layer)
    def _():
        s1.small_end()
        s1.big_start()

    ms_step(4)
    s0.big_mid()
    ms_step(5)
    s0.big_end()
    s0.shared_end()
    s_store0 = pltpu.make_async_copy(s.at[0], s_out.at[0], local_sem.at[2])
    s_store0.start()
    ms_step(6)
    msq[0, 0] = jnp.sum(ms_own[7]) / (LAYERS * TOK * D)

    @pl.loop(0, 2)
    def _(n):
        feature_grad(0, n)

    @pl.when(first_layer)
    def _():
        s1.big_mid()

    @pl.loop(2, 4)
    def _(n):
        feature_grad(0, n)

    s_store1 = pltpu.make_async_copy(s.at[1], s_out.at[1], local_sem.at[3])

    @pl.when(first_layer)
    def _():
        s1.big_end()
        s1.shared_end()
        s_store1.start()

        @pl.loop(0, 4)
        def _(n):
            feature_grad(1, n)

    @pl.loop(0, 4)
    def _(n):
        cols = pl.ds(pl.multiple_of(n * 256, 256), 256)
        grad = jnp.where(pre[:, cols] > 0.0, fg[:, cols], 0.0).astype(BF16)
        pg[:, cols] = grad
        bg[:, cols] = jnp.sum(grad.astype(F32), 0, keepdims=True)

    pg_store = pltpu.make_async_copy(pg, pg_out, local_sem.at[4])
    pg_store.start()

    @pl.loop(0, 4)
    def _(n):
        cols = pl.ds(pl.multiple_of(n * 256, 256), 256)
        ft[cols, :] = feat[:, cols].T

    ft_store = pltpu.make_async_copy(ft, ft_out, local_sem.at[5])
    ft_store.start()

    @pl.loop(0, 8)
    def _(m):
        block = column_block(g, (0,), lax.div(m, 4), lax.rem(lax.div(m, 2), 2), lax.rem(m, 2))
        gt[pl.ds(pl.multiple_of(m * 256, 256), 256), :] = block.T

    gt_store = pltpu.make_async_copy(gt, gt_out, local_sem.at[6])
    gt_store.start()

    tok_y.wait_send()
    tokens.drain()
    part_copy(0).wait_send()
    big_scatter(0).drain()
    small_scatter(0).drain()
    y_copy(0).wait_send()
    s_y.wait_send()
    s0.drain()
    for i in range(7):
        ms_copy(i).wait_send()

    @pl.when(first_layer)
    def _():
        part_copy(1).wait_send()
        big_scatter(1).drain()
        small_scatter(1).drain()
        y_copy(1).wait_send()
        cross_copy().wait_send()
        s_fwd.wait_send()
        s1.drain()
        s_store1.wait()

    @pl.when(second_layer)
    def _():
        s_cross.wait_send()

    s_store0.wait()
    pg_store.wait()
    ft_store.wait()
    gt_store.wait()


def weight_grads_kernel(gt, ft, s, pg, dec_grad, enc_grad):
    i = pl.program_id(0)
    first_layer = lax.axis_index("layer") < 8

    def dec_block(t):
        m = i - 8 * t
        block = column_block(
            s, (t,), lax.div(m, 4), lax.rem(lax.div(m, 2), 2), lax.rem(m, 2)
        )
        dec_grad[0] = jnp.dot(ft[...], block, preferred_element_type=F32).astype(BF16)

    @pl.when(i < 8)
    def _():
        dec_block(0)

    @pl.when((i >= 8) & (i < 16) & first_layer)
    def _():
        dec_block(1)

    @pl.when((i >= 8) & (i < 16) & jnp.logical_not(first_layer))
    def _():
        dec_grad[...] = jnp.zeros_like(dec_grad)

    @pl.when(i >= 16)
    def _():
        rows = pl.ds(pl.multiple_of((i - 16) * 256, 256), 256)
        enc_grad[...] = jnp.dot(
            gt[rows, :], pg[...], preferred_element_type=F32
        ).astype(BF16)


def on_device(tokens_in, targets, enc_weight, enc_bias, dec_weight):
    vmem = pl.BlockSpec(memory_space=pltpu.VMEM)
    anywhere = pl.BlockSpec(memory_space=pl.ANY)
    shape = jax.ShapeDtypeStruct
    blocks = (2, 2, 4, 4, ROWS, COLS)
    rerr, msq, gt, ft, s, pg, bg = pl.pallas_call(
        step_kernel,
        out_shape=(
            shape((ROWS, COLS), F32),
            shape((1, 1), F32),
            shape((D, TOK), BF16),
            shape((SHARD, TOK), BF16),
            shape((2, *blocks), BF16),
            shape((TOK, SHARD), BF16),
            shape((1, SHARD), F32),
        ),
        in_specs=[vmem, vmem, anywhere, vmem, anywhere],
        out_specs=(
            vmem,
            pl.BlockSpec(memory_space=pltpu.SMEM),
            anywhere,
            anywhere,
            anywhere,
            anywhere,
            vmem,
        ),
        scratch_shapes=[
            pltpu.VMEM((D, SHARD), BF16),
            pltpu.VMEM((2, SHARD, D), BF16),
            pltpu.VMEM((1, *blocks), BF16),
            pltpu.VMEM((TOK, SHARD), F32),
            pltpu.VMEM((TOK, SHARD), BF16),
            pltpu.VMEM((2, *blocks), BF16),
            pltpu.VMEM((2, 2, 4, 4, ROWS, COLS), BF16),
            pltpu.VMEM((2, 6, 4, ROWS, COLS), BF16),
            pltpu.VMEM((2, 2, 4, ROWS, COLS), BF16),
            pltpu.VMEM((2, 6, ROWS, COLS), BF16),
            pltpu.VMEM((2, 2, ROWS, COLS), BF16),
            pltpu.VMEM((2, ROWS, COLS), BF16),
            pltpu.VMEM((ROWS, COLS), BF16),
            pltpu.VMEM((ROWS, COLS), BF16),
            pltpu.VMEM((ROWS, COLS), F32),
            pltpu.VMEM((2, *blocks), BF16),
            pltpu.VMEM((TOK, SHARD), F32),
            pltpu.VMEM((D, TOK), BF16),
            pltpu.VMEM((SHARD, TOK), BF16),
            pltpu.VMEM((TOK, SHARD), BF16),
            pltpu.VMEM((7, 8, 128), F32),
            pltpu.VMEM((8, 8, 128), F32),
            pltpu.SemaphoreType.DMA((K_COUNT,)),
            pltpu.SemaphoreType.DMA((K_COUNT,)),
            pltpu.SemaphoreType.DMA((7,)),
        ],
        compiler_params=pltpu.CompilerParams(
            collective_id=0, has_side_effects=True, vmem_limit_bytes=56 * 2**20
        ),
        name="step",
    )(tokens_in, targets, enc_weight, enc_bias.reshape(1, SHARD), dec_weight)

    dec_grad, enc_grad = pl.pallas_call(
        weight_grads_kernel,
        grid=(24,),
        out_shape=(shape((2, SHARD, D), BF16), shape((D, SHARD), BF16)),
        in_specs=[vmem] * 4,
        out_specs=(
            pl.BlockSpec(
                (1, SHARD, 256),
                lambda i: (jnp.minimum(i, 15) // 8, 0, jnp.minimum(i, 15) % 8),
            ),
            pl.BlockSpec((256, SHARD), lambda i: (jnp.maximum(i - 16, 0), 0)),
        ),
        compiler_params=pltpu.CompilerParams(vmem_limit_bytes=40 * 2**20),
        name="weight_grads",
    )(gt, ft, s, pg)
    return (rerr, msq.reshape(()), enc_grad, bg.reshape(SHARD), dec_grad)


def solution(mesh):
    placed = (
        P("feat", "layer"),
        P("feat", "layer"),
        P(None, ("layer", "feat")),
        P(("layer", "feat")),
        P(None, ("layer", "feat"), None),
    )
    return jax.shard_map(
        on_device,
        mesh=mesh,
        in_specs=placed,
        out_specs=(
            P("feat", "layer"),
            P(),
            P(None, ("layer", "feat")),
            P(("layer", "feat")),
            P(None, ("layer", "feat"), None),
        ),
        check_vma=False,
    )
```

```python
import jax
import jax.numpy as jnp
from jax import lax
from jax.experimental import pallas as pl
from jax.experimental.pallas import tpu as pltpu
from jax.sharding import PartitionSpec as P

D = 2048
LAYERS = 2
TOK = 512
SHARD = 1024
ROWS = 64
COLS = 256
LOSS_SCALE = 64.0
MESH = pl.DeviceIdType.MESH
BF16 = jnp.bfloat16
F32 = jnp.float32


def place(x, y, z, core):
    return (y * 4 + lax.div(z, 2) * 2 + core, x * 2 + lax.rem(z, 2))


def block_at(half, z, x):
    return z * (1 - half) + x * half, x * (1 - half) + z * half


def column_block(ref, lead, half, z_high, core):
    pieces = []
    for x in range(4):
        for z_low in range(2):
            big, small = block_at(half, z_high * 2 + z_low, x)
            pieces.append(ref[(*lead, half, core, big, small)])
    return jnp.concatenate(pieces, 0)


def all_columns(ref, lead):
    return jnp.concatenate(
        [column_block(ref, lead, m // 4, m // 2 % 2, m % 2) for m in range(8)], 1
    )


class Numbers:
    def __init__(self):
        self.count = 0

    def take(self, *dims):
        if not dims:
            self.count += 1
            return self.count - 1
        return [self.take(*dims[1:]) for _ in range(dims[0])]


NUMBERS = Numbers()
K_GATHER = [
    dict(
        y=NUMBERS.take(),
        small=NUMBERS.take(2, 4),
        big=NUMBERS.take(2, 4),
        shared=NUMBERS.take(2, 4),
    )
    for _ in range(3)
]
K_PART = NUMBERS.take(2, 2)
K_BIG = NUMBERS.take(2, 2, 4)
K_SMALL = NUMBERS.take(2, 2, 4)
K_Y = NUMBERS.take()
K_CROSS = NUMBERS.take(2)
K_BACK = NUMBERS.take(2)
K_SQUARE = NUMBERS.take(4, 4)
K_COUNT = NUMBERS.count


def step_kernel(
    tok, tgt, enc, bias, dec,
    rerr, msq, gt_out, ft_out, s_out, pg_out, bg,
    encv, decv, g, pre, feat, p, rc, big_in, r1, small_in, r2, y_in, cross_in,
    s, fg, gt, ft, pg, squares_in, squares_own, send_sem, recv_sem, local_sem,
):
    me_layer = lax.axis_index("layer")
    me_feat = lax.axis_index("feat")
    core = lax.rem(me_layer, 2)
    y = lax.div(me_layer, 4)
    x = lax.div(me_feat, 2)
    z = lax.rem(lax.div(me_layer, 2), 2) * 2 + lax.rem(me_feat, 2)
    yb = lax.rem(y, 2)
    first_layer = y < 2
    second_layer = y >= 2

    def turn(v, step):
        return lax.rem(v + step, 4)

    partner = place(x, y, z, 1 - core)
    y_pair = place(x, y + 1 - 2 * yb, z, core)
    x_peers = [None] + [place(turn(x, o), y, z, core) for o in (1, 2, 3)]
    y_peers = [None] + [place(x, turn(y, o), z, core) for o in (1, 2, 3)]
    z_peers = [None] + [place(x, y, turn(z, o), core) for o in (1, 2, 3)]
    big_pos, small_pos = (z, x), (x, z)
    big_peers, small_peers = (z_peers, x_peers), (x_peers, z_peers)
    HALVES = (0, 1)
    OFFSETS = (1, 3, 2)

    def send(src, dst, number, device):
        return pltpu.make_async_remote_copy(
            src_ref=src,
            dst_ref=dst,
            send_sem=send_sem.at[number],
            recv_sem=recv_sem.at[number],
            device_id=device,
            device_id_type=MESH,
        )

    sent = []
    sent_first = []

    def go(log, make, *args):
        make(*args).start()
        log.append((make, args))

    def drain(log):
        for make, args in log:
            make(*args).wait_send()

    enc_copy = pltpu.make_async_copy(enc, encv, local_sem.at[0])
    dec_copy = pltpu.make_async_copy(dec, decv, local_sem.at[1])
    enc_copy.start()
    dec_copy.start()

    barrier = pltpu.get_barrier_semaphore()
    for device in (partner, *x_peers[1:], *y_peers[1:], *z_peers[1:]):
        pl.semaphore_signal(barrier, inc=1, device_id=device, device_id_type=MESH)
    pl.semaphore_wait(barrier, 10)

    class Gather:
        def __init__(self, buf, t, numbers, log):
            self.buf, self.t, self.numbers, self.log = buf, t, numbers, log

        def piece(self, half):
            return self.buf.at[self.t, half, core, big_pos[half], small_pos[half]]

        def chunk(self, half, i):
            return self.buf.at[self.t, half, core, i]

        def small_copy(self, half, o):
            ref = self.piece(half)
            return send(ref, ref, self.numbers["small"][half][o], small_peers[half][o])

        def big_copy(self, half, o):
            ref = self.chunk(half, big_pos[half])
            return send(ref, ref, self.numbers["big"][half][o], big_peers[half][o])

        def shared_copy(self, half, o):
            ref = self.chunk(half, turn(big_pos[half], 4 - o))
            return send(ref, ref, self.numbers["shared"][half][o], partner)

        def small(self, half):
            for o in OFFSETS:
                go(self.log, self.small_copy, half, o)

        def big(self, half):
            for o in OFFSETS:
                self.small_copy(half, o).wait_recv()
            for o in OFFSETS:
                go(self.log, self.big_copy, half, o)
            go(self.log, self.shared_copy, half, 0)

        def share(self, half):
            for o in OFFSETS:
                self.big_copy(half, o).wait_recv()
                go(self.log, self.shared_copy, half, o)

        def done(self):
            for half in HALVES:
                for o in range(4):
                    self.shared_copy(half, o).wait_recv()

    def own_half(buf, value):
        big, small = block_at(yb, z, x)
        buf[0, yb, core, big, small] = value
        return buf.at[0, yb, core, big, small]

    def by_half(fn):
        @pl.when(yb == 0)
        def _():
            fn(0, 1)

        @pl.when(yb == 1)
        def _():
            fn(1, 0)

    own = own_half(g, tok[...])
    tok_y = send(own, own, K_GATHER[2]["y"], y_pair)
    go(sent, lambda: tok_y)
    unlogged = []

    def first_hops(gather, y_copy):
        def run(mine, other):
            gather.small(mine)
            y_copy.wait_recv()
            gather.small(other)

        return run

    tokens = Gather(g, 0, K_GATHER[2], unlogged)
    by_half(first_hops(tokens, tok_y))

    def big_hops(gather):
        def run(mine, other):
            gather.big(mine)
            gather.big(other)

        return run

    by_half(big_hops(tokens))

    def share_hops(gather):
        def run(mine, other):
            gather.share(mine)
            gather.share(other)

        return run

    by_half(share_hops(tokens))
    tokens.done()

    enc_copy.wait()

    @pl.loop(0, 4)
    def _(n):
        cols = pl.ds(pl.multiple_of(n * 256, 256), 256)
        act = (
            jnp.dot(all_columns(g, (0,)), encv[:, cols], preferred_element_type=F32)
            + bias[:, cols]
        )
        pre[:, cols] = act
        feat[:, cols] = jnp.maximum(act, 0.0).astype(BF16)

    dec_copy.wait()

    def decode(t, to_core, half):
        @pl.loop(0, 2)
        def _(z_high):
            first = pl.multiple_of((half * 4 + z_high * 2 + to_core) * 256, 256)
            value = jnp.dot(
                feat[...], decv[t, :, pl.ds(first, 256)], preferred_element_type=F32
            ).astype(BF16)
            for to_x in range(4):
                for z_low in range(2):
                    big, small = block_at(half, z_high * 2 + z_low, to_x)
                    at = (to_x * 2 + z_low) * ROWS
                    p[t, half, to_core, big, small] = value[at : at + ROWS]

    def part_copy(t, half):
        return send(p.at[t, half, 1 - core], rc.at[t, half], K_PART[t][half], partner)

    def part_add(t, half):
        part_copy(t, half).wait_recv()

        @pl.loop(0, 4)
        def _(b):
            p[t, half, core, b] = (
                p[t, half, core, b].astype(F32) + rc[t, half, b].astype(F32)
            ).astype(BF16)

    def big_sum_copy(t, half, o):
        return send(
            p.at[t, half, core, turn(big_pos[half], o)],
            big_in.at[t, half, o - 1],
            K_BIG[t][half][o],
            big_peers[half][o],
        )

    def small_sum_copy(t, half, o):
        return send(
            r1.at[t, half, turn(small_pos[half], o)],
            small_in.at[t, half, o - 1],
            K_SMALL[t][half][o],
            small_peers[half][o],
        )

    def decode_slot(t, log):
        for half in HALVES:
            decode(t, 1 - core, half)
            go(log, part_copy, t, half)
        for half in HALVES:
            decode(t, core, half)
            part_add(t, half)
            for o in (2, 1, 3):
                go(log, big_sum_copy, t, half, o)

    def big_sum(t, half, log):
        for o in OFFSETS:
            big_sum_copy(t, half, o).wait_recv()
        for i in range(4):
            value = p[t, half, core, big_pos[half], i].astype(F32)
            for o in OFFSETS:
                value = value + big_in[t, half, o - 1, i].astype(F32)
            r1[t, half, i] = value.astype(BF16)
        for o in (2, 1, 3):
            go(log, small_sum_copy, t, half, o)

    def small_sum(t, half):
        for o in OFFSETS:
            small_sum_copy(t, half, o).wait_recv()
        value = r1[t, half, small_pos[half]].astype(F32)
        for o in OFFSETS:
            value = value + small_in[t, half, o - 1].astype(F32)
        r2[t, half] = value.astype(BF16)

    def cross_send(half, from_y):
        return send(
            r2.at[1, half],
            cross_in.at[from_y],
            K_CROSS[from_y],
            place(x, 2 + half, z, core),
        )

    @pl.when(first_layer)
    def _():
        decode_slot(1, sent_first)

    decode_slot(0, sent)

    @pl.loop(0, 4)
    def _(n):
        cols = pl.ds(pl.multiple_of(n * 256, 256), 256)
        ft[cols, :] = feat[:, cols].T

    ft_store = pltpu.make_async_copy(ft, ft_out, local_sem.at[5])
    ft_store.start()

    for half in HALVES:

        @pl.loop(0, 4)
        def _(m):
            z_high, to_core = lax.div(m, 2), lax.rem(m, 2)
            block = column_block(g, (0,), half, z_high, to_core)
            rows = pl.ds(pl.multiple_of((half * 4 + m) * 256, 256), 256)
            gt[rows, :] = block.T

    gt_store = pltpu.make_async_copy(gt, gt_out, local_sem.at[6])
    gt_store.start()

    @pl.when(first_layer)
    def _():
        for half in HALVES:
            big_sum(1, half, sent_first)
        for half in HALVES:
            small_sum(1, half)
            for from_y in (0, 1):

                @pl.when(yb == from_y)
                def _():
                    cross_send(half, from_y).start()

    for half in HALVES:
        big_sum(0, half, sent)
    for half in HALVES:
        small_sum(0, half)
    y_copy = send(r2.at[0, 1 - yb], y_in, K_Y, y_pair)
    go(sent, lambda: y_copy)
    y_copy.wait_recv()
    total = r2[0, yb].astype(F32) + y_in[...].astype(F32) - tgt[...].astype(F32)
    rerr[...] = total

    @pl.when(second_layer)
    def _():
        for from_y in (0, 1):
            cross_send(0, from_y).wait_recv()
        rerr[...] = rerr[...] + cross_in[0].astype(F32) + cross_in[1].astype(F32)

    error = rerr[...]
    own_s = own_half(s, (LOSS_SCALE / TOK * error).astype(BF16))

    def back_copy(to_y, half):
        big, small = block_at(half, z, x)
        return send(
            own_s,
            s.at[1, half, core, big, small],
            K_BACK[half],
            place(x, to_y, z, core),
        )

    @pl.when(second_layer)
    def _():
        for half in HALVES:

            @pl.when(yb == half)
            def _():
                for to_y in (0, 1):
                    back_copy(to_y, half).start()

    s_y = send(own_s, own_s, K_GATHER[0]["y"], y_pair)
    go(sent, lambda: s_y)
    s0 = Gather(s, 0, K_GATHER[0], unlogged)
    s1 = Gather(s, 1, K_GATHER[1], sent_first)

    def s0_mine(mine, other):
        s0.small(mine)

    by_half(s0_mine)

    square = error * error
    tile = jnp.zeros((8, 128), F32)
    for i in range(8):
        for j in range(2):
            tile = tile + square[i * 8 : i * 8 + 8, j * 128 : j * 128 + 128]

    def square_copy(stage, o):
        peers = ([None, partner], x_peers, z_peers, y_peers)[stage]
        pos = (core, x, z, y)[stage]
        return send(
            squares_own.at[stage], squares_in.at[stage, pos], K_SQUARE[stage][o], peers[o]
        )

    def square_offsets(stage):
        return (1,) if stage == 0 else (1, 2, 3)

    def squares_start(stage, value):
        squares_own[stage] = value
        squares_in[stage, (core, x, z, y)[stage]] = value
        for o in square_offsets(stage):
            go(sent, square_copy, stage, o)

    def squares_end(stage):
        for o in square_offsets(stage):
            square_copy(stage, o).wait_recv()
        value = squares_in[stage, 0]
        for i in range(1, 2 if stage == 0 else 4):
            value = value + squares_in[stage, i]
        return value

    squares_start(0, tile)

    def feature_grad(t, n):
        rows = pl.ds(pl.multiple_of(n * 256, 256), 256)
        return lax.dot_general(
            all_columns(s, (t,)),
            decv[t, rows, :],
            (((1,), (1,)), ((), ())),
            preferred_element_type=F32,
        )

    def pg_copy(n):
        cols = pl.ds(pl.multiple_of(n * 256, 256), 256)
        return pltpu.make_async_copy(pg.at[:, cols], pg_out.at[:, cols], local_sem.at[7 + n])

    def preact_grad(n, value):
        cols = pl.ds(pl.multiple_of(n * 256, 256), 256)
        grad = jnp.where(pre[:, cols] > 0.0, value, 0.0).astype(BF16)
        pg[:, cols] = grad
        bg[:, cols] = jnp.sum(grad.astype(F32), 0, keepdims=True)
        pg_copy(n).start()

    def s0_other(mine, other):
        s_y.wait_recv()
        s0.small(other)

    by_half(s0_other)

    @pl.when(first_layer)
    def _():
        for half in HALVES:
            back_copy(0, half).wait_recv()
            s1.small(half)

    squares_start(1, squares_end(0))
    by_half(big_hops(s0))
    squares_start(2, squares_end(1))

    @pl.when(first_layer)
    def _():
        for half in HALVES:
            s1.big(half)

    squares_start(3, squares_end(2))
    by_half(share_hops(s0))
    msq[0, 0] = jnp.sum(squares_end(3)) / (LAYERS * TOK * D)
    s0.done()
    s_store0 = pltpu.make_async_copy(s.at[0], s_out.at[0], local_sem.at[2])
    s_store0.start()
    s_store1 = pltpu.make_async_copy(s.at[1], s_out.at[1], local_sem.at[3])

    @pl.when(second_layer)
    def _():
        @pl.loop(0, 4)
        def _(n):
            preact_grad(n, feature_grad(0, n))

    @pl.when(first_layer)
    def _():
        @pl.loop(0, 4)
        def _(n):
            rows = pl.ds(pl.multiple_of(n * 256, 256), 256)
            fg[:, rows] = feature_grad(0, n)

    @pl.when(first_layer)
    def _():
        for half in HALVES:
            s1.share(half)
        s1.done()
        s_store1.start()

    @pl.when(first_layer)
    def _():
        @pl.loop(0, 4)
        def _(n):
            rows = pl.ds(pl.multiple_of(n * 256, 256), 256)
            preact_grad(n, fg[:, rows] + feature_grad(1, n))

    drain(sent)
    for gather in (tokens, s0):
        for half in HALVES:
            for o in OFFSETS:
                gather.small_copy(half, o).wait_send()
                gather.big_copy(half, o).wait_send()
            for o in range(4):
                gather.shared_copy(half, o).wait_send()

    @pl.when(first_layer)
    def _():
        drain(sent_first)
        for half in HALVES:
            for from_y in (0, 1):

                @pl.when(yb == from_y)
                def _():
                    cross_send(half, from_y).wait_send()

        s_store1.wait()

    @pl.when(second_layer)
    def _():
        for half in HALVES:

            @pl.when(yb == half)
            def _():
                for to_y in (0, 1):
                    back_copy(to_y, half).wait_send()

    s_store0.wait()
    ft_store.wait()
    gt_store.wait()
    for n in range(4):
        pg_copy(n).wait()


def weight_grads_kernel(
    gt_in, ft_in, s_in, pg_in, rerr_in, msq_in, bg_in,
    dec_grad, enc_grad, rerr, msq, bg,
    gt, ft, s, pg, dec_out, enc_out, in_sem, dec_sem, enc_sem,
):
    y = lax.div(lax.axis_index("layer"), 4)
    first_layer = y < 2
    second_layer = y >= 2
    ft_copy = pltpu.make_async_copy(ft_in, ft, in_sem.at[0])
    s_copies = [pltpu.make_async_copy(s_in.at[t], s.at[t], in_sem.at[1 + t]) for t in (0, 1)]
    pg_copy = pltpu.make_async_copy(pg_in, pg, in_sem.at[3])
    gt_copy = pltpu.make_async_copy(gt_in, gt, in_sem.at[4])
    ft_copy.start()
    s_copies[0].start()

    @pl.when(first_layer)
    def _():
        s_copies[1].start()

    pg_copy.start()
    gt_copy.start()
    rerr[...] = rerr_in[...]
    bg[...] = bg_in[...]
    msq[0, 0] = msq_in[0, 0]

    def dec_copy(t, m):
        cols = pl.ds(pl.multiple_of(m * 256, 256), 256)
        return pltpu.make_async_copy(
            dec_out.at[t, m], dec_grad.at[t, :, cols], dec_sem.at[t, m]
        )

    def dec_half(t, half):
        @pl.loop(0, 4)
        def _(i):
            m = half * 4 + i
            block = column_block(s, (t,), half, lax.div(i, 2), lax.rem(i, 2))
            dec_out[t, m] = jnp.dot(
                ft[...], block, preferred_element_type=F32
            ).astype(BF16)
            dec_copy(t, m).start()

    @pl.when(second_layer)
    def _():
        @pl.loop(0, 8)
        def _(m):
            dec_out[1, m] = jnp.zeros((SHARD, 256), BF16)
            dec_copy(1, m).start()

    ft_copy.wait()
    s_copies[0].wait()
    dec_half(0, 0)
    dec_half(0, 1)

    @pl.when(first_layer)
    def _():
        s_copies[1].wait()
        dec_half(1, 0)
        dec_half(1, 1)

    pg_copy.wait()
    gt_copy.wait()

    def enc_copy(n):
        rows = pl.ds(pl.multiple_of(n * 512, 512), 512)
        return pltpu.make_async_copy(
            enc_out.at[rows, :], enc_grad.at[rows, :], enc_sem.at[n]
        )

    @pl.loop(0, 4)
    def _(n):
        rows = pl.ds(pl.multiple_of(n * 512, 512), 512)
        enc_out[rows, :] = jnp.dot(
            gt[rows, :], pg[...], preferred_element_type=F32
        ).astype(BF16)
        enc_copy(n).start()

    for t in (0, 1):
        for m in range(8):
            dec_copy(t, m).wait()
    for n in range(4):
        enc_copy(n).wait()


def on_device(tokens_in, targets, enc_weight, enc_bias, dec_weight):
    vmem = pl.BlockSpec(memory_space=pltpu.VMEM)
    smem = pl.BlockSpec(memory_space=pltpu.SMEM)
    anywhere = pl.BlockSpec(memory_space=pl.ANY)
    shape = jax.ShapeDtypeStruct
    blocks = (2, 2, 4, 4, ROWS, COLS)
    rerr, msq, gt, ft, s, pg, bg = pl.pallas_call(
        step_kernel,
        out_shape=(
            shape((ROWS, COLS), F32),
            shape((1, 1), F32),
            shape((D, TOK), BF16),
            shape((SHARD, TOK), BF16),
            shape((2, *blocks), BF16),
            shape((TOK, SHARD), BF16),
            shape((1, SHARD), F32),
        ),
        in_specs=[vmem, vmem, anywhere, vmem, anywhere],
        out_specs=(vmem, smem, anywhere, anywhere, anywhere, anywhere, vmem),
        scratch_shapes=[
            pltpu.VMEM((D, SHARD), BF16),
            pltpu.VMEM((2, SHARD, D), BF16),
            pltpu.VMEM((1, *blocks), BF16),
            pltpu.VMEM((TOK, SHARD), F32),
            pltpu.VMEM((TOK, SHARD), BF16),
            pltpu.VMEM((2, *blocks), BF16),
            pltpu.VMEM((2, 2, 4, 4, ROWS, COLS), BF16),
            pltpu.VMEM((2, 2, 3, 4, ROWS, COLS), BF16),
            pltpu.VMEM((2, 2, 4, ROWS, COLS), BF16),
            pltpu.VMEM((2, 2, 3, ROWS, COLS), BF16),
            pltpu.VMEM((2, 2, ROWS, COLS), BF16),
            pltpu.VMEM((ROWS, COLS), BF16),
            pltpu.VMEM((2, ROWS, COLS), BF16),
            pltpu.VMEM((2, *blocks), BF16),
            pltpu.VMEM((TOK, SHARD), F32),
            pltpu.VMEM((D, TOK), BF16),
            pltpu.VMEM((SHARD, TOK), BF16),
            pltpu.VMEM((TOK, SHARD), BF16),
            pltpu.VMEM((4, 4, 8, 128), F32),
            pltpu.VMEM((4, 8, 128), F32),
            pltpu.SemaphoreType.DMA((K_COUNT,)),
            pltpu.SemaphoreType.DMA((K_COUNT,)),
            pltpu.SemaphoreType.DMA((11,)),
        ],
        compiler_params=pltpu.CompilerParams(
            collective_id=0, has_side_effects=True, vmem_limit_bytes=60 * 2**20
        ),
        name="step",
    )(tokens_in, targets, enc_weight, enc_bias.reshape(1, SHARD), dec_weight)

    dec_grad, enc_grad, rerr, msq, bg = pl.pallas_call(
        weight_grads_kernel,
        out_shape=(
            shape((2, SHARD, D), BF16),
            shape((D, SHARD), BF16),
            shape((ROWS, COLS), F32),
            shape((1, 1), F32),
            shape((1, SHARD), F32),
        ),
        in_specs=[anywhere] * 4 + [vmem, smem, vmem],
        out_specs=(anywhere, anywhere, vmem, smem, vmem),
        scratch_shapes=[
            pltpu.VMEM((D, TOK), BF16),
            pltpu.VMEM((SHARD, TOK), BF16),
            pltpu.VMEM((2, *blocks), BF16),
            pltpu.VMEM((TOK, SHARD), BF16),
            pltpu.VMEM((2, 8, SHARD, 256), BF16),
            pltpu.VMEM((D, SHARD), BF16),
            pltpu.SemaphoreType.DMA((5,)),
            pltpu.SemaphoreType.DMA((2, 8)),
            pltpu.SemaphoreType.DMA((4,)),
        ],
        compiler_params=pltpu.CompilerParams(vmem_limit_bytes=60 * 2**20),
        name="weight_grads",
    )(gt, ft, s, pg, rerr, msq, bg)
    return (rerr, msq.reshape(()), enc_grad, bg.reshape(SHARD), dec_grad)


def solution(mesh):
    placed = (
        P("feat", "layer"),
        P("feat", "layer"),
        P(None, ("layer", "feat")),
        P(("layer", "feat")),
        P(None, ("layer", "feat"), None),
    )
    return jax.shard_map(
        on_device,
        mesh=mesh,
        in_specs=placed,
        out_specs=(
            P("feat", "layer"),
            P(),
            P(None, ("layer", "feat")),
            P(("layer", "feat")),
            P(None, ("layer", "feat"), None),
        ),
        check_vma=False,
    )
```

```python
import jax
import jax.numpy as jnp
from jax import lax
from jax.experimental import pallas as pl
from jax.experimental.pallas import tpu as pltpu
from jax.sharding import PartitionSpec as P

D = 2048
LAYERS = 2
TOK = 512
SHARD = 1024
ROWS = 64
COLS = 256
LOSS_SCALE = 64.0
MESH = pl.DeviceIdType.MESH
BF16 = jnp.bfloat16
F32 = jnp.float32


def place(x, y, z, core):
    return (y * 4 + lax.div(z, 2) * 2 + core, x * 2 + lax.rem(z, 2))


def block_at(half, z, x):
    return z * (1 - half) + x * half, x * (1 - half) + z * half


def column_block(ref, lead, half, z_high, core):
    pieces = []
    for x in range(4):
        for z_low in range(2):
            big, small = block_at(half, z_high * 2 + z_low, x)
            pieces.append(ref[(*lead, half, core, big, small)])
    return jnp.concatenate(pieces, 0)


def core_columns(ref, lead, core):
    return jnp.concatenate(
        [column_block(ref, lead, m // 2, m % 2, core) for m in range(4)], 1
    )


def core_shards(core):
    return [pl.ds(pl.multiple_of((m * 2 + core) * 256, 256), 256) for m in range(4)]


class Numbers:
    def __init__(self):
        self.count = 0

    def take(self, *dims):
        if not dims:
            self.count += 1
            return self.count - 1
        return [self.take(*dims[1:]) for _ in range(dims[0])]


NUMBERS = Numbers()
def gather_numbers():
    return dict(
        y=NUMBERS.take(),
        small=NUMBERS.take(2),
        big=NUMBERS.take(2, 4),
        shared=NUMBERS.take(),
    )


K_GATHER = [gather_numbers(), gather_numbers()]
K_PART = NUMBERS.take(2, 2)
K_BIG = NUMBERS.take(2, 2)
K_SMALL = NUMBERS.take(2, 2)
K_Y = NUMBERS.take()
K_CROSS = NUMBERS.take(2)
K_BACK = NUMBERS.take(2)
K_PASS = NUMBERS.take(2)
K_SQUARE = NUMBERS.take(4)
K_COUNT = NUMBERS.count


def step_kernel(
    tok, tgt_in, enc, bias_in, dec,
    rerr_out, squares_out, gt_out, ft_out, s_out, pg_out, bg_out,
    tgt, bias, rerr, bg, encv, decv, g, pre, feat, p, rc, big_in, r1, small_in, r2, y_in, cross_in,
    s, fg, gt, ft, pg, squares_in, squares_own, send_sem, recv_sem, local_sem,
):
    me_layer = lax.axis_index("layer")
    me_feat = lax.axis_index("feat")
    core = lax.rem(me_layer, 2)
    y = lax.div(me_layer, 4)
    x = lax.div(me_feat, 2)
    z = lax.rem(lax.div(me_layer, 2), 2) * 2 + lax.rem(me_feat, 2)
    yb = lax.rem(y, 2)
    first_layer = y < 2
    second_layer = y >= 2

    def turn(v, step):
        return lax.rem(v + step, 4)

    partner = place(x, y, z, 1 - core)
    y_pair = place(x, y + 1 - 2 * yb, z, core)
    x_peers = [None] + [place(turn(x, o), y, z, core) for o in (1, 2, 3)]
    y_peers = [None] + [place(x, turn(y, o), z, core) for o in (1, 2, 3)]
    z_peers = [None] + [place(x, y, turn(z, o), core) for o in (1, 2, 3)]
    big_pos, small_pos = (z, x), (x, z)
    big_peers, small_peers = (z_peers, x_peers), (x_peers, z_peers)
    HALVES = (0, 1)
    OFFSETS = (2, 1, 3)

    def send(src, dst, number, device):
        return pltpu.make_async_remote_copy(
            src_ref=src,
            dst_ref=dst,
            send_sem=send_sem.at[number],
            recv_sem=recv_sem.at[number],
            device_id=device,
            device_id_type=MESH,
        )

    def own_block(buf):
        big, small = block_at(yb, z, x)
        return buf.at[0, yb, core, big, small]

    enc_copy = pltpu.make_async_copy(enc, encv, local_sem.at[0])
    dec_copy = pltpu.make_async_copy(dec, decv, local_sem.at[1])
    tok_copy = pltpu.make_async_copy(tok, own_block(g), local_sem.at[2])
    tgt_copy = pltpu.make_async_copy(tgt_in, tgt, local_sem.at[3])
    bias_copy = pltpu.make_async_copy(bias_in, bias, local_sem.at[4])
    tok_copy.start()
    enc_copy.start()
    dec_copy.start()
    tgt_copy.start()
    bias_copy.start()

    barrier = pltpu.get_barrier_semaphore()
    for device in (partner, *x_peers[1:], *y_peers[1:], *z_peers[1:]):
        pl.semaphore_signal(barrier, inc=1, device_id=device, device_id_type=MESH)
    tok_copy.wait()
    pl.semaphore_wait(barrier, 10)

    class Gather:
        def __init__(self, buf, t, numbers, offsets=OFFSETS):
            self.buf, self.t, self.numbers = buf, t, numbers
            self.offsets = offsets

        def piece(self, half):
            return self.buf.at[self.t, half, core, big_pos[half], small_pos[half]]

        def chunk(self, half, i):
            return self.buf.at[self.t, half, core, i]

        def small_copy(self, half, o):
            ref = self.piece(half)
            return send(ref, ref, self.numbers["small"][half], small_peers[half][o])

        def all_small(self, half):
            ref = self.buf.at[self.t, half, core, 0, 0:3]
            return send(ref, ref, self.numbers["small"][half], partner)

        def big_copy(self, half, o):
            ref = self.chunk(half, big_pos[half])
            return send(ref, ref, self.numbers["big"][half][o], big_peers[half][o])

        def shared_copy(self, half, o):
            ref = self.chunk(half, turn(big_pos[half], 4 - o))
            return send(ref, ref, self.numbers["shared"], partner)

        def all_shared(self, of_core):
            ref = self.buf.at[self.t, :, of_core]
            return send(ref, ref, self.numbers["shared"], partner)

        def small(self, half):
            for o in OFFSETS:
                self.small_copy(half, o).start()

        def big(self, half):
            self.all_small(half).wait_recv()
            for o in self.offsets:
                self.big_copy(half, o).start()
            self.shared_copy(half, 0).start()

        def share(self, half):
            for o in self.offsets:
                self.big_copy(half, o).wait_recv()
                self.shared_copy(half, o).start()

        def done(self):
            self.all_shared(1 - core).wait_recv()

        def drain(self):
            for half in HALVES:
                self.all_small(half).wait_send()
                for o in self.offsets:
                    self.big_copy(half, o).wait_send()
            self.all_shared(core).wait_send()

    def by_half(fn):
        @pl.when(yb == 0)
        def _():
            fn(0, 1)

        @pl.when(yb == 1)
        def _():
            fn(1, 0)

    own = own_block(g)
    tok_y = send(own, own, K_GATHER[0]["y"], y_pair)
    tok_y.start()
    def first_hops(gather, y_copy):
        def run(mine, other):
            gather.small(mine)
            y_copy.wait_recv()
            gather.small(other)

        return run

    tokens = Gather(g, 0, K_GATHER[0])
    by_half(first_hops(tokens, tok_y))

    def big_hops(gather):
        def run(mine, other):
            gather.big(mine)
            gather.big(other)

        return run

    by_half(big_hops(tokens))

    def share_hops(gather):
        def run(mine, other):
            gather.share(mine)
            gather.share(other)

        return run

    by_half(share_hops(tokens))
    enc_copy.wait()
    bias_copy.wait()

    def encode_part(from_core, n):
        cols = pl.ds(pl.multiple_of(n * 256, 256), 256)
        weights = jnp.concatenate([encv[rows, cols] for rows in core_shards(from_core)], 0)
        return cols, jnp.dot(
            core_columns(g, (0,), from_core), weights, preferred_element_type=F32
        )

    @pl.loop(0, 4)
    def _(n):
        cols, value = encode_part(core, n)
        pre[:, cols] = value + bias[:, cols]

    tokens.done()

    @pl.loop(0, 4)
    def _(n):
        cols, value = encode_part(1 - core, n)
        act = pre[:, cols] + value
        pre[:, cols] = act
        feat[:, cols] = jnp.maximum(act, 0.0).astype(BF16)

    dec_copy.wait()

    def decode(t, to_core, half):
        for z_high in range(2):
            first = pl.multiple_of((half * 4 + z_high * 2 + to_core) * 256, 256)
            value = jnp.dot(
                feat[...], decv[t, :, pl.ds(first, 256)], preferred_element_type=F32
            ).astype(BF16)
            for to_x in range(4):
                for z_low in range(2):
                    big, small = block_at(half, z_high * 2 + z_low, to_x)
                    at = (to_x * 2 + z_low) * ROWS
                    p[t, half, to_core, big, small] = value[at : at + ROWS]

    def part_copy(t, half):
        return send(p.at[t, half, 1 - core], rc.at[t, half], K_PART[t][half], partner)

    def part_add(t, half):
        part_copy(t, half).wait_recv()

        @pl.loop(0, 4)
        def _(b):
            p[t, half, core, b] = (
                p[t, half, core, b].astype(F32) + rc[t, half, b].astype(F32)
            ).astype(BF16)

    def big_sum_copy(t, half, o):
        return send(
            p.at[t, half, core, turn(big_pos[half], o)],
            big_in.at[t, half, o - 1],
            K_BIG[t][half],
            big_peers[half][o],
        )

    def all_big_sums(t, half):
        return send(p.at[t, half, core, 0:3], big_in.at[t, half], K_BIG[t][half], partner)

    def small_sum_copy(t, half, o):
        return send(
            r1.at[t, half, turn(small_pos[half], o)],
            small_in.at[t, half, o - 1],
            K_SMALL[t][half],
            small_peers[half][o],
        )

    def all_small_sums(t, half):
        return send(r1.at[t, half, 0:3], small_in.at[t, half], K_SMALL[t][half], partner)

    def big_sum_send(t, half):
        for o in OFFSETS:
            big_sum_copy(t, half, o).start()

    def decode_slot(t, after):
        for half in HALVES:
            decode(t, 1 - core, half)
            part_copy(t, half).start()
        for half in HALVES:
            decode(t, core, half)
            part_add(t, half)
            after(half)

    def big_sum(t, half):
        all_big_sums(t, half).wait_recv()
        for i in range(4):
            value = p[t, half, core, big_pos[half], i].astype(F32)
            for o in OFFSETS:
                value = value + big_in[t, half, o - 1, i].astype(F32)
            r1[t, half, i] = value.astype(BF16)
        for o in OFFSETS:
            small_sum_copy(t, half, o).start()

    def small_sum(t, half):
        all_small_sums(t, half).wait_recv()
        value = r1[t, half, small_pos[half]].astype(F32)
        for o in OFFSETS:
            value = value + small_in[t, half, o - 1].astype(F32)
        r2[t, half] = value.astype(BF16)

    def cross_send(half, from_y):
        return send(
            r2.at[1, half],
            cross_in.at[from_y],
            K_CROSS[from_y],
            place(x, 2 + half, z, core),
        )

    @pl.when(first_layer)
    def _():
        decode_slot(1, lambda half: big_sum_send(1, half))

    def send_early(half):
        @pl.when(second_layer)
        def _():
            big_sum_send(0, half)

    decode_slot(0, send_early)

    @pl.loop(0, 4)
    def _(n):
        cols = pl.ds(pl.multiple_of(n * 256, 256), 256)
        ft[cols, :] = feat[:, cols].T

    ft_store = pltpu.make_async_copy(ft, ft_out, local_sem.at[0])
    ft_store.start()

    for half in HALVES:

        @pl.loop(0, 4)
        def _(m):
            z_high, to_core = lax.div(m, 2), lax.rem(m, 2)
            block = column_block(g, (0,), half, z_high, to_core)
            rows = pl.ds(pl.multiple_of((half * 4 + m) * 256, 256), 256)
            gt[rows, :] = block.T

    gt_store = pltpu.make_async_copy(gt, gt_out, local_sem.at[1])
    gt_store.start()

    @pl.when(first_layer)
    def _():
        for half in HALVES:
            big_sum(1, half)
        for half in HALVES:
            big_sum_send(0, half)
        for half in HALVES:
            small_sum(1, half)
            for from_y in (0, 1):

                @pl.when(yb == from_y)
                def _():
                    cross_send(half, from_y).start()

    for half in HALVES:
        big_sum(0, half)

    tok_y.wait_send()
    tokens.drain()
    s0 = Gather(s, 0, K_GATHER[0])
    s1 = Gather(s, 1, K_GATHER[1], (1, 3))

    def back_copy(to_y, half):
        big, small = block_at(half, z, x)
        return send(
            own_block(s),
            s.at[1, half, core, big, small],
            K_BACK[half],
            place(x, to_y, z, core),
        )

    def pass_copy(half):
        opposite = turn(big_pos[half], 2)
        return send(
            s.at[0, half, core, opposite],
            s.at[1, half, core, opposite],
            K_PASS[half],
            place(x, 3 - y, z, core),
        )

    @pl.when(first_layer)
    def _():
        for half in HALVES:
            back_copy(0, half).wait_recv()
            s1.small(half)

    for half in HALVES:
        small_sum(0, half)
    y_copy = send(r2.at[0, 1 - yb], y_in, K_Y, y_pair)
    y_copy.start()

    @pl.when(first_layer)
    def _():
        for half in HALVES:
            s1.big(half)

    y_copy.wait_recv()
    tgt_copy.wait()
    total = r2[0, yb].astype(F32) + y_in[...].astype(F32) - tgt[...].astype(F32)
    rerr[...] = total

    @pl.when(second_layer)
    def _():
        for from_y in (0, 1):
            cross_send(0, from_y).wait_recv()
        rerr[...] = rerr[...] + cross_in[0].astype(F32) + cross_in[1].astype(F32)

    error = rerr[...]
    own_s = own_block(s)
    own_s[...] = (LOSS_SCALE / TOK * error).astype(BF16)

    @pl.when(second_layer)
    def _():
        for half in HALVES:

            @pl.when(yb == half)
            def _():
                for to_y in (0, 1):
                    back_copy(to_y, half).start()

    s_y = send(own_s, own_s, K_GATHER[0]["y"], y_pair)
    s_y.start()

    def s0_mine(mine, other):
        s0.small(mine)

    by_half(s0_mine)
    rerr_copy = pltpu.make_async_copy(rerr, rerr_out, local_sem.at[11])
    rerr_copy.start()

    square = error * error
    tile = jnp.zeros((8, 128), F32)
    for i in range(8):
        for j in range(2):
            tile = tile + square[i * 8 : i * 8 + 8, j * 128 : j * 128 + 128]

    def square_copy(stage, o):
        peers = (x_peers, z_peers, y_peers, [None, partner])[stage]
        pos = (x, z, y, core)[stage]
        return send(
            squares_own.at[stage], squares_in.at[stage, pos], K_SQUARE[stage], peers[o]
        )

    def square_offsets(stage):
        return (1, 2, 3) if stage < 3 else (1,)

    def all_squares(stage):
        ref = squares_in.at[stage, 0 : len(square_offsets(stage))]
        return send(ref, ref, K_SQUARE[stage], partner)

    def squares_start(stage, value):
        squares_own[stage] = value
        squares_in[stage, (x, z, y, core)[stage]] = value
        for o in square_offsets(stage):
            square_copy(stage, o).start()

    def squares_end(stage):
        all_squares(stage).wait_recv()
        value = squares_in[stage, 0]
        for i in range(1, 4 if stage < 3 else 2):
            value = value + squares_in[stage, i]
        return value

    squares_start(0, tile)

    def feature_grad(t, from_core, n):
        rows = pl.ds(pl.multiple_of(n * 256, 256), 256)
        weights = jnp.concatenate(
            [decv[t, rows, cols] for cols in core_shards(from_core)], 1
        )
        return rows, lax.dot_general(
            core_columns(s, (t,), from_core),
            weights,
            (((1,), (1,)), ((), ())),
            preferred_element_type=F32,
        )

    def pg_copy(n):
        cols = pl.ds(pl.multiple_of(n * 256, 256), 256)
        return pltpu.make_async_copy(pg.at[:, cols], pg_out.at[:, cols], local_sem.at[7 + n])

    def grad_start(t, from_core):
        @pl.loop(0, 4)
        def _(n):
            cols, value = feature_grad(t, from_core, n)
            fg[:, cols] = value

    def grad_more(t, from_core):
        @pl.loop(0, 4)
        def _(n):
            cols, value = feature_grad(t, from_core, n)
            fg[:, cols] = fg[:, cols] + value

    def grad_end(t, from_core):
        @pl.loop(0, 4)
        def _(n):
            cols, value = feature_grad(t, from_core, n)
            grad = jnp.where(pre[:, cols] > 0.0, fg[:, cols] + value, 0.0).astype(BF16)
            pg[:, cols] = grad
            bg[:, cols] = jnp.sum(grad.astype(F32), 0, keepdims=True)
            pg_copy(n).start()

    def s0_other(mine, other):
        s_y.wait_recv()
        s0.small(other)

    by_half(s0_other)
    squares_start(1, squares_end(0))
    by_half(big_hops(s0))

    s_store0 = pltpu.make_async_copy(s.at[0], s_out.at[0], local_sem.at[5])
    s_store1 = pltpu.make_async_copy(s.at[1], s_out.at[1], local_sem.at[6])

    @pl.when(second_layer)
    def _():
        for half in HALVES:
            s0.big_copy(half, 2).wait_recv()
            pass_copy(half).start()
            s0.shared_copy(half, 2).start()
        for half in HALVES:
            for o in (1, 3):
                s0.big_copy(half, o).wait_recv()
                s0.shared_copy(half, o).start()

    @pl.when(first_layer)
    def _():
        for half in HALVES:
            s1.share(half)

    squares_start(2, squares_end(1))

    @pl.when(first_layer)
    def _():
        for half in HALVES:
            pass_copy(half).wait_recv()
            s1.shared_copy(half, 2).start()

    squares_start(3, squares_end(2))

    @pl.when(first_layer)
    def _():
        grad_start(1, core)

    @pl.when(first_layer)
    def _():
        for half in HALVES:
            s0.share(half)
        s1.done()
        s_store1.start()

    @pl.when(first_layer)
    def _():
        grad_more(1, 1 - core)
        grad_more(0, core)

    @pl.when(second_layer)
    def _():
        grad_start(0, core)

    squares_own[4] = squares_end(3)
    squares_copy = pltpu.make_async_copy(squares_own.at[4], squares_out, local_sem.at[12])
    squares_copy.start()

    s0.done()
    s_store0.start()
    grad_end(0, 1 - core)
    bg_copy = pltpu.make_async_copy(bg, bg_out, local_sem.at[13])
    bg_copy.start()

    def drain_sums(t):
        for half in HALVES:
            part_copy(t, half).wait_send()
            all_big_sums(t, half).wait_send()
            all_small_sums(t, half).wait_send()

    drain_sums(0)
    y_copy.wait_send()
    s_y.wait_send()
    s0.drain()
    for stage in range(4):
        all_squares(stage).wait_send()

    @pl.when(first_layer)
    def _():
        drain_sums(1)
        s1.drain()
        for half in HALVES:
            for from_y in (0, 1):

                @pl.when(yb == from_y)
                def _():
                    cross_send(half, from_y).wait_send()

        s_store1.wait()

    @pl.when(second_layer)
    def _():
        for half in HALVES:

            @pl.when(yb == half)
            def _():
                for to_y in (0, 1):
                    back_copy(to_y, half).wait_send()

            pass_copy(half).wait_send()

    s_store0.wait()
    rerr_copy.wait()
    squares_copy.wait()
    bg_copy.wait()
    ft_store.wait()
    gt_store.wait()
    for n in range(4):
        pg_copy(n).wait()


def weight_grads_kernel(
    gt_in, ft_in, s_in, pg_in, rerr_in, squares_in, bg_in,
    dec_grad, enc_grad, rerr_out, mean_out, bg_out,
    gt, ft, s, pg, rerr, squares, mean, bg, dec_out, enc_out,
    in_sem, dec_sem, enc_sem, small_sem,
):
    y = lax.div(lax.axis_index("layer"), 4)
    first_layer = y < 2
    second_layer = y >= 2
    ft_copy = pltpu.make_async_copy(ft_in, ft, in_sem.at[0])
    s_copies = [
        [
            pltpu.make_async_copy(s_in.at[t, half], s.at[t, half], in_sem.at[1 + 2 * t + half])
            for half in (0, 1)
        ]
        for t in (0, 1)
    ]
    pg_copy = pltpu.make_async_copy(pg_in, pg, in_sem.at[5])
    gt_copy = pltpu.make_async_copy(gt_in, gt, in_sem.at[6])
    ft_copy.start()
    for copy in s_copies[0]:
        copy.start()

    @pl.when(first_layer)
    def _():
        for copy in s_copies[1]:
            copy.start()

    pg_copy.start()
    gt_copy.start()
    small_in = [
        pltpu.make_async_copy(src, dst, small_sem.at[i])
        for i, (src, dst) in enumerate(((rerr_in, rerr), (squares_in, squares), (bg_in, bg)))
    ]
    small_out = [
        pltpu.make_async_copy(src, dst, small_sem.at[3 + i])
        for i, (src, dst) in enumerate(((rerr, rerr_out), (mean, mean_out), (bg, bg_out)))
    ]
    for copy in small_in:
        copy.start()

    def dec_copy(t, m):
        cols = pl.ds(pl.multiple_of(m * 256, 256), 256)
        return pltpu.make_async_copy(
            dec_out.at[t, m], dec_grad.at[t, :, cols], dec_sem.at[t, m]
        )

    def dec_half(t, half):
        s_copies[t][half].wait()

        @pl.loop(0, 4, unroll=2)
        def _(i):
            m = half * 4 + i
            block = column_block(s, (t,), half, lax.div(i, 2), lax.rem(i, 2))
            dec_out[t, m] = jnp.dot(
                ft[...], block, preferred_element_type=F32
            ).astype(BF16)
            dec_copy(t, m).start()

    @pl.when(second_layer)
    def _():
        @pl.loop(0, 8)
        def _(m):
            dec_out[1, m] = jnp.zeros((SHARD, 256), BF16)
            dec_copy(1, m).start()

    ft_copy.wait()
    dec_half(0, 0)
    dec_half(0, 1)

    @pl.when(first_layer)
    def _():
        dec_half(1, 0)
        dec_half(1, 1)

    for copy in small_in:
        copy.wait()
    mean[...] = jnp.sum(squares[...], keepdims=True) / (LAYERS * TOK * D)
    for copy in small_out:
        copy.start()
    pg_copy.wait()
    gt_copy.wait()

    def enc_copy(n):
        rows = pl.ds(pl.multiple_of(n * 512, 512), 512)
        return pltpu.make_async_copy(
            enc_out.at[rows, :], enc_grad.at[rows, :], enc_sem.at[n]
        )

    @pl.loop(0, 4)
    def _(n):
        rows = pl.ds(pl.multiple_of(n * 512, 512), 512)
        enc_out[rows, :] = jnp.dot(
            gt[rows, :], pg[...], preferred_element_type=F32
        ).astype(BF16)
        enc_copy(n).start()

    for t in (0, 1):
        for m in range(8):
            dec_copy(t, m).wait()
    for n in range(4):
        enc_copy(n).wait()
    for copy in small_out:
        copy.wait()


def on_device(tokens_in, targets, enc_weight, enc_bias, dec_weight):
    anywhere = pl.BlockSpec(memory_space=pl.ANY)
    shape = jax.ShapeDtypeStruct
    blocks = (2, 2, 4, 4, ROWS, COLS)
    rerr, squares, gt, ft, s, pg, bg = pl.pallas_call(
        step_kernel,
        out_shape=(
            shape((ROWS, COLS), F32),
            shape((8, 128), F32),
            shape((D, TOK), BF16),
            shape((SHARD, TOK), BF16),
            shape((2, *blocks), BF16),
            shape((TOK, SHARD), BF16),
            shape((1, SHARD), F32),
        ),
        in_specs=[anywhere] * 5,
        out_specs=[anywhere] * 7,
        scratch_shapes=[
            pltpu.VMEM((ROWS, COLS), BF16),
            pltpu.VMEM((1, SHARD), F32),
            pltpu.VMEM((ROWS, COLS), F32),
            pltpu.VMEM((1, SHARD), F32),
            pltpu.VMEM((D, SHARD), BF16),
            pltpu.VMEM((2, SHARD, D), BF16),
            pltpu.VMEM((1, *blocks), BF16),
            pltpu.VMEM((TOK, SHARD), F32),
            pltpu.VMEM((TOK, SHARD), BF16),
            pltpu.VMEM((2, *blocks), BF16),
            pltpu.VMEM((2, 2, 4, 4, ROWS, COLS), BF16),
            pltpu.VMEM((2, 2, 3, 4, ROWS, COLS), BF16),
            pltpu.VMEM((2, 2, 4, ROWS, COLS), BF16),
            pltpu.VMEM((2, 2, 3, ROWS, COLS), BF16),
            pltpu.VMEM((2, 2, ROWS, COLS), BF16),
            pltpu.VMEM((ROWS, COLS), BF16),
            pltpu.VMEM((2, ROWS, COLS), BF16),
            pltpu.VMEM((2, *blocks), BF16),
            pltpu.VMEM((TOK, SHARD), F32),
            pltpu.VMEM((D, TOK), BF16),
            pltpu.VMEM((SHARD, TOK), BF16),
            pltpu.VMEM((TOK, SHARD), BF16),
            pltpu.VMEM((4, 4, 8, 128), F32),
            pltpu.VMEM((5, 8, 128), F32),
            pltpu.SemaphoreType.DMA((K_COUNT,)),
            pltpu.SemaphoreType.DMA((K_COUNT,)),
            pltpu.SemaphoreType.DMA((14,)),
        ],
        compiler_params=pltpu.CompilerParams(
            collective_id=0, has_side_effects=True, vmem_limit_bytes=60 * 2**20
        ),
        name="step",
    )(tokens_in, targets, enc_weight, enc_bias.reshape(1, SHARD), dec_weight)

    dec_grad, enc_grad, rerr, mean, bg = pl.pallas_call(
        weight_grads_kernel,
        out_shape=(
            shape((2, SHARD, D), BF16),
            shape((D, SHARD), BF16),
            shape((ROWS, COLS), F32),
            shape((1, 1), F32),
            shape((1, SHARD), F32),
        ),
        in_specs=[anywhere] * 7,
        out_specs=[anywhere] * 5,
        scratch_shapes=[
            pltpu.VMEM((D, TOK), BF16),
            pltpu.VMEM((SHARD, TOK), BF16),
            pltpu.VMEM((2, *blocks), BF16),
            pltpu.VMEM((TOK, SHARD), BF16),
            pltpu.VMEM((ROWS, COLS), F32),
            pltpu.VMEM((8, 128), F32),
            pltpu.VMEM((1, 1), F32),
            pltpu.VMEM((1, SHARD), F32),
            pltpu.VMEM((2, 8, SHARD, 256), BF16),
            pltpu.VMEM((D, SHARD), BF16),
            pltpu.SemaphoreType.DMA((7,)),
            pltpu.SemaphoreType.DMA((2, 8)),
            pltpu.SemaphoreType.DMA((4,)),
            pltpu.SemaphoreType.DMA((6,)),
        ],
        compiler_params=pltpu.CompilerParams(vmem_limit_bytes=60 * 2**20),
        name="weight_grads",
    )(gt, ft, s, pg, rerr, squares, bg)
    return (rerr, mean.reshape(()), enc_grad, bg.reshape(SHARD), dec_grad)


def solution(mesh):
    placed = (
        P("feat", "layer"),
        P("feat", "layer"),
        P(None, ("layer", "feat")),
        P(("layer", "feat")),
        P(None, ("layer", "feat"), None),
    )
    return jax.shard_map(
        on_device,
        mesh=mesh,
        in_specs=placed,
        out_specs=(
            P("feat", "layer"),
            P(),
            P(None, ("layer", "feat")),
            P(("layer", "feat")),
            P(None, ("layer", "feat"), None),
        ),
        check_vma=False,
    )
```

```python
import jax
import jax.numpy as jnp
from jax import lax
from jax.experimental import pallas as pl
from jax.experimental.pallas import tpu as pltpu
from jax.sharding import PartitionSpec as P

D = 2048
LAYERS = 2
TOK = 512
SHARD = 1024
ROWS = 64
COLS = 256
LOSS_SCALE = 64.0
MESH = pl.DeviceIdType.MESH
HELD = (2,)
PASS = (0, 1)
ORDER = (0, 1)
BF16 = jnp.bfloat16
F32 = jnp.float32


def place(x, y, z, core):
    return (y * 4 + lax.div(z, 2) * 2 + core, x * 2 + lax.rem(z, 2))


def block_at(half, z, x):
    return z * (1 - half) + x * half, x * (1 - half) + z * half


def column_block(ref, lead, half, z_high, core):
    pieces = []
    for x in range(4):
        for z_low in range(2):
            big, small = block_at(half, z_high * 2 + z_low, x)
            pieces.append(ref[(*lead, half, core, big, small)])
    return jnp.concatenate(pieces, 0)


def core_columns(ref, lead, core):
    return jnp.concatenate(
        [column_block(ref, lead, m // 2, m % 2, core) for m in range(4)], 1
    )


def all_columns(ref, lead):
    return jnp.concatenate(
        [column_block(ref, lead, m // 4, m // 2 % 2, m % 2) for m in range(8)], 1
    )


def core_shards(core):
    return [pl.ds(pl.multiple_of((m * 2 + core) * 256, 256), 256) for m in range(4)]


class Numbers:
    def __init__(self):
        self.count = 0

    def take(self, *dims):
        if not dims:
            self.count += 1
            return self.count - 1
        return [self.take(*dims[1:]) for _ in range(dims[0])]


NUMBERS = Numbers()
def gather_numbers():
    return dict(
        small=NUMBERS.take(2),
        big=NUMBERS.take(2, 4),
        shared=NUMBERS.take(),
    )


K_GATHER = [gather_numbers(), gather_numbers()]
K_PART = NUMBERS.take(2, 2)
K_BIG = NUMBERS.take(2, 2)
K_SMALL = NUMBERS.take(2)
K_FINAL = NUMBERS.take()
K_CROSS = NUMBERS.take(2)
K_BACK = NUMBERS.take(2)
K_PASS = NUMBERS.take(2)
K_SQUARE = NUMBERS.take(4)
K_COUNT = NUMBERS.count


def step_kernel(
    tok, tgt_in, enc, bias_in, dec,
    rerr_out, squares_out, gt_out, ft_out, s_out, pg_out, bg_out,
    tgt, bias, rerr, bg, encv, decv, g, pre, feat, p, rc, big_in, r1, small_in, r2, final_in, cross_in,
    s, fg, gt, ft, pg, squares_in, squares_own, send_sem, recv_sem, local_sem,
):
    me_layer = lax.axis_index("layer")
    me_feat = lax.axis_index("feat")
    core = lax.rem(me_layer, 2)
    y = lax.div(me_layer, 4)
    x = lax.div(me_feat, 2)
    z = lax.rem(lax.div(me_layer, 2), 2) * 2 + lax.rem(me_feat, 2)
    yb = lax.rem(y, 2)
    first_layer = y < 2
    second_layer = y >= 2

    def turn(v, step):
        return lax.rem(v + step, 4)

    partner = place(x, y, z, 1 - core)
    y_pair = y + 1 - 2 * yb
    x_peers = [None] + [place(turn(x, o), y, z, core) for o in (1, 2, 3)]
    y_peers = [None] + [place(x, turn(y, o), z, core) for o in (1, 2, 3)]
    z_peers = [None] + [place(x, y, turn(z, o), core) for o in (1, 2, 3)]
    big_pos, small_pos = (z, x), (x, z)
    big_peers, small_peers = (z_peers, x_peers), (x_peers, z_peers)
    pair_peers = (
        [place(turn(x, o), y_pair, z, core) for o in range(4)],
        [place(x, y_pair, turn(z, o), core) for o in range(4)],
    )
    HALVES = (0, 1)
    OFFSETS = (2, 1, 3)

    def send(src, dst, number, device):
        return pltpu.make_async_remote_copy(
            src_ref=src,
            dst_ref=dst,
            send_sem=send_sem.at[number],
            recv_sem=recv_sem.at[number],
            device_id=device,
            device_id_type=MESH,
        )

    def own_block(buf):
        big, small = block_at(yb, z, x)
        return buf.at[0, yb, core, big, small]

    enc_copy = pltpu.make_async_copy(enc, encv, local_sem.at[0])
    dec_copy = pltpu.make_async_copy(dec, decv, local_sem.at[1])
    tok_copy = pltpu.make_async_copy(tok, own_block(g), local_sem.at[2])
    tgt_copy = pltpu.make_async_copy(tgt_in, tgt, local_sem.at[3])
    bias_copy = pltpu.make_async_copy(bias_in, bias, local_sem.at[4])
    tok_copy.start()
    enc_copy.start()
    dec_copy.start()
    tgt_copy.start()
    bias_copy.start()

    barrier = pltpu.get_barrier_semaphore()
    for device in (
        partner,
        *x_peers[1:],
        *y_peers[1:],
        *z_peers[1:],
        *pair_peers[0][1:],
        *pair_peers[1][1:],
    ):
        pl.semaphore_signal(barrier, inc=1, device_id=device, device_id_type=MESH)
    tok_copy.wait()
    pl.semaphore_wait(barrier, 16)

    class Gather:
        def __init__(self, buf, t, numbers, offsets=(OFFSETS, OFFSETS)):
            self.buf, self.t, self.numbers = buf, t, numbers
            self.offsets = offsets

        def piece(self, half):
            return self.buf.at[self.t, half, core, big_pos[half], small_pos[half]]

        def chunk(self, half, i):
            return self.buf.at[self.t, half, core, i]

        def small_copy(self, half, o):
            ref = self.piece(half)
            return send(ref, ref, self.numbers["small"][half], small_peers[half][o])

        def pair_copy(self, half, o):
            ref = self.piece(half)
            return send(ref, ref, self.numbers["small"][half], pair_peers[half][o])

        def all_small(self, half, count=3):
            ref = self.buf.at[self.t, half, core, 0, 0:count]
            return send(ref, ref, self.numbers["small"][half], partner)

        def all_joint(self, half):
            return send(final_in, final_in, self.numbers["small"][half], partner)

        def joint(self, mine, other):
            for o in (2, 1, 3, 0):
                self.pair_copy(mine, o).start()
                if o > 0:
                    self.small_copy(mine, o).start()

        def big_copy(self, half, o):
            ref = self.chunk(half, big_pos[half])
            return send(ref, ref, self.numbers["big"][half][o], big_peers[half][o])

        def shared_copy(self, half, o):
            ref = self.chunk(half, turn(big_pos[half], 4 - o))
            return send(ref, ref, self.numbers["shared"], partner)

        def all_shared(self, of_core):
            ref = self.buf.at[self.t, :, of_core]
            return send(ref, ref, self.numbers["shared"], partner)

        def small(self, half):
            for o in OFFSETS:
                self.small_copy(half, o).start()

        def big(self, half, count=3):
            self.all_small(half, count).wait_recv()
            for o in self.offsets[half]:
                self.big_copy(half, o).start()
            self.shared_copy(half, 0).start()

        def share(self, half):
            for o in self.offsets[half]:
                self.big_copy(half, o).wait_recv()
                self.shared_copy(half, o).start()

        def done(self):
            self.all_shared(1 - core).wait_recv()

        def drain(self, joint):
            if joint:
                by_half(lambda mine, other: self.all_joint(mine).wait_send())
            for half in HALVES:
                if not joint:
                    self.all_small(half).wait_send()
                for o in self.offsets[half]:
                    self.big_copy(half, o).wait_send()
            self.all_shared(core).wait_send()

    def by_half(fn):
        @pl.when(yb == 0)
        def _():
            fn(0, 1)

        @pl.when(yb == 1)
        def _():
            fn(1, 0)

    tokens = Gather(g, 0, K_GATHER[0])
    by_half(tokens.joint)

    def big_hops(gather):
        def run(mine, other):
            gather.big(mine)
            gather.big(other, 4)

        return run

    by_half(big_hops(tokens))

    def share_hops(gather):
        def run(mine, other):
            gather.share(mine)
            gather.share(other)

        return run

    by_half(share_hops(tokens))
    enc_copy.wait()
    bias_copy.wait()

    def encode_part(from_core, n):
        cols = pl.ds(pl.multiple_of(n * 256, 256), 256)
        weights = jnp.concatenate([encv[rows, cols] for rows in core_shards(from_core)], 0)
        return cols, jnp.dot(
            core_columns(g, (0,), from_core), weights, preferred_element_type=F32
        )

    @pl.loop(0, 4, unroll=2)
    def _(n):
        cols, value = encode_part(core, n)
        pre[:, cols] = value + bias[:, cols]

    tokens.done()

    @pl.loop(0, 4, unroll=2)
    def _(n):
        cols, value = encode_part(1 - core, n)
        act = pre[:, cols] + value
        pre[:, cols] = act
        feat[:, cols] = jnp.maximum(act, 0.0).astype(BF16)

    dec_copy.wait()

    def decode(t, to_core, half):
        for z_high in range(2):
            first = pl.multiple_of((half * 4 + z_high * 2 + to_core) * 256, 256)
            value = jnp.dot(
                feat[...], decv[t, :, pl.ds(first, 256)], preferred_element_type=F32
            ).astype(BF16)
            for to_x in range(4):
                for z_low in range(2):
                    big, small = block_at(half, z_high * 2 + z_low, to_x)
                    at = (to_x * 2 + z_low) * ROWS
                    p[t, half, to_core, big, small] = value[at : at + ROWS]

    def part_copy(t, half):
        return send(p.at[t, half, 1 - core], rc.at[t, half], K_PART[t][half], partner)

    def part_add(t, half):
        part_copy(t, half).wait_recv()

        @pl.loop(0, 4)
        def _(b):
            p[t, half, core, b] = (
                p[t, half, core, b].astype(F32) + rc[t, half, b].astype(F32)
            ).astype(BF16)

    def big_sum_copy(t, half, o):
        return send(
            p.at[t, half, core, turn(big_pos[half], o)],
            big_in.at[t, half, o - 1],
            K_BIG[t][half],
            big_peers[half][o],
        )

    def all_big_sums(t, half):
        return send(p.at[t, half, core, 0:3], big_in.at[t, half], K_BIG[t][half], partner)

    def small_sum_copy(half, o):
        return send(
            r1.at[1, half, turn(small_pos[half], o)],
            small_in.at[half, o - 1],
            K_SMALL[half],
            small_peers[half][o],
        )

    def all_small_sums(half):
        return send(r1.at[1, half, 0:3], small_in.at[half], K_SMALL[half], partner)

    def final_copy(half, o, pair):
        return send(
            r1.at[0, half, turn(small_pos[half], o)],
            final_in.at[3 + o if pair else o - 1],
            K_FINAL,
            (pair_peers if pair else small_peers)[half][o],
        )

    def final_mine(mine, other):
        for o in OFFSETS:
            final_copy(mine, o, False).start()

    def final_other(mine, other):
        for o in (2, 1, 3, 0):
            final_copy(other, o, True).start()

    all_finals = send(final_in, final_in, K_FINAL, partner)

    def big_sum_send(t, half, offsets=OFFSETS):
        for o in offsets:
            big_sum_copy(t, half, o).start()

    def decode_slot(t, after):
        for half in HALVES:
            decode(t, 1 - core, half)
            part_copy(t, half).start()
        for half in HALVES:
            decode(t, core, half)
            part_add(t, half)
            after(half)

    def big_sum(t, half):
        all_big_sums(t, half).wait_recv()
        for i in range(4):
            value = p[t, half, core, big_pos[half], i].astype(F32)
            for o in OFFSETS:
                value = value + big_in[t, half, o - 1, i].astype(F32)
            r1[t, half, i] = value.astype(BF16)

    def small_sum(half):
        all_small_sums(half).wait_recv()
        value = r1[1, half, small_pos[half]].astype(F32)
        for o in OFFSETS:
            value = value + small_in[half, o - 1].astype(F32)
        r2[half] = value.astype(BF16)

    def cross_send(half, from_y):
        return send(
            r2.at[half],
            cross_in.at[from_y],
            K_CROSS[from_y],
            place(x, 2 + half, z, core),
        )

    @pl.when(first_layer)
    def _():
        decode_slot(1, lambda half: big_sum_send(1, half))

    def send_early(half):
        big_sum_send(0, half, [o for o in OFFSETS if o not in HELD])

        @pl.when(second_layer)
        def _():
            big_sum_send(0, half, HELD)

    decode_slot(0, send_early)

    @pl.loop(0, 4)
    def _(n):
        cols = pl.ds(pl.multiple_of(n * 256, 256), 256)
        ft[cols, :] = feat[:, cols].T

    ft_store = pltpu.make_async_copy(ft, ft_out, local_sem.at[0])
    ft_store.start()

    for half in HALVES:

        @pl.loop(0, 4)
        def _(m):
            z_high, to_core = lax.div(m, 2), lax.rem(m, 2)
            block = column_block(g, (0,), half, z_high, to_core)
            rows = pl.ds(pl.multiple_of((half * 4 + m) * 256, 256), 256)
            gt[rows, :] = block.T

    gt_store = pltpu.make_async_copy(gt, gt_out, local_sem.at[1])
    gt_store.start()

    @pl.when(first_layer)
    def _():
        for half in HALVES:
            big_sum(1, half)
            for o in OFFSETS:
                small_sum_copy(half, o).start()
        for half in HALVES:
            big_sum_send(0, half, HELD)
        for half in HALVES:
            small_sum(half)
            for from_y in (0, 1):

                @pl.when(yb == from_y)
                def _():
                    cross_send(half, from_y).start()

    def last_sums(mine, other):
        big_sum(0, other)
        final_other(mine, other)
        big_sum(0, mine)
        final_mine(mine, other)

    by_half(last_sums)

    tokens.drain(True)
    s0 = Gather(s, 0, K_GATHER[0])
    s1 = Gather(
        s, 1, K_GATHER[1], [(1, 3) if half in PASS else OFFSETS for half in HALVES]
    )

    def back_copy(to_y, half):
        big, small = block_at(half, z, x)
        return send(
            own_block(s),
            s.at[1, half, core, big, small],
            K_BACK[half],
            place(x, to_y, z, core),
        )

    def pass_copy(half):
        opposite = turn(big_pos[half], 2)
        return send(
            s.at[0, half, core, opposite],
            s.at[1, half, core, opposite],
            K_PASS[half],
            place(x, 3 - y, z, core),
        )

    tgt_copy.wait()
    all_finals.wait_recv()
    total = r1[0, yb, block_at(yb, z, x)[1]].astype(F32) - tgt[...].astype(F32)
    for i in range(7):
        total = total + final_in[i].astype(F32)
    rerr[...] = total

    @pl.when(second_layer)
    def _():
        for from_y in (0, 1):
            cross_send(0, from_y).wait_recv()
        rerr[...] = rerr[...] + cross_in[0].astype(F32) + cross_in[1].astype(F32)

    error = rerr[...]
    own_s = own_block(s)
    own_s[...] = (LOSS_SCALE / TOK * error).astype(BF16)

    @pl.when(second_layer)
    def _():
        for half in HALVES:

            @pl.when(yb == half)
            def _():
                for to_y in (0, 1):
                    back_copy(to_y, half).start()

    by_half(s0.joint)
    rerr_copy = pltpu.make_async_copy(rerr, rerr_out, local_sem.at[11])
    rerr_copy.start()

    square = error * error
    tile = jnp.zeros((8, 128), F32)
    for i in range(8):
        for j in range(2):
            tile = tile + square[i * 8 : i * 8 + 8, j * 128 : j * 128 + 128]

    def square_copy(stage, o):
        peers = ([None, partner], y_peers, x_peers, z_peers)[stage]
        pos = (core, y, x, z)[stage]
        return send(
            squares_own.at[stage], squares_in.at[stage, pos], K_SQUARE[stage], peers[o]
        )

    def square_offsets(stage):
        return (1, 2, 3) if stage > 0 else (1,)

    def all_squares(stage):
        ref = squares_in.at[stage, 0 : len(square_offsets(stage))]
        return send(ref, ref, K_SQUARE[stage], partner)

    def squares_start(stage, value):
        squares_own[stage] = value
        squares_in[stage, (core, y, x, z)[stage]] = value
        for o in square_offsets(stage):
            square_copy(stage, o).start()

    def squares_end(stage):
        all_squares(stage).wait_recv()
        value = squares_in[stage, 0]
        for i in range(1, 4 if stage > 0 else 2):
            value = value + squares_in[stage, i]
        return value

    squares_start(0, tile)

    def feature_grad(t, n):
        rows = pl.ds(pl.multiple_of(n * 256, 256), 256)
        return rows, lax.dot_general(
            all_columns(s, (t,)),
            decv[t, rows, :],
            (((1,), (1,)), ((), ())),
            preferred_element_type=F32,
        )

    def pg_copy(n):
        cols = pl.ds(pl.multiple_of(n * 256, 256), 256)
        return pltpu.make_async_copy(pg.at[:, cols], pg_out.at[:, cols], local_sem.at[7 + n])

    def grad_first(t):
        @pl.loop(0, 4, unroll=2)
        def _(n):
            cols, value = feature_grad(t, n)
            fg[:, cols] = value

    def grad_last(t, more):
        @pl.loop(0, 4, unroll=2)
        def _(n):
            cols, value = feature_grad(t, n)
            if more:
                value = fg[:, cols] + value
            grad = jnp.where(pre[:, cols] > 0.0, value, 0.0).astype(BF16)
            pg[:, cols] = grad
            bg[:, cols] = jnp.sum(grad.astype(F32), 0, keepdims=True)
            pg_copy(n).start()

    @pl.when(first_layer)
    def _():
        for half in HALVES:
            back_copy(0, half).wait_recv()
            s1.small(half)

    squares_start(1, squares_end(0))
    for t in ORDER:
        if t == 0:
            by_half(big_hops(s0))
        else:

            @pl.when(first_layer)
            def _():
                for half in HALVES:
                    s1.big(half)

    stores = [
        pltpu.make_async_copy(s.at[t], s_out.at[t], local_sem.at[5 + t]) for t in (0, 1)
    ]

    def share_slot(t):
        if t == 0:
            for half in HALVES:
                s0.share(half)
        else:
            for half in HALVES:
                s1.share(half)
            for half in PASS:
                pass_copy(half).wait_recv()
                s1.shared_copy(half, 2).start()

    def done_slot(t):
        (s0, s1)[t].done()
        stores[t].start()

    @pl.when(second_layer)
    def _():
        for half in HALVES:
            s0.big_copy(half, 2).wait_recv()
            if half in PASS:
                pass_copy(half).start()
            s0.shared_copy(half, 2).start()
        for half in HALVES:
            for o in (1, 3):
                s0.big_copy(half, o).wait_recv()
                s0.shared_copy(half, o).start()

    @pl.when(first_layer)
    def _():
        share_slot(ORDER[0])
        done_slot(ORDER[0])

    squares_start(2, squares_end(1))
    @pl.when(first_layer)
    def _():
        grad_first(ORDER[0])

    @pl.when(first_layer)
    def _():
        share_slot(ORDER[1])

    squares_start(3, squares_end(2))

    @pl.when(first_layer)
    def _():
        done_slot(ORDER[1])

    @pl.when(second_layer)
    def _():
        done_slot(0)

    @pl.when(first_layer)
    def _():
        grad_last(ORDER[1], True)

    @pl.when(second_layer)
    def _():
        grad_last(0, False)

    bg_copy = pltpu.make_async_copy(bg, bg_out, local_sem.at[13])
    bg_copy.start()
    squares_own[4] = squares_end(3)
    squares_copy = pltpu.make_async_copy(squares_own.at[4], squares_out, local_sem.at[12])
    squares_copy.start()

    def drain_sums(t):
        for half in HALVES:
            part_copy(t, half).wait_send()
            all_big_sums(t, half).wait_send()

    drain_sums(0)
    all_finals.wait_send()
    s0.drain(True)
    for stage in range(4):
        all_squares(stage).wait_send()

    @pl.when(first_layer)
    def _():
        drain_sums(1)
        s1.drain(False)
        for half in HALVES:
            all_small_sums(half).wait_send()
            for from_y in (0, 1):

                @pl.when(yb == from_y)
                def _():
                    cross_send(half, from_y).wait_send()

        stores[1].wait()

    @pl.when(second_layer)
    def _():
        for half in HALVES:

            @pl.when(yb == half)
            def _():
                for to_y in (0, 1):
                    back_copy(to_y, half).wait_send()

            if half in PASS:
                pass_copy(half).wait_send()

    stores[0].wait()
    rerr_copy.wait()
    squares_copy.wait()
    bg_copy.wait()
    ft_store.wait()
    gt_store.wait()
    for n in range(4):
        pg_copy(n).wait()


def weight_grads_kernel(
    gt_in, ft_in, s_in, pg_in, rerr_in, squares_in, bg_in,
    dec_grad, enc_grad, rerr_out, mean_out, bg_out,
    gt, ft, s, pg, rerr, squares, mean, bg, dec_out, enc_out,
    in_sem, dec_sem, enc_sem, small_sem,
):
    y = lax.div(lax.axis_index("layer"), 4)
    first_layer = y < 2
    second_layer = y >= 2
    ft_copy = pltpu.make_async_copy(ft_in, ft, in_sem.at[0])
    s_copies = [
        [
            pltpu.make_async_copy(s_in.at[t, half], s.at[t, half], in_sem.at[1 + 2 * t + half])
            for half in (0, 1)
        ]
        for t in (0, 1)
    ]
    pg_copy = pltpu.make_async_copy(pg_in, pg, in_sem.at[5])
    gt_copy = pltpu.make_async_copy(gt_in, gt, in_sem.at[6])
    ft_copy.start()
    for copy in s_copies[0]:
        copy.start()

    @pl.when(first_layer)
    def _():
        for copy in s_copies[1]:
            copy.start()

    pg_copy.start()
    gt_copy.start()
    small_in = [
        pltpu.make_async_copy(src, dst, small_sem.at[i])
        for i, (src, dst) in enumerate(((rerr_in, rerr), (squares_in, squares), (bg_in, bg)))
    ]
    small_out = [
        pltpu.make_async_copy(src, dst, small_sem.at[3 + i])
        for i, (src, dst) in enumerate(((rerr, rerr_out), (mean, mean_out), (bg, bg_out)))
    ]
    for copy in small_in:
        copy.start()

    def dec_copy(t, m):
        cols = pl.ds(pl.multiple_of(m * 256, 256), 256)
        return pltpu.make_async_copy(
            dec_out.at[t, m], dec_grad.at[t, :, cols], dec_sem.at[t, m]
        )

    def dec_half(t, half):
        s_copies[t][half].wait()

        @pl.loop(0, 4, unroll=4)
        def _(i):
            m = half * 4 + i
            block = column_block(s, (t,), half, lax.div(i, 2), lax.rem(i, 2))
            dec_out[t, m] = jnp.dot(
                ft[...], block, preferred_element_type=F32
            ).astype(BF16)
            dec_copy(t, m).start()

    @pl.when(second_layer)
    def _():
        @pl.loop(0, 8)
        def _(m):
            dec_out[1, m] = jnp.zeros((SHARD, 256), BF16)
            dec_copy(1, m).start()

    ft_copy.wait()
    dec_half(0, 0)
    dec_half(0, 1)

    @pl.when(first_layer)
    def _():
        dec_half(1, 0)
        dec_half(1, 1)

    for copy in small_in:
        copy.wait()
    mean[...] = jnp.sum(squares[...], keepdims=True) / (LAYERS * TOK * D)
    for copy in small_out:
        copy.start()
    pg_copy.wait()
    gt_copy.wait()

    def enc_copy(n):
        rows = pl.ds(pl.multiple_of(n * 512, 512), 512)
        return pltpu.make_async_copy(
            enc_out.at[rows, :], enc_grad.at[rows, :], enc_sem.at[n]
        )

    @pl.loop(0, 4, unroll=2)
    def _(n):
        rows = pl.ds(pl.multiple_of(n * 512, 512), 512)
        enc_out[rows, :] = jnp.dot(
            gt[rows, :], pg[...], preferred_element_type=F32
        ).astype(BF16)
        enc_copy(n).start()

    for t in (0, 1):
        for m in range(8):
            dec_copy(t, m).wait()
    for n in range(4):
        enc_copy(n).wait()
    for copy in small_out:
        copy.wait()


def on_device(tokens_in, targets, enc_weight, enc_bias, dec_weight):
    anywhere = pl.BlockSpec(memory_space=pl.ANY)
    shape = jax.ShapeDtypeStruct
    blocks = (2, 2, 4, 4, ROWS, COLS)
    rerr, squares, gt, ft, s, pg, bg = pl.pallas_call(
        step_kernel,
        out_shape=(
            shape((ROWS, COLS), F32),
            shape((8, 128), F32),
            shape((D, TOK), BF16),
            shape((SHARD, TOK), BF16),
            shape((2, *blocks), BF16),
            shape((TOK, SHARD), BF16),
            shape((1, SHARD), F32),
        ),
        in_specs=[anywhere] * 5,
        out_specs=[anywhere] * 7,
        scratch_shapes=[
            pltpu.VMEM((ROWS, COLS), BF16),
            pltpu.VMEM((1, SHARD), F32),
            pltpu.VMEM((ROWS, COLS), F32),
            pltpu.VMEM((1, SHARD), F32),
            pltpu.VMEM((D, SHARD), BF16),
            pltpu.VMEM((2, SHARD, D), BF16),
            pltpu.VMEM((1, *blocks), BF16),
            pltpu.VMEM((TOK, SHARD), F32),
            pltpu.VMEM((TOK, SHARD), BF16),
            pltpu.VMEM((2, *blocks), BF16),
            pltpu.VMEM((2, 2, 4, 4, ROWS, COLS), BF16),
            pltpu.VMEM((2, 2, 3, 4, ROWS, COLS), BF16),
            pltpu.VMEM((2, 2, 4, ROWS, COLS), BF16),
            pltpu.VMEM((2, 3, ROWS, COLS), BF16),
            pltpu.VMEM((2, ROWS, COLS), BF16),
            pltpu.VMEM((7, ROWS, COLS), BF16),
            pltpu.VMEM((2, ROWS, COLS), BF16),
            pltpu.VMEM((2, *blocks), BF16),
            pltpu.VMEM((TOK, SHARD), F32),
            pltpu.VMEM((D, TOK), BF16),
            pltpu.VMEM((SHARD, TOK), BF16),
            pltpu.VMEM((TOK, SHARD), BF16),
            pltpu.VMEM((4, 4, 8, 128), F32),
            pltpu.VMEM((5, 8, 128), F32),
            pltpu.SemaphoreType.DMA((K_COUNT,)),
            pltpu.SemaphoreType.DMA((K_COUNT,)),
            pltpu.SemaphoreType.DMA((14,)),
        ],
        compiler_params=pltpu.CompilerParams(
            collective_id=0, has_side_effects=True, vmem_limit_bytes=60 * 2**20
        ),
        name="step",
    )(tokens_in, targets, enc_weight, enc_bias.reshape(1, SHARD), dec_weight)

    dec_grad, enc_grad, rerr, mean, bg = pl.pallas_call(
        weight_grads_kernel,
        out_shape=(
            shape((2, SHARD, D), BF16),
            shape((D, SHARD), BF16),
            shape((ROWS, COLS), F32),
            shape((1, 1), F32),
            shape((1, SHARD), F32),
        ),
        in_specs=[anywhere] * 7,
        out_specs=[anywhere] * 5,
        scratch_shapes=[
            pltpu.VMEM((D, TOK), BF16),
            pltpu.VMEM((SHARD, TOK), BF16),
            pltpu.VMEM((2, *blocks), BF16),
            pltpu.VMEM((TOK, SHARD), BF16),
            pltpu.VMEM((ROWS, COLS), F32),
            pltpu.VMEM((8, 128), F32),
            pltpu.VMEM((1, 1), F32),
            pltpu.VMEM((1, SHARD), F32),
            pltpu.VMEM((2, 8, SHARD, 256), BF16),
            pltpu.VMEM((D, SHARD), BF16),
            pltpu.SemaphoreType.DMA((7,)),
            pltpu.SemaphoreType.DMA((2, 8)),
            pltpu.SemaphoreType.DMA((4,)),
            pltpu.SemaphoreType.DMA((6,)),
        ],
        compiler_params=pltpu.CompilerParams(vmem_limit_bytes=60 * 2**20),
        name="weight_grads",
    )(gt, ft, s, pg, rerr, squares, bg)
    return (rerr, mean.reshape(()), enc_grad, bg.reshape(SHARD), dec_grad)


def solution(mesh):
    placed = (
        P("feat", "layer"),
        P("feat", "layer"),
        P(None, ("layer", "feat")),
        P(("layer", "feat")),
        P(None, ("layer", "feat"), None),
    )
    return jax.shard_map(
        on_device,
        mesh=mesh,
        in_specs=placed,
        out_specs=(
            P("feat", "layer"),
            P(),
            P(None, ("layer", "feat")),
            P(("layer", "feat")),
            P(None, ("layer", "feat"), None),
        ),
        check_vma=False,
    )
```

```python
import jax
import jax.numpy as jnp
from jax import lax
from jax.experimental import pallas as pl
from jax.experimental.pallas import tpu as pltpu
from jax.sharding import PartitionSpec as P

D = 2048
LAYERS = 2
TOK = 512
SHARD = 1024
ROWS = 64
COLS = 256
LOSS_SCALE = 64.0
MESH = pl.DeviceIdType.MESH
FORWARD_TOKENS = False
FORWARD_SCALED = False
PASS = (0, 1)
ORDER = (0, 1)
EARLY = True
EARLY1 = True
BF16 = jnp.bfloat16
F32 = jnp.float32


def place(x, y, z, core):
    return (y * 4 + lax.div(z, 2) * 2 + core, x * 2 + lax.rem(z, 2))


def block_at(half, z, x):
    return z * (1 - half) + x * half, x * (1 - half) + z * half


def column_block(ref, lead, half, z_high, core):
    pieces = []
    for x in range(4):
        for z_low in range(2):
            big, small = block_at(half, z_high * 2 + z_low, x)
            pieces.append(ref[(*lead, half, core, big, small)])
    return jnp.concatenate(pieces, 0)


def core_columns(ref, lead, core):
    return jnp.concatenate(
        [column_block(ref, lead, m // 2, m % 2, core) for m in range(4)], 1
    )


def all_columns(ref, lead):
    return jnp.concatenate(
        [column_block(ref, lead, m // 4, m // 2 % 2, m % 2) for m in range(8)], 1
    )


def core_shards(core):
    return [pl.ds(pl.multiple_of((m * 2 + core) * 256, 256), 256) for m in range(4)]


class Numbers:
    def __init__(self):
        self.count = 0

    def take(self, *dims):
        if not dims:
            self.count += 1
            return self.count - 1
        return [self.take(*dims[1:]) for _ in range(dims[0])]


NUMBERS = Numbers()
def gather_numbers():
    return dict(
        small=NUMBERS.take(2),
        big=NUMBERS.take(2, 4),
        shared=NUMBERS.take(),
    )


K_GATHER = [gather_numbers(), gather_numbers()]
K_PART = NUMBERS.take(2, 2)
K_TURN = NUMBERS.take(2, 2)
K_BIG = NUMBERS.take(2, 2)
K_SMALL = NUMBERS.take(2)
K_FINAL = NUMBERS.take()
K_CROSS = NUMBERS.take(2)
K_BACK = NUMBERS.take(2)
K_PASS = NUMBERS.take(2)
K_SQUARE = NUMBERS.take(4)
K_COUNT = NUMBERS.count


def step_kernel(
    tok, tgt_in, enc, bias_in, dec,
    rerr_out, squares_out, gt_out, ft_out, s_out, pg_out, bg_out,
    tgt, bias, rerr, bg, encv, decv, g, pre, feat, p, rc, turn_in, big_in, r1, small_in, r2, final_in, cross_in,
    s, fg, gt, ft, pg, squares_in, squares_own, send_sem, recv_sem, local_sem,
):
    me_layer = lax.axis_index("layer")
    me_feat = lax.axis_index("feat")
    core = lax.rem(me_layer, 2)
    y = lax.div(me_layer, 4)
    x = lax.div(me_feat, 2)
    z = lax.rem(lax.div(me_layer, 2), 2) * 2 + lax.rem(me_feat, 2)
    yb = lax.rem(y, 2)
    first_layer = y < 2
    second_layer = y >= 2

    def turn(v, step):
        return lax.rem(v + step, 4)

    partner = place(x, y, z, 1 - core)
    y_pair = y + 1 - 2 * yb
    x_peers = [None] + [place(turn(x, o), y, z, core) for o in (1, 2, 3)]
    y_peers = [None] + [place(x, turn(y, o), z, core) for o in (1, 2, 3)]
    z_peers = [None] + [place(x, y, turn(z, o), core) for o in (1, 2, 3)]
    big_pos, small_pos = (z, x), (x, z)
    big_peers, small_peers = (z_peers, x_peers), (x_peers, z_peers)
    pair_peers = (
        [place(turn(x, o), y_pair, z, core) for o in range(4)],
        [place(x, y_pair, turn(z, o), core) for o in range(4)],
    )
    HALVES = (0, 1)
    OFFSETS = (2, 1, 3)

    def send(src, dst, number, device):
        return pltpu.make_async_remote_copy(
            src_ref=src,
            dst_ref=dst,
            send_sem=send_sem.at[number],
            recv_sem=recv_sem.at[number],
            device_id=device,
            device_id_type=MESH,
        )

    def own_block(buf):
        big, small = block_at(yb, z, x)
        return buf.at[0, yb, core, big, small]

    enc_copy = pltpu.make_async_copy(enc, encv, local_sem.at[0])
    dec_copy = pltpu.make_async_copy(dec, decv, local_sem.at[1])
    tok_copy = pltpu.make_async_copy(tok, own_block(g), local_sem.at[2])
    tgt_copy = pltpu.make_async_copy(tgt_in, tgt, local_sem.at[3])
    bias_copy = pltpu.make_async_copy(bias_in, bias, local_sem.at[4])
    tok_copy.start()
    enc_copy.start()
    dec_copy.start()
    tgt_copy.start()
    bias_copy.start()

    barrier = pltpu.get_barrier_semaphore()
    for device in (
        partner,
        *x_peers[1:],
        *y_peers[1:],
        *z_peers[1:],
        *pair_peers[0][1:],
        *pair_peers[1][1:],
    ):
        pl.semaphore_signal(barrier, inc=1, device_id=device, device_id_type=MESH)
    tok_copy.wait()
    pl.semaphore_wait(barrier, 16)

    class Gather:
        def __init__(self, buf, t, numbers, offsets=(OFFSETS, OFFSETS), forward=False):
            self.forward = forward
            if forward:
                offsets = ((1, 3), (1, 3))
            self.buf, self.t, self.numbers = buf, t, numbers
            self.offsets = offsets

        def piece(self, half):
            return self.buf.at[self.t, half, core, big_pos[half], small_pos[half]]

        def chunk(self, half, i):
            return self.buf.at[self.t, half, core, i]

        def small_copy(self, half, o):
            ref = self.piece(half)
            return send(ref, ref, self.numbers["small"][half], small_peers[half][o])

        def pair_copy(self, half, o):
            ref = self.piece(half)
            return send(ref, ref, self.numbers["small"][half], pair_peers[half][o])

        def all_small(self, half, count=3):
            ref = self.buf.at[self.t, half, core, 0, 0:count]
            return send(ref, ref, self.numbers["small"][half], partner)

        def all_joint(self, half):
            return send(final_in, final_in, self.numbers["small"][half], partner)

        def joint(self, mine, other):
            for o in (2, 1, 3, 0):
                self.pair_copy(mine, o).start()
                if o > 0:
                    self.small_copy(mine, o).start()
            if EARLY:
                self.early(mine)

        def big_copy(self, half, o):
            ref = self.chunk(half, big_pos[half])
            return send(ref, ref, self.numbers["big"][half][o], big_peers[half][o])

        def piece_copy(self, half, o, i):
            ref = self.buf.at[self.t, half, core, big_pos[half], i]
            return send(ref, ref, self.numbers["big"][half][o], big_peers[half][o])

        def early(self, half):
            for o in self.offsets[half]:
                self.piece_copy(half, o, small_pos[half]).start()

        def shared_copy(self, half, o):
            ref = self.chunk(half, turn(big_pos[half], 4 - o))
            return send(ref, ref, self.numbers["shared"], partner)

        def all_shared(self, of_core):
            ref = self.buf.at[self.t, :, of_core]
            return send(ref, ref, self.numbers["shared"], partner)

        def small(self, half):
            for o in OFFSETS:
                self.small_copy(half, o).start()

        def big(self, half, count=3, early=False):
            self.all_small(half, count).wait_recv()
            for o in self.offsets[half]:
                if not early:
                    self.big_copy(half, o).start()
                for d in OFFSETS if early else ():
                    self.piece_copy(half, o, turn(small_pos[half], d)).start()
            self.shared_copy(half, 0).start()

        def forward_copy(self, half, o):
            part = pl.ds(0 if o == 1 else 2, 2)
            ref = self.buf.at[self.t, half, core, turn(big_pos[half], 4 - o), part]
            return send(ref, ref, self.numbers["big"][half][2], big_peers[half][o])

        def share(self, half):
            for o in self.offsets[half]:
                self.big_copy(half, o).wait_recv()
                if self.forward:
                    self.forward_copy(half, o).start()
                self.shared_copy(half, o).start()

        def share_opposite(self, half):
            if self.forward:
                self.big_copy(half, 2).wait_recv()
                self.shared_copy(half, 2).start()

        def done(self):
            self.all_shared(1 - core).wait_recv()

        def drain(self, joint):
            if joint:
                by_half(lambda mine, other: self.all_joint(mine).wait_send())
            for half in HALVES:
                if not joint:
                    self.all_small(half).wait_send()
                for o in OFFSETS if self.forward else self.offsets[half]:
                    self.big_copy(half, o).wait_send()
            self.all_shared(core).wait_send()

    def by_half(fn):
        @pl.when(yb == 0)
        def _():
            fn(0, 1)

        @pl.when(yb == 1)
        def _():
            fn(1, 0)

    tokens = Gather(g, 0, K_GATHER[0], forward=FORWARD_TOKENS)
    by_half(tokens.joint)

    def big_hops(gather):
        def run(mine, other):
            gather.big(mine, 3, EARLY)
            gather.big(other, 4)

        return run

    by_half(big_hops(tokens))

    def share_hops(gather):
        def run(mine, other):
            gather.share(mine)
            gather.share(other)
            gather.share_opposite(mine)
            gather.share_opposite(other)

        return run

    by_half(share_hops(tokens))
    enc_copy.wait()
    bias_copy.wait()

    def encode_part(from_core, n):
        cols = pl.ds(pl.multiple_of(n * 256, 256), 256)
        weights = jnp.concatenate([encv[rows, cols] for rows in core_shards(from_core)], 0)
        return cols, jnp.dot(
            core_columns(g, (0,), from_core), weights, preferred_element_type=F32
        )

    @pl.loop(0, 4, unroll=2)
    def _(n):
        cols, value = encode_part(core, n)
        pre[:, cols] = value + bias[:, cols]

    tokens.done()

    @pl.loop(0, 4, unroll=2)
    def _(n):
        cols, value = encode_part(1 - core, n)
        act = pre[:, cols] + value
        pre[:, cols] = act
        feat[:, cols] = jnp.maximum(act, 0.0).astype(BF16)

    dec_copy.wait()

    def decode(t, to_core, half):
        for z_high in range(2):
            first = pl.multiple_of((half * 4 + z_high * 2 + to_core) * 256, 256)
            value = jnp.dot(
                feat[...], decv[t, :, pl.ds(first, 256)], preferred_element_type=F32
            ).astype(BF16)
            for to_x in range(4):
                for z_low in range(2):
                    big, small = block_at(half, z_high * 2 + z_low, to_x)
                    at = (to_x * 2 + z_low) * ROWS
                    p[t, half, to_core, big, small] = value[at : at + ROWS]

    def part_copy(t, half):
        return send(p.at[t, half, 1 - core], rc.at[t, half], K_PART[t][half], partner)

    def part_add(t, half):
        part_copy(t, half).wait_recv()

        @pl.loop(0, 4)
        def _(b):
            p[t, half, core, b] = (
                p[t, half, core, b].astype(F32) + rc[t, half, b].astype(F32)
            ).astype(BF16)

    LOW, HIGH = pl.ds(0, 2), pl.ds(2, 2)

    def chunk_sum(t, half, o, part):
        return p.at[t, half, core, turn(big_pos[half], o), part]

    def turn_copies(t, half):
        return [
            send(
                chunk_sum(t, half, 2, part),
                turn_in.at[t, half, i],
                K_TURN[t][half],
                big_peers[half][o],
            )
            for i, (part, o) in enumerate(((LOW, 1), (HIGH, 3)))
        ]

    def direct_copies(t, half):
        return [
            send(
                chunk_sum(t, half, o, part), big_in.at[t, half, i], K_BIG[t][half], big_peers[half][o]
            )
            for i, part, o in ((0, LOW, 3), (2, HIGH, 1))
        ]

    def summed_copies(t, half):
        return [
            send(
                chunk_sum(t, half, o, part), big_in.at[t, half, i], K_BIG[t][half], big_peers[half][o]
            )
            for i, part, o in ((1, LOW, 1), (3, HIGH, 3))
        ]

    def all_turns(t, half):
        return send(turn_in.at[t, half], turn_in.at[t, half], K_TURN[t][half], partner)

    def all_big_sums(t, half):
        return send(big_in.at[t, half], big_in.at[t, half], K_BIG[t][half], partner)

    def big_start(t, half):
        for copy in (*turn_copies(t, half), *direct_copies(t, half)):
            copy.start()

    def big_mid(t, half):
        all_turns(t, half).wait_recv()
        for i, (part, o) in enumerate(((LOW, 1), (HIGH, 3))):
            ref = chunk_sum(t, half, o, part)
            ref[...] = (ref[...].astype(F32) + turn_in[t, half, i].astype(F32)).astype(BF16)
            summed_copies(t, half)[i].start()

    def big_sum(t, half):
        all_big_sums(t, half).wait_recv()
        for i in range(4):
            first = i // 2 * 2
            r1[t, half, i] = (
                p[t, half, core, big_pos[half], i].astype(F32)
                + big_in[t, half, first, i % 2].astype(F32)
                + big_in[t, half, first + 1, i % 2].astype(F32)
            ).astype(BF16)

    def small_sum_copy(half, o):
        return send(
            r1.at[1, half, turn(small_pos[half], o)],
            small_in.at[half, o - 1],
            K_SMALL[half],
            small_peers[half][o],
        )

    def all_small_sums(half):
        return send(r1.at[1, half, 0:3], small_in.at[half], K_SMALL[half], partner)

    def final_copy(half, o, pair):
        return send(
            r1.at[0, half, turn(small_pos[half], o)],
            final_in.at[3 + o if pair else o - 1],
            K_FINAL,
            (pair_peers if pair else small_peers)[half][o],
        )

    def final_mine(mine, other):
        for o in OFFSETS:
            final_copy(mine, o, False).start()

    def final_other(mine, other):
        for o in (2, 1, 3, 0):
            final_copy(other, o, True).start()

    all_finals = send(final_in, final_in, K_FINAL, partner)

    def decode_slot(t, between=None):
        for half in HALVES:
            decode(t, 1 - core, half)
            part_copy(t, half).start()
        for half in HALVES:
            decode(t, core, half)
            part_add(t, half)
            if between is None:
                big_start(t, half)
        if between is not None:
            between()
            for half in HALVES:
                big_start(t, half)

    def small_sum(half):
        all_small_sums(half).wait_recv()
        value = r1[1, half, small_pos[half]].astype(F32)
        for o in OFFSETS:
            value = value + small_in[half, o - 1].astype(F32)
        r2[half] = value.astype(BF16)

    def cross_send(half, from_y):
        return send(
            r2.at[half],
            cross_in.at[from_y],
            K_CROSS[from_y],
            place(x, 2 + half, z, core),
        )

    @pl.when(first_layer)
    def _():
        decode_slot(1)

    def first_turns():
        @pl.when(first_layer)
        def _():
            for half in HALVES:
                big_mid(1, half)

    decode_slot(0, first_turns)

    @pl.loop(0, 4)
    def _(n):
        cols = pl.ds(pl.multiple_of(n * 256, 256), 256)
        ft[cols, :] = feat[:, cols].T

    ft_store = pltpu.make_async_copy(ft, ft_out, local_sem.at[0])
    ft_store.start()

    for half in HALVES:

        @pl.loop(0, 4)
        def _(m):
            z_high, to_core = lax.div(m, 2), lax.rem(m, 2)
            block = column_block(g, (0,), half, z_high, to_core)
            rows = pl.ds(pl.multiple_of((half * 4 + m) * 256, 256), 256)
            gt[rows, :] = block.T

    gt_store = pltpu.make_async_copy(gt, gt_out, local_sem.at[1])
    gt_store.start()

    @pl.when(first_layer)
    def _():
        for half in HALVES:
            big_sum(1, half)
            for o in OFFSETS:
                small_sum_copy(half, o).start()

    for half in HALVES:
        big_mid(0, half)

    @pl.when(first_layer)
    def _():
        for half in HALVES:
            small_sum(half)
            for from_y in (0, 1):

                @pl.when(yb == from_y)
                def _():
                    cross_send(half, from_y).start()

    def last_sums(mine, other):
        big_sum(0, other)
        final_other(mine, other)
        big_sum(0, mine)
        final_mine(mine, other)

    by_half(last_sums)

    tokens.drain(True)
    s0 = Gather(s, 0, K_GATHER[0], forward=FORWARD_SCALED)
    s1 = Gather(
        s, 1, K_GATHER[1], [(1, 3) if half in PASS else OFFSETS for half in HALVES]
    )

    def back_copy(to_y, half):
        big, small = block_at(half, z, x)
        return send(
            own_block(s),
            s.at[1, half, core, big, small],
            K_BACK[half],
            place(x, to_y, z, core),
        )

    def pass_copy(half):
        opposite = turn(big_pos[half], 2)
        return send(
            s.at[0, half, core, opposite],
            s.at[1, half, core, opposite],
            K_PASS[half],
            place(x, 3 - y, z, core),
        )

    tgt_copy.wait()
    all_finals.wait_recv()
    total = r1[0, yb, block_at(yb, z, x)[1]].astype(F32) - tgt[...].astype(F32)
    for i in range(7):
        total = total + final_in[i].astype(F32)
    rerr[...] = total

    @pl.when(second_layer)
    def _():
        for from_y in (0, 1):
            cross_send(0, from_y).wait_recv()
        rerr[...] = rerr[...] + cross_in[0].astype(F32) + cross_in[1].astype(F32)

    error = rerr[...]
    own_s = own_block(s)
    own_s[...] = (LOSS_SCALE / TOK * error).astype(BF16)

    @pl.when(second_layer)
    def _():
        for half in HALVES:

            @pl.when(yb == half)
            def _():
                for to_y in (0, 1):
                    back_copy(to_y, half).start()

    by_half(s0.joint)
    rerr_copy = pltpu.make_async_copy(rerr, rerr_out, local_sem.at[11])
    rerr_copy.start()

    square = error * error
    tile = jnp.zeros((8, 128), F32)
    for i in range(8):
        for j in range(2):
            tile = tile + square[i * 8 : i * 8 + 8, j * 128 : j * 128 + 128]

    def square_copy(stage, o):
        peers = ([None, partner], y_peers, x_peers, z_peers)[stage]
        pos = (core, y, x, z)[stage]
        return send(
            squares_own.at[stage], squares_in.at[stage, pos], K_SQUARE[stage], peers[o]
        )

    def square_offsets(stage):
        return (1, 2, 3) if stage > 0 else (1,)

    def all_squares(stage):
        ref = squares_in.at[stage, 0 : len(square_offsets(stage))]
        return send(ref, ref, K_SQUARE[stage], partner)

    def squares_start(stage, value):
        squares_own[stage] = value
        squares_in[stage, (core, y, x, z)[stage]] = value
        for o in square_offsets(stage):
            square_copy(stage, o).start()

    def squares_end(stage):
        all_squares(stage).wait_recv()
        value = squares_in[stage, 0]
        for i in range(1, 4 if stage > 0 else 2):
            value = value + squares_in[stage, i]
        return value

    squares_start(0, tile)

    def feature_grad(t, n):
        rows = pl.ds(pl.multiple_of(n * 256, 256), 256)
        return rows, lax.dot_general(
            all_columns(s, (t,)),
            decv[t, rows, :],
            (((1,), (1,)), ((), ())),
            preferred_element_type=F32,
        )

    def feature_grad_part(t, from_core, n):
        rows = pl.ds(pl.multiple_of(n * 256, 256), 256)
        weights = jnp.concatenate(
            [decv[t, rows, cols] for cols in core_shards(from_core)], 1
        )
        return rows, lax.dot_general(
            core_columns(s, (t,), from_core),
            weights,
            (((1,), (1,)), ((), ())),
            preferred_element_type=F32,
        )

    def pg_copy(n):
        cols = pl.ds(pl.multiple_of(n * 256, 256), 256)
        return pltpu.make_async_copy(pg.at[:, cols], pg_out.at[:, cols], local_sem.at[7 + n])

    def grad_first(t):
        @pl.loop(0, 4, unroll=2)
        def _(n):
            cols, value = feature_grad(t, n)
            fg[:, cols] = value

    def grad_half(t, from_core, more):
        @pl.loop(0, 4, unroll=2)
        def _(n):
            cols, value = feature_grad_part(t, from_core, n)
            fg[:, cols] = fg[:, cols] + value if more else value

    def grad_last(t, from_core):
        @pl.loop(0, 4, unroll=2)
        def _(n):
            cols, value = feature_grad_part(t, from_core, n)
            grad = jnp.where(pre[:, cols] > 0.0, fg[:, cols] + value, 0.0).astype(BF16)
            pg[:, cols] = grad
            bg[:, cols] = jnp.sum(grad.astype(F32), 0, keepdims=True)
            pg_copy(n).start()

    @pl.when(first_layer)
    def _():
        for half in HALVES:
            back_copy(0, half).wait_recv()
            s1.small(half)
            if EARLY1:
                s1.early(half)

    squares_start(1, squares_end(0))
    for t in ORDER:
        if t == 0:
            by_half(big_hops(s0))
        else:

            @pl.when(first_layer)
            def _():
                for half in HALVES:
                    s1.big(half, 3, EARLY1)

    stores = [
        pltpu.make_async_copy(s.at[t], s_out.at[t], local_sem.at[5 + t]) for t in (0, 1)
    ]

    def share_slot(t):
        if t == 0:
            for half in HALVES:
                s0.share(half)
            for half in HALVES:
                s0.share_opposite(half)
        else:
            for half in HALVES:
                s1.share(half)
            for half in PASS:
                pass_copy(half).wait_recv()
                s1.shared_copy(half, 2).start()

    def done_slot(t):
        (s0, s1)[t].done()
        stores[t].start()

    @pl.when(second_layer)
    def _():
        if FORWARD_SCALED:
            for half in HALVES:
                s0.share(half)
        for half in HALVES:
            s0.big_copy(half, 2).wait_recv()
            if half in PASS:
                pass_copy(half).start()
            s0.shared_copy(half, 2).start()
        if not FORWARD_SCALED:
            for half in HALVES:
                for o in (1, 3):
                    s0.big_copy(half, o).wait_recv()
                    s0.shared_copy(half, o).start()

    @pl.when(first_layer)
    def _():
        share_slot(ORDER[0])
        done_slot(ORDER[0])

    squares_start(2, squares_end(1))
    @pl.when(first_layer)
    def _():
        grad_first(ORDER[0])

    @pl.when(first_layer)
    def _():
        share_slot(ORDER[1])

    squares_start(3, squares_end(2))

    @pl.when(first_layer)
    def _():
        grad_half(ORDER[1], core, True)

    @pl.when(second_layer)
    def _():
        grad_half(0, core, False)


    @pl.when(first_layer)
    def _():
        done_slot(ORDER[1])

    @pl.when(second_layer)
    def _():
        done_slot(0)

    @pl.when(first_layer)
    def _():
        grad_last(ORDER[1], 1 - core)

    @pl.when(second_layer)
    def _():
        grad_last(0, 1 - core)

    bg_copy = pltpu.make_async_copy(bg, bg_out, local_sem.at[13])
    bg_copy.start()
    squares_own[4] = squares_end(3)
    squares_copy = pltpu.make_async_copy(squares_own.at[4], squares_out, local_sem.at[12])
    squares_copy.start()

    def drain_sums(t):
        for half in HALVES:
            part_copy(t, half).wait_send()
            all_turns(t, half).wait_send()
            all_big_sums(t, half).wait_send()

    drain_sums(0)
    all_finals.wait_send()
    s0.drain(True)
    for stage in range(4):
        all_squares(stage).wait_send()

    @pl.when(first_layer)
    def _():
        drain_sums(1)
        s1.drain(False)
        for half in HALVES:
            all_small_sums(half).wait_send()
            for from_y in (0, 1):

                @pl.when(yb == from_y)
                def _():
                    cross_send(half, from_y).wait_send()

        stores[1].wait()

    @pl.when(second_layer)
    def _():
        for half in HALVES:

            @pl.when(yb == half)
            def _():
                for to_y in (0, 1):
                    back_copy(to_y, half).wait_send()

            if half in PASS:
                pass_copy(half).wait_send()

    stores[0].wait()
    rerr_copy.wait()
    squares_copy.wait()
    bg_copy.wait()
    ft_store.wait()
    gt_store.wait()
    for n in range(4):
        pg_copy(n).wait()


def weight_grads_kernel(
    gt_in, ft_in, s_in, pg_in, rerr_in, squares_in, bg_in,
    dec_grad, enc_grad, rerr_out, mean_out, bg_out,
    gt, ft, s, pg, rerr, squares, mean, bg, dec_out, enc_out,
    in_sem, dec_sem, enc_sem, small_sem,
):
    y = lax.div(lax.axis_index("layer"), 4)
    first_layer = y < 2
    second_layer = y >= 2
    ft_copy = pltpu.make_async_copy(ft_in, ft, in_sem.at[0])
    s_copies = [
        [
            pltpu.make_async_copy(s_in.at[t, half], s.at[t, half], in_sem.at[1 + 2 * t + half])
            for half in (0, 1)
        ]
        for t in (0, 1)
    ]
    pg_copy = pltpu.make_async_copy(pg_in, pg, in_sem.at[5])
    gt_copy = pltpu.make_async_copy(gt_in, gt, in_sem.at[6])
    ft_copy.start()
    for copy in s_copies[0]:
        copy.start()

    small_in = [
        pltpu.make_async_copy(src, dst, small_sem.at[i])
        for i, (src, dst) in enumerate(((rerr_in, rerr), (squares_in, squares), (bg_in, bg)))
    ]
    small_out = [
        pltpu.make_async_copy(src, dst, small_sem.at[3 + i])
        for i, (src, dst) in enumerate(((rerr, rerr_out), (mean, mean_out), (bg, bg_out)))
    ]

    def dec_copy(t, m):
        cols = pl.ds(pl.multiple_of(m * 256, 256), 256)
        return pltpu.make_async_copy(
            dec_out.at[t, m], dec_grad.at[t, :, cols], dec_sem.at[t, m]
        )

    def dec_half(t, half):
        s_copies[t][half].wait()

        @pl.loop(0, 4, unroll=4)
        def _(i):
            m = half * 4 + i
            block = column_block(s, (t,), half, lax.div(i, 2), lax.rem(i, 2))
            dec_out[t, m] = jnp.dot(
                ft[...], block, preferred_element_type=F32
            ).astype(BF16)
            dec_copy(t, m).start()

    ft_copy.wait()

    @pl.when(first_layer)
    def _():
        for copy in s_copies[1]:
            copy.start()

    gt_copy.start()
    pg_copy.start()
    for copy in small_in:
        copy.start()
    dec_half(0, 0)
    dec_half(0, 1)

    @pl.when(first_layer)
    def _():
        dec_half(1, 0)
        dec_half(1, 1)

    @pl.when(second_layer)
    def _():
        @pl.loop(0, 8)
        def _(m):
            dec_out[1, m] = jnp.zeros((SHARD, 256), BF16)
            dec_copy(1, m).start()

    for copy in small_in:
        copy.wait()
    mean[...] = jnp.sum(squares[...], keepdims=True) / (LAYERS * TOK * D)
    for copy in small_out:
        copy.start()
    pg_copy.wait()
    gt_copy.wait()

    def enc_copy(n):
        rows = pl.ds(pl.multiple_of(n * 256, 256), 256)
        return pltpu.make_async_copy(
            enc_out.at[rows, :], enc_grad.at[rows, :], enc_sem.at[n]
        )

    @pl.loop(0, 8, unroll=4)
    def _(n):
        rows = pl.ds(pl.multiple_of(n * 256, 256), 256)
        enc_out[rows, :] = jnp.dot(
            gt[rows, :], pg[...], preferred_element_type=F32
        ).astype(BF16)
        enc_copy(n).start()

    for t in (0, 1):
        for m in range(8):
            dec_copy(t, m).wait()
    for n in range(8):
        enc_copy(n).wait()
    for copy in small_out:
        copy.wait()


def on_device(tokens_in, targets, enc_weight, enc_bias, dec_weight):
    anywhere = pl.BlockSpec(memory_space=pl.ANY)
    shape = jax.ShapeDtypeStruct
    blocks = (2, 2, 4, 4, ROWS, COLS)
    rerr, squares, gt, ft, s, pg, bg = pl.pallas_call(
        step_kernel,
        out_shape=(
            shape((ROWS, COLS), F32),
            shape((8, 128), F32),
            shape((D, TOK), BF16),
            shape((SHARD, TOK), BF16),
            shape((2, *blocks), BF16),
            shape((TOK, SHARD), BF16),
            shape((1, SHARD), F32),
        ),
        in_specs=[anywhere] * 5,
        out_specs=[anywhere] * 7,
        scratch_shapes=[
            pltpu.VMEM((ROWS, COLS), BF16),
            pltpu.VMEM((1, SHARD), F32),
            pltpu.VMEM((ROWS, COLS), F32),
            pltpu.VMEM((1, SHARD), F32),
            pltpu.VMEM((D, SHARD), BF16),
            pltpu.VMEM((2, SHARD, D), BF16),
            pltpu.VMEM((1, *blocks), BF16),
            pltpu.VMEM((TOK, SHARD), F32),
            pltpu.VMEM((TOK, SHARD), BF16),
            pltpu.VMEM((2, *blocks), BF16),
            pltpu.VMEM((2, 2, 4, 4, ROWS, COLS), BF16),
            pltpu.VMEM((2, 2, 2, 2, ROWS, COLS), BF16),
            pltpu.VMEM((2, 2, 4, 2, ROWS, COLS), BF16),
            pltpu.VMEM((2, 2, 4, ROWS, COLS), BF16),
            pltpu.VMEM((2, 3, ROWS, COLS), BF16),
            pltpu.VMEM((2, ROWS, COLS), BF16),
            pltpu.VMEM((7, ROWS, COLS), BF16),
            pltpu.VMEM((2, ROWS, COLS), BF16),
            pltpu.VMEM((2, *blocks), BF16),
            pltpu.VMEM((TOK, SHARD), F32),
            pltpu.VMEM((D, TOK), BF16),
            pltpu.VMEM((SHARD, TOK), BF16),
            pltpu.VMEM((TOK, SHARD), BF16),
            pltpu.VMEM((4, 4, 8, 128), F32),
            pltpu.VMEM((5, 8, 128), F32),
            pltpu.SemaphoreType.DMA((K_COUNT,)),
            pltpu.SemaphoreType.DMA((K_COUNT,)),
            pltpu.SemaphoreType.DMA((14,)),
        ],
        compiler_params=pltpu.CompilerParams(
            collective_id=0, has_side_effects=True, vmem_limit_bytes=60 * 2**20
        ),
        name="step",
    )(tokens_in, targets, enc_weight, enc_bias.reshape(1, SHARD), dec_weight)

    dec_grad, enc_grad, rerr, mean, bg = pl.pallas_call(
        weight_grads_kernel,
        out_shape=(
            shape((2, SHARD, D), BF16),
            shape((D, SHARD), BF16),
            shape((ROWS, COLS), F32),
            shape((1, 1), F32),
            shape((1, SHARD), F32),
        ),
        in_specs=[anywhere] * 7,
        out_specs=[anywhere] * 5,
        scratch_shapes=[
            pltpu.VMEM((D, TOK), BF16),
            pltpu.VMEM((SHARD, TOK), BF16),
            pltpu.VMEM((2, *blocks), BF16),
            pltpu.VMEM((TOK, SHARD), BF16),
            pltpu.VMEM((ROWS, COLS), F32),
            pltpu.VMEM((8, 128), F32),
            pltpu.VMEM((1, 1), F32),
            pltpu.VMEM((1, SHARD), F32),
            pltpu.VMEM((2, 8, SHARD, 256), BF16),
            pltpu.VMEM((D, SHARD), BF16),
            pltpu.SemaphoreType.DMA((7,)),
            pltpu.SemaphoreType.DMA((2, 8)),
            pltpu.SemaphoreType.DMA((8,)),
            pltpu.SemaphoreType.DMA((6,)),
        ],
        compiler_params=pltpu.CompilerParams(vmem_limit_bytes=60 * 2**20),
        name="weight_grads",
    )(gt, ft, s, pg, rerr, squares, bg)
    return (rerr, mean.reshape(()), enc_grad, bg.reshape(SHARD), dec_grad)


def solution(mesh):
    placed = (
        P("feat", "layer"),
        P("feat", "layer"),
        P(None, ("layer", "feat")),
        P(("layer", "feat")),
        P(None, ("layer", "feat"), None),
    )
    return jax.shard_map(
        on_device,
        mesh=mesh,
        in_specs=placed,
        out_specs=(
            P("feat", "layer"),
            P(),
            P(None, ("layer", "feat")),
            P(("layer", "feat")),
            P(None, ("layer", "feat"), None),
        ),
        check_vma=False,
    )
```

```python
import jax
import jax.numpy as jnp
from jax import lax
from jax.experimental import pallas as pl
from jax.experimental.pallas import tpu as pltpu
from jax.sharding import PartitionSpec as P

D = 2048
LAYERS = 2
TOK = 512
SHARD = 1024
ROWS = 64
COLS = 256
LOSS_SCALE = 64.0
MESH = pl.DeviceIdType.MESH
PASS = (0, 1)
ORDER = (0, 1)
EARLY = True
EARLY1 = True
BF16 = jnp.bfloat16
F32 = jnp.float32


def place(x, y, z, core):
    return (y * 4 + lax.div(z, 2) * 2 + core, x * 2 + lax.rem(z, 2))


def block_at(half, z, x):
    return z * (1 - half) + x * half, x * (1 - half) + z * half


def column_block(ref, lead, half, z_high, core):
    pieces = []
    for x in range(4):
        for z_low in range(2):
            big, small = block_at(half, z_high * 2 + z_low, x)
            pieces.append(ref[(*lead, half, core, big, small)])
    return jnp.concatenate(pieces, 0)


def core_columns(ref, lead, core):
    return jnp.concatenate(
        [column_block(ref, lead, m // 2, m % 2, core) for m in range(4)], 1
    )


def all_columns(ref, lead):
    return jnp.concatenate(
        [column_block(ref, lead, m // 4, m // 2 % 2, m % 2) for m in range(8)], 1
    )


def core_shards(core):
    return [pl.ds(pl.multiple_of((m * 2 + core) * 256, 256), 256) for m in range(4)]


class Numbers:
    def __init__(self):
        self.count = 0

    def take(self, *dims):
        if not dims:
            self.count += 1
            return self.count - 1
        return [self.take(*dims[1:]) for _ in range(dims[0])]


NUMBERS = Numbers()
def gather_numbers():
    return dict(
        small=NUMBERS.take(2),
        big=NUMBERS.take(2, 4),
        shared=NUMBERS.take(),
    )


K_GATHER = [gather_numbers(), gather_numbers()]
K_PART = NUMBERS.take(2, 2)
K_TURN = NUMBERS.take(2, 2)
K_BIG = NUMBERS.take(2, 2)
K_SMALL = NUMBERS.take(2)
K_FINAL = NUMBERS.take()
K_CROSS = NUMBERS.take(2)
K_BACK = NUMBERS.take(2)
K_PASS = NUMBERS.take(2)
K_SQUARE = NUMBERS.take(4)
K_COUNT = NUMBERS.count


def step_kernel(
    tok, tgt_in, enc, bias_in, dec,
    rerr_out, squares_out, gt_out, ft_out, s_out, pg_out, bg_out,
    tgt, bias, rerr, bg, encv, decv, g, pre, feat, p, rc, turn_in, big_in, r1, small_in, r2, final_in, cross_in,
    s, fg, gt, ft, pg, squares_in, squares_own, send_sem, recv_sem, local_sem,
):
    me_layer = lax.axis_index("layer")
    me_feat = lax.axis_index("feat")
    core = lax.rem(me_layer, 2)
    y = lax.div(me_layer, 4)
    x = lax.div(me_feat, 2)
    z = lax.rem(lax.div(me_layer, 2), 2) * 2 + lax.rem(me_feat, 2)
    yb = lax.rem(y, 2)
    first_layer = y < 2
    second_layer = y >= 2

    def turn(v, step):
        return lax.rem(v + step, 4)

    partner = place(x, y, z, 1 - core)
    y_pair = y + 1 - 2 * yb
    x_peers = [None] + [place(turn(x, o), y, z, core) for o in (1, 2, 3)]
    y_peers = [None] + [place(x, turn(y, o), z, core) for o in (1, 2, 3)]
    z_peers = [None] + [place(x, y, turn(z, o), core) for o in (1, 2, 3)]
    big_pos, small_pos = (z, x), (x, z)
    big_peers, small_peers = (z_peers, x_peers), (x_peers, z_peers)
    pair_peers = (
        [place(turn(x, o), y_pair, z, core) for o in range(4)],
        [place(x, y_pair, turn(z, o), core) for o in range(4)],
    )
    HALVES = (0, 1)
    OFFSETS = (2, 1, 3)

    def send(src, dst, number, device):
        return pltpu.make_async_remote_copy(
            src_ref=src,
            dst_ref=dst,
            send_sem=send_sem.at[number],
            recv_sem=recv_sem.at[number],
            device_id=device,
            device_id_type=MESH,
        )

    def own_block(buf):
        big, small = block_at(yb, z, x)
        return buf.at[0, yb, core, big, small]

    enc_copy = pltpu.make_async_copy(enc, encv, local_sem.at[0])
    dec_copy = pltpu.make_async_copy(dec, decv, local_sem.at[1])
    tok_copy = pltpu.make_async_copy(tok, own_block(g), local_sem.at[2])
    tgt_copy = pltpu.make_async_copy(tgt_in, tgt, local_sem.at[3])
    bias_copy = pltpu.make_async_copy(bias_in, bias, local_sem.at[4])
    tok_copy.start()
    enc_copy.start()
    dec_copy.start()
    tgt_copy.start()
    bias_copy.start()

    barrier = pltpu.get_barrier_semaphore()
    for device in (
        partner,
        *x_peers[1:],
        *y_peers[1:],
        *z_peers[1:],
        *pair_peers[0][1:],
        *pair_peers[1][1:],
    ):
        pl.semaphore_signal(barrier, inc=1, device_id=device, device_id_type=MESH)
    tok_copy.wait()
    pl.semaphore_wait(barrier, 16)

    class Gather:
        def __init__(self, buf, t, numbers, offsets=(OFFSETS, OFFSETS)):
            self.buf, self.t, self.numbers = buf, t, numbers
            self.offsets = offsets

        def piece(self, half):
            return self.buf.at[self.t, half, core, big_pos[half], small_pos[half]]

        def chunk(self, half, i):
            return self.buf.at[self.t, half, core, i]

        def small_copy(self, half, o):
            ref = self.piece(half)
            return send(ref, ref, self.numbers["small"][half], small_peers[half][o])

        def pair_copy(self, half, o):
            ref = self.piece(half)
            return send(ref, ref, self.numbers["small"][half], pair_peers[half][o])

        def all_small(self, half, count=3):
            ref = self.buf.at[self.t, half, core, 0, 0:count]
            return send(ref, ref, self.numbers["small"][half], partner)

        def all_joint(self, half):
            return send(final_in, final_in, self.numbers["small"][half], partner)

        def joint(self, mine, other):
            for o in (2, 1, 3, 0):
                self.pair_copy(mine, o).start()
                if o > 0:
                    self.small_copy(mine, o).start()
            if EARLY:
                self.early(mine)

        def big_copy(self, half, o):
            ref = self.chunk(half, big_pos[half])
            return send(ref, ref, self.numbers["big"][half][o], big_peers[half][o])

        def piece_copy(self, half, o, i):
            ref = self.buf.at[self.t, half, core, big_pos[half], i]
            return send(ref, ref, self.numbers["big"][half][o], big_peers[half][o])

        def early(self, half):
            for o in self.offsets[half]:
                self.piece_copy(half, o, small_pos[half]).start()

        def shared_copy(self, half, o):
            ref = self.chunk(half, turn(big_pos[half], 4 - o))
            return send(ref, ref, self.numbers["shared"], partner)

        def all_shared(self, of_core):
            ref = self.buf.at[self.t, :, of_core]
            return send(ref, ref, self.numbers["shared"], partner)

        def small(self, half):
            for o in OFFSETS:
                self.small_copy(half, o).start()

        def big(self, half, count=3, early=False):
            self.all_small(half, count).wait_recv()
            for o in self.offsets[half]:
                if not early:
                    self.big_copy(half, o).start()
                for d in OFFSETS if early else ():
                    self.piece_copy(half, o, turn(small_pos[half], d)).start()
            self.shared_copy(half, 0).start()

        def share(self, half):
            for o in self.offsets[half]:
                self.big_copy(half, o).wait_recv()
                self.shared_copy(half, o).start()

        def done(self):
            self.all_shared(1 - core).wait_recv()

        def drain(self, joint):
            if joint:
                by_half(lambda mine, other: self.all_joint(mine).wait_send())
            for half in HALVES:
                if not joint:
                    self.all_small(half).wait_send()
                for o in self.offsets[half]:
                    self.big_copy(half, o).wait_send()
            self.all_shared(core).wait_send()

    def by_half(fn):
        @pl.when(yb == 0)
        def _():
            fn(0, 1)

        @pl.when(yb == 1)
        def _():
            fn(1, 0)

    tokens = Gather(g, 0, K_GATHER[0])
    by_half(tokens.joint)

    def big_hops(gather):
        def run(mine, other):
            gather.big(mine, 3, EARLY)
            gather.big(other, 4)

        return run

    by_half(big_hops(tokens))

    def share_hops(gather):
        def run(mine, other):
            gather.share(mine)
            gather.share(other)

        return run

    by_half(share_hops(tokens))
    enc_copy.wait()
    bias_copy.wait()

    def encode_part(from_core, n):
        cols = pl.ds(pl.multiple_of(n * 256, 256), 256)
        weights = jnp.concatenate([encv[rows, cols] for rows in core_shards(from_core)], 0)
        return cols, jnp.dot(
            core_columns(g, (0,), from_core), weights, preferred_element_type=F32
        )

    @pl.loop(0, 4, unroll=4)
    def _(n):
        cols, value = encode_part(core, n)
        pre[:, cols] = value + bias[:, cols]

    tokens.done()

    @pl.loop(0, 4, unroll=4)
    def _(n):
        cols, value = encode_part(1 - core, n)
        act = pre[:, cols] + value
        pre[:, cols] = act
        feat[:, cols] = jnp.maximum(act, 0.0).astype(BF16)

    dec_copy.wait()

    def decode(t, to_core, half):
        firsts = [
            pl.multiple_of((half * 4 + z_high * 2 + to_core) * 256, 256) for z_high in range(2)
        ]
        weights = jnp.concatenate([decv[t, :, pl.ds(first, 256)] for first in firsts], 1)
        value = jnp.dot(feat[...], weights, preferred_element_type=F32).astype(BF16)
        for z_high in range(2):
            for to_x in range(4):
                for z_low in range(2):
                    big, small = block_at(half, z_high * 2 + z_low, to_x)
                    at = (to_x * 2 + z_low) * ROWS
                    p[t, half, to_core, big, small] = value[
                        at : at + ROWS, z_high * 256 : z_high * 256 + 256
                    ]

    def part_copy(t, half):
        return send(p.at[t, half, 1 - core], rc.at[t, half], K_PART[t][half], partner)

    def part_add(t, half):
        part_copy(t, half).wait_recv()

        @pl.loop(0, 4)
        def _(b):
            p[t, half, core, b] = (
                p[t, half, core, b].astype(F32) + rc[t, half, b].astype(F32)
            ).astype(BF16)

    LOW, HIGH = pl.ds(0, 2), pl.ds(2, 2)

    def chunk_sum(t, half, o, part):
        return p.at[t, half, core, turn(big_pos[half], o), part]

    def turn_copies(t, half):
        return [
            send(
                chunk_sum(t, half, 2, part),
                turn_in.at[t, half, i],
                K_TURN[t][half],
                big_peers[half][o],
            )
            for i, (part, o) in enumerate(((LOW, 1), (HIGH, 3)))
        ]

    def direct_copies(t, half):
        return [
            send(
                chunk_sum(t, half, o, part), big_in.at[t, half, i], K_BIG[t][half], big_peers[half][o]
            )
            for i, part, o in ((0, LOW, 3), (2, HIGH, 1))
        ]

    def summed_copies(t, half):
        return [
            send(
                chunk_sum(t, half, o, part), big_in.at[t, half, i], K_BIG[t][half], big_peers[half][o]
            )
            for i, part, o in ((1, LOW, 1), (3, HIGH, 3))
        ]

    def all_turns(t, half):
        return send(turn_in.at[t, half], turn_in.at[t, half], K_TURN[t][half], partner)

    def all_big_sums(t, half):
        return send(big_in.at[t, half], big_in.at[t, half], K_BIG[t][half], partner)

    def big_start(t, half):
        for copy in (*turn_copies(t, half), *direct_copies(t, half)):
            copy.start()

    def big_mid(t, half):
        all_turns(t, half).wait_recv()
        for i, (part, o) in enumerate(((LOW, 1), (HIGH, 3))):
            ref = chunk_sum(t, half, o, part)
            ref[...] = (ref[...].astype(F32) + turn_in[t, half, i].astype(F32)).astype(BF16)
            summed_copies(t, half)[i].start()

    def big_sum(t, half):
        all_big_sums(t, half).wait_recv()
        for i in range(4):
            first = i // 2 * 2
            r1[t, half, i] = (
                p[t, half, core, big_pos[half], i].astype(F32)
                + big_in[t, half, first, i % 2].astype(F32)
                + big_in[t, half, first + 1, i % 2].astype(F32)
            ).astype(BF16)

    def small_sum_copy(half, o):
        return send(
            r1.at[1, half, turn(small_pos[half], o)],
            small_in.at[half, o - 1],
            K_SMALL[half],
            small_peers[half][o],
        )

    def all_small_sums(half):
        return send(r1.at[1, half, 0:3], small_in.at[half], K_SMALL[half], partner)

    def final_copy(half, o, pair):
        return send(
            r1.at[0, half, turn(small_pos[half], o)],
            final_in.at[3 + o if pair else o - 1],
            K_FINAL,
            (pair_peers if pair else small_peers)[half][o],
        )

    def final_mine(mine, other):
        for o in OFFSETS:
            final_copy(mine, o, False).start()

    def final_other(mine, other):
        for o in (2, 1, 3, 0):
            final_copy(other, o, True).start()

    all_finals = send(final_in, final_in, K_FINAL, partner)

    def decode_slot(t, between=None):
        for half in HALVES:
            decode(t, 1 - core, half)
            part_copy(t, half).start()
        for half in HALVES:
            decode(t, core, half)
            part_add(t, half)
            if between is None:
                big_start(t, half)
        if between is not None:
            between()
            for half in HALVES:
                big_start(t, half)

    def small_sum(half):
        all_small_sums(half).wait_recv()
        value = r1[1, half, small_pos[half]].astype(F32)
        for o in OFFSETS:
            value = value + small_in[half, o - 1].astype(F32)
        r2[half] = value.astype(BF16)

    def cross_send(half, from_y):
        return send(
            r2.at[half],
            cross_in.at[from_y],
            K_CROSS[from_y],
            place(x, 2 + half, z, core),
        )

    @pl.when(first_layer)
    def _():
        decode_slot(1)

    def first_turns():
        @pl.when(first_layer)
        def _():
            for half in HALVES:
                big_mid(1, half)

    decode_slot(0, first_turns)

    @pl.loop(0, 4)
    def _(n):
        cols = pl.ds(pl.multiple_of(n * 256, 256), 256)
        ft[cols, :] = feat[:, cols].T

    ft_store = pltpu.make_async_copy(ft, ft_out, local_sem.at[0])
    ft_store.start()

    for half in HALVES:

        @pl.loop(0, 4)
        def _(m):
            z_high, to_core = lax.div(m, 2), lax.rem(m, 2)
            block = column_block(g, (0,), half, z_high, to_core)
            rows = pl.ds(pl.multiple_of((half * 4 + m) * 256, 256), 256)
            gt[rows, :] = block.T

    gt_store = pltpu.make_async_copy(gt, gt_out, local_sem.at[1])
    gt_store.start()

    @pl.when(first_layer)
    def _():
        for half in HALVES:
            big_sum(1, half)
            for o in OFFSETS:
                small_sum_copy(half, o).start()

    for half in HALVES:
        big_mid(0, half)

    @pl.when(first_layer)
    def _():
        for half in HALVES:
            small_sum(half)
            for from_y in (0, 1):

                @pl.when(yb == from_y)
                def _():
                    cross_send(half, from_y).start()

    def last_sums(mine, other):
        big_sum(0, other)
        final_other(mine, other)
        big_sum(0, mine)
        final_mine(mine, other)

    by_half(last_sums)

    tokens.drain(True)
    s0 = Gather(s, 0, K_GATHER[0])
    s1 = Gather(
        s, 1, K_GATHER[1], [(1, 3) if half in PASS else OFFSETS for half in HALVES]
    )

    def back_copy(to_y, half):
        big, small = block_at(half, z, x)
        return send(
            own_block(s),
            s.at[1, half, core, big, small],
            K_BACK[half],
            place(x, to_y, z, core),
        )

    def pass_copy(half):
        opposite = turn(big_pos[half], 2)
        return send(
            s.at[0, half, core, opposite],
            s.at[1, half, core, opposite],
            K_PASS[half],
            place(x, 3 - y, z, core),
        )

    tgt_copy.wait()
    all_finals.wait_recv()
    total = r1[0, yb, block_at(yb, z, x)[1]].astype(F32) - tgt[...].astype(F32)
    for i in range(7):
        total = total + final_in[i].astype(F32)
    rerr[...] = total

    @pl.when(second_layer)
    def _():
        for from_y in (0, 1):
            cross_send(0, from_y).wait_recv()
        rerr[...] = rerr[...] + cross_in[0].astype(F32) + cross_in[1].astype(F32)

    error = rerr[...]
    own_s = own_block(s)
    own_s[...] = (LOSS_SCALE / TOK * error).astype(BF16)

    @pl.when(second_layer)
    def _():
        for half in HALVES:

            @pl.when(yb == half)
            def _():
                for to_y in (0, 1):
                    back_copy(to_y, half).start()

    by_half(s0.joint)
    rerr_copy = pltpu.make_async_copy(rerr, rerr_out, local_sem.at[11])
    rerr_copy.start()

    square = error * error
    tile = jnp.zeros((8, 128), F32)
    for i in range(8):
        for j in range(2):
            tile = tile + square[i * 8 : i * 8 + 8, j * 128 : j * 128 + 128]

    def square_copy(stage, o):
        peers = ([None, partner], y_peers, x_peers, z_peers)[stage]
        pos = (core, y, x, z)[stage]
        return send(
            squares_own.at[stage], squares_in.at[stage, pos], K_SQUARE[stage], peers[o]
        )

    def square_offsets(stage):
        return (1, 2, 3) if stage > 0 else (1,)

    def all_squares(stage):
        ref = squares_in.at[stage, 0 : len(square_offsets(stage))]
        return send(ref, ref, K_SQUARE[stage], partner)

    def squares_start(stage, value):
        squares_own[stage] = value
        squares_in[stage, (core, y, x, z)[stage]] = value
        for o in square_offsets(stage):
            square_copy(stage, o).start()

    def squares_end(stage):
        all_squares(stage).wait_recv()
        value = squares_in[stage, 0]
        for i in range(1, 4 if stage > 0 else 2):
            value = value + squares_in[stage, i]
        return value

    squares_start(0, tile)

    def feature_grad(t, n):
        rows = pl.ds(pl.multiple_of(n * 256, 256), 256)
        return rows, lax.dot_general(
            all_columns(s, (t,)),
            decv[t, rows, :],
            (((1,), (1,)), ((), ())),
            preferred_element_type=F32,
        )

    def feature_grad_part(t, from_core, n):
        rows = pl.ds(pl.multiple_of(n * 256, 256), 256)
        weights = jnp.concatenate(
            [decv[t, rows, cols] for cols in core_shards(from_core)], 1
        )
        return rows, lax.dot_general(
            core_columns(s, (t,), from_core),
            weights,
            (((1,), (1,)), ((), ())),
            preferred_element_type=F32,
        )

    def pg_copy(n):
        cols = pl.ds(pl.multiple_of(n * 256, 256), 256)
        return pltpu.make_async_copy(pg.at[:, cols], pg_out.at[:, cols], local_sem.at[7 + n])

    def grad_first(t):
        @pl.loop(0, 4, unroll=4)
        def _(n):
            cols, value = feature_grad(t, n)
            fg[:, cols] = value

    def grad_half(t, from_core, more):
        @pl.loop(0, 4, unroll=4)
        def _(n):
            cols, value = feature_grad_part(t, from_core, n)
            fg[:, cols] = fg[:, cols] + value if more else value

    def grad_last(t, from_core):
        @pl.loop(0, 4, unroll=4)
        def _(n):
            cols, value = feature_grad_part(t, from_core, n)
            grad = jnp.where(pre[:, cols] > 0.0, fg[:, cols] + value, 0.0).astype(BF16)
            pg[:, cols] = grad
            bg[:, cols] = jnp.sum(grad.astype(F32), 0, keepdims=True)
            pg_copy(n).start()

    @pl.when(first_layer)
    def _():
        for half in HALVES:
            back_copy(0, half).wait_recv()
            s1.small(half)
            if EARLY1:
                s1.early(half)

    squares_start(1, squares_end(0))
    for t in ORDER:
        if t == 0:
            by_half(big_hops(s0))
        else:

            @pl.when(first_layer)
            def _():
                for half in HALVES:
                    s1.big(half, 3, EARLY1)

    stores = [
        pltpu.make_async_copy(s.at[t], s_out.at[t], local_sem.at[5 + t]) for t in (0, 1)
    ]

    def share_slot(t):
        if t == 0:
            for half in HALVES:
                s0.share(half)
        else:
            for half in HALVES:
                s1.share(half)
            for half in PASS:
                pass_copy(half).wait_recv()
                s1.shared_copy(half, 2).start()

    def done_slot(t):
        (s0, s1)[t].done()
        stores[t].start()

    @pl.when(second_layer)
    def _():
        for half in HALVES:
            s0.big_copy(half, 2).wait_recv()
            if half in PASS:
                pass_copy(half).start()
            s0.shared_copy(half, 2).start()
        for half in HALVES:
            for o in (1, 3):
                s0.big_copy(half, o).wait_recv()
                s0.shared_copy(half, o).start()

    @pl.when(first_layer)
    def _():
        share_slot(ORDER[0])
        done_slot(ORDER[0])

    squares_start(2, squares_end(1))
    @pl.when(first_layer)
    def _():
        grad_first(ORDER[0])

    @pl.when(first_layer)
    def _():
        share_slot(ORDER[1])

    squares_start(3, squares_end(2))

    @pl.when(first_layer)
    def _():
        grad_half(ORDER[1], core, True)

    @pl.when(second_layer)
    def _():
        grad_half(0, core, False)


    @pl.when(first_layer)
    def _():
        done_slot(ORDER[1])

    @pl.when(second_layer)
    def _():
        done_slot(0)

    @pl.when(first_layer)
    def _():
        grad_last(ORDER[1], 1 - core)

    @pl.when(second_layer)
    def _():
        grad_last(0, 1 - core)

    bg_copy = pltpu.make_async_copy(bg, bg_out, local_sem.at[13])
    bg_copy.start()
    squares_own[4] = squares_end(3)
    squares_copy = pltpu.make_async_copy(squares_own.at[4], squares_out, local_sem.at[12])
    squares_copy.start()

    def drain_sums(t):
        for half in HALVES:
            part_copy(t, half).wait_send()
            all_turns(t, half).wait_send()
            all_big_sums(t, half).wait_send()

    drain_sums(0)
    all_finals.wait_send()
    s0.drain(True)
    for stage in range(4):
        all_squares(stage).wait_send()

    @pl.when(first_layer)
    def _():
        drain_sums(1)
        s1.drain(False)
        for half in HALVES:
            all_small_sums(half).wait_send()
            for from_y in (0, 1):

                @pl.when(yb == from_y)
                def _():
                    cross_send(half, from_y).wait_send()

        stores[1].wait()

    @pl.when(second_layer)
    def _():
        for half in HALVES:

            @pl.when(yb == half)
            def _():
                for to_y in (0, 1):
                    back_copy(to_y, half).wait_send()

            if half in PASS:
                pass_copy(half).wait_send()

    stores[0].wait()
    rerr_copy.wait()
    squares_copy.wait()
    bg_copy.wait()
    ft_store.wait()
    gt_store.wait()
    for n in range(4):
        pg_copy(n).wait()


def weight_grads_kernel(
    gt_in, ft_in, s_in, pg_in, rerr_in, squares_in, bg_in,
    dec_grad, enc_grad, rerr_out, mean_out, bg_out,
    gt, ft, s, pg, rerr, squares, mean, bg, dec_out, enc_out,
    in_sem, dec_sem, enc_sem, small_sem,
):
    y = lax.div(lax.axis_index("layer"), 4)
    first_layer = y < 2
    second_layer = y >= 2
    ft_copy = pltpu.make_async_copy(ft_in, ft, in_sem.at[0])
    s_copies = [
        [
            pltpu.make_async_copy(s_in.at[t, half], s.at[t, half], in_sem.at[1 + 2 * t + half])
            for half in (0, 1)
        ]
        for t in (0, 1)
    ]
    pg_copy = pltpu.make_async_copy(pg_in, pg, in_sem.at[5])
    gt_copy = pltpu.make_async_copy(gt_in, gt, in_sem.at[6])
    ft_copy.start()
    for copy in s_copies[0]:
        copy.start()

    small_in = [
        pltpu.make_async_copy(src, dst, small_sem.at[i])
        for i, (src, dst) in enumerate(((rerr_in, rerr), (squares_in, squares), (bg_in, bg)))
    ]
    small_out = [
        pltpu.make_async_copy(src, dst, small_sem.at[3 + i])
        for i, (src, dst) in enumerate(((rerr, rerr_out), (mean, mean_out), (bg, bg_out)))
    ]

    def dec_copy(t, m):
        cols = pl.ds(pl.multiple_of(m * 256, 256), 256)
        return pltpu.make_async_copy(
            dec_out.at[t, m], dec_grad.at[t, :, cols], dec_sem.at[t, m]
        )

    def dec_half(t, half):
        s_copies[t][half].wait()

        @pl.loop(0, 4, unroll=4)
        def _(i):
            m = half * 4 + i
            block = column_block(s, (t,), half, lax.div(i, 2), lax.rem(i, 2))
            dec_out[t, m] = jnp.dot(
                ft[...], block, preferred_element_type=F32
            ).astype(BF16)
            dec_copy(t, m).start()

    ft_copy.wait()

    @pl.when(first_layer)
    def _():
        for copy in s_copies[1]:
            copy.start()

    gt_copy.start()
    pg_copy.start()
    for copy in small_in:
        copy.start()
    dec_half(0, 0)
    dec_half(0, 1)

    @pl.when(first_layer)
    def _():
        dec_half(1, 0)
        dec_half(1, 1)

    @pl.when(second_layer)
    def _():
        @pl.loop(0, 8)
        def _(m):
            dec_out[1, m] = jnp.zeros((SHARD, 256), BF16)
            dec_copy(1, m).start()

    for copy in small_in:
        copy.wait()
    mean[...] = jnp.sum(squares[...], keepdims=True) / (LAYERS * TOK * D)
    for copy in small_out:
        copy.start()
    pg_copy.wait()
    gt_copy.wait()

    def enc_copy(n):
        rows = pl.ds(pl.multiple_of(n * 256, 256), 256)
        return pltpu.make_async_copy(
            enc_out.at[rows, :], enc_grad.at[rows, :], enc_sem.at[n]
        )

    @pl.loop(0, 8, unroll=4)
    def _(n):
        rows = pl.ds(pl.multiple_of(n * 256, 256), 256)
        enc_out[rows, :] = jnp.dot(
            gt[rows, :], pg[...], preferred_element_type=F32
        ).astype(BF16)
        enc_copy(n).start()

    for t in (0, 1):
        for m in range(8):
            dec_copy(t, m).wait()
    for n in range(8):
        enc_copy(n).wait()
    for copy in small_out:
        copy.wait()


def on_device(tokens_in, targets, enc_weight, enc_bias, dec_weight):
    anywhere = pl.BlockSpec(memory_space=pl.ANY)
    shape = jax.ShapeDtypeStruct
    blocks = (2, 2, 4, 4, ROWS, COLS)
    rerr, squares, gt, ft, s, pg, bg = pl.pallas_call(
        step_kernel,
        out_shape=(
            shape((ROWS, COLS), F32),
            shape((8, 128), F32),
            shape((D, TOK), BF16),
            shape((SHARD, TOK), BF16),
            shape((2, *blocks), BF16),
            shape((TOK, SHARD), BF16),
            shape((1, SHARD), F32),
        ),
        in_specs=[anywhere] * 5,
        out_specs=[anywhere] * 7,
        scratch_shapes=[
            pltpu.VMEM((ROWS, COLS), BF16),
            pltpu.VMEM((1, SHARD), F32),
            pltpu.VMEM((ROWS, COLS), F32),
            pltpu.VMEM((1, SHARD), F32),
            pltpu.VMEM((D, SHARD), BF16),
            pltpu.VMEM((2, SHARD, D), BF16),
            pltpu.VMEM((1, *blocks), BF16),
            pltpu.VMEM((TOK, SHARD), F32),
            pltpu.VMEM((TOK, SHARD), BF16),
            pltpu.VMEM((2, *blocks), BF16),
            pltpu.VMEM((2, 2, 4, 4, ROWS, COLS), BF16),
            pltpu.VMEM((2, 2, 2, 2, ROWS, COLS), BF16),
            pltpu.VMEM((2, 2, 4, 2, ROWS, COLS), BF16),
            pltpu.VMEM((2, 2, 4, ROWS, COLS), BF16),
            pltpu.VMEM((2, 3, ROWS, COLS), BF16),
            pltpu.VMEM((2, ROWS, COLS), BF16),
            pltpu.VMEM((7, ROWS, COLS), BF16),
            pltpu.VMEM((2, ROWS, COLS), BF16),
            pltpu.VMEM((2, *blocks), BF16),
            pltpu.VMEM((TOK, SHARD), F32),
            pltpu.VMEM((D, TOK), BF16),
            pltpu.VMEM((SHARD, TOK), BF16),
            pltpu.VMEM((TOK, SHARD), BF16),
            pltpu.VMEM((4, 4, 8, 128), F32),
            pltpu.VMEM((5, 8, 128), F32),
            pltpu.SemaphoreType.DMA((K_COUNT,)),
            pltpu.SemaphoreType.DMA((K_COUNT,)),
            pltpu.SemaphoreType.DMA((14,)),
        ],
        compiler_params=pltpu.CompilerParams(
            collective_id=0, has_side_effects=True, vmem_limit_bytes=60 * 2**20
        ),
        name="step",
    )(tokens_in, targets, enc_weight, enc_bias.reshape(1, SHARD), dec_weight)

    dec_grad, enc_grad, rerr, mean, bg = pl.pallas_call(
        weight_grads_kernel,
        out_shape=(
            shape((2, SHARD, D), BF16),
            shape((D, SHARD), BF16),
            shape((ROWS, COLS), F32),
            shape((1, 1), F32),
            shape((1, SHARD), F32),
        ),
        in_specs=[anywhere] * 7,
        out_specs=[anywhere] * 5,
        scratch_shapes=[
            pltpu.VMEM((D, TOK), BF16),
            pltpu.VMEM((SHARD, TOK), BF16),
            pltpu.VMEM((2, *blocks), BF16),
            pltpu.VMEM((TOK, SHARD), BF16),
            pltpu.VMEM((ROWS, COLS), F32),
            pltpu.VMEM((8, 128), F32),
            pltpu.VMEM((1, 1), F32),
            pltpu.VMEM((1, SHARD), F32),
            pltpu.VMEM((2, 8, SHARD, 256), BF16),
            pltpu.VMEM((D, SHARD), BF16),
            pltpu.SemaphoreType.DMA((7,)),
            pltpu.SemaphoreType.DMA((2, 8)),
            pltpu.SemaphoreType.DMA((8,)),
            pltpu.SemaphoreType.DMA((6,)),
        ],
        compiler_params=pltpu.CompilerParams(vmem_limit_bytes=60 * 2**20),
        name="weight_grads",
    )(gt, ft, s, pg, rerr, squares, bg)
    return (rerr, mean.reshape(()), enc_grad, bg.reshape(SHARD), dec_grad)


def solution(mesh):
    placed = (
        P("feat", "layer"),
        P("feat", "layer"),
        P(None, ("layer", "feat")),
        P(("layer", "feat")),
        P(None, ("layer", "feat"), None),
    )
    return jax.shard_map(
        on_device,
        mesh=mesh,
        in_specs=placed,
        out_specs=(
            P("feat", "layer"),
            P(),
            P(None, ("layer", "feat")),
            P(("layer", "feat")),
            P(None, ("layer", "feat"), None),
        ),
        check_vma=False,
    )
```

```python
import jax
import jax.numpy as jnp
from jax import lax
from jax.experimental import pallas as pl
from jax.experimental.pallas import tpu as pltpu
from jax.sharding import PartitionSpec as P

D = 2048
LAYERS = 2
TOK = 512
SHARD = 1024
ROWS = 64
COLS = 256
LOSS_SCALE = 64.0
MESH = pl.DeviceIdType.MESH
PASS = (0, 1)
ORDER = (0, 1)
EARLY = True
EARLY1 = False
BF16 = jnp.bfloat16
F32 = jnp.float32


def place(x, y, z, core):
    return (y * 4 + lax.div(z, 2) * 2 + core, x * 2 + lax.rem(z, 2))


def block_at(half, z, x):
    return z * (1 - half) + x * half, x * (1 - half) + z * half


def column_block(ref, lead, half, z_high, core):
    pieces = []
    for x in range(4):
        for z_low in range(2):
            big, small = block_at(half, z_high * 2 + z_low, x)
            pieces.append(ref[(*lead, half, core, big, small)])
    return jnp.concatenate(pieces, 0)


def core_columns(ref, lead, core):
    return jnp.concatenate(
        [column_block(ref, lead, m // 2, m % 2, core) for m in range(4)], 1
    )


def all_columns(ref, lead):
    return jnp.concatenate(
        [column_block(ref, lead, m // 4, m // 2 % 2, m % 2) for m in range(8)], 1
    )


def core_shards(core):
    return [pl.ds(pl.multiple_of((m * 2 + core) * 256, 256), 256) for m in range(4)]


class Numbers:
    def __init__(self):
        self.count = 0

    def take(self, *dims):
        if not dims:
            self.count += 1
            return self.count - 1
        return [self.take(*dims[1:]) for _ in range(dims[0])]


NUMBERS = Numbers()
def gather_numbers():
    return dict(
        small=NUMBERS.take(2),
        big=NUMBERS.take(2, 3),
        shared=NUMBERS.take(),
    )


K_GATHER = [gather_numbers(), gather_numbers()]
K_PART = NUMBERS.take(2, 2)
K_TURN = NUMBERS.take(2, 2)
K_BIG = NUMBERS.take(2, 2)
K_SMALL = NUMBERS.take(2)
K_FINAL = NUMBERS.take()
K_CROSS = NUMBERS.take(2)
K_BACK = NUMBERS.take(2)
K_PASS = NUMBERS.take(2)
K_SQUARE = NUMBERS.take(4)
K_COUNT = NUMBERS.count


def step_kernel(
    tok, tgt_in, enc, bias_in, dec,
    rerr_out, squares_out, gt_out, ft_out, s_out, pg_out, bg_out,
    tgt, bias, rerr, bg, encv, decv, g, pre, feat, p, rc, turn_in, big_in, r1, small_in, r2, final_in, cross_in,
    s, fg, gt, ft, pg, squares_in, squares_own, send_sem, recv_sem, local_sem,
):
    me_layer = lax.axis_index("layer")
    me_feat = lax.axis_index("feat")
    core = lax.rem(me_layer, 2)
    y = lax.div(me_layer, 4)
    x = lax.div(me_feat, 2)
    z = lax.rem(lax.div(me_layer, 2), 2) * 2 + lax.rem(me_feat, 2)
    yb = lax.rem(y, 2)
    first_layer = y < 2
    second_layer = y >= 2

    def turn(v, step):
        return lax.rem(v + step, 4)

    partner = place(x, y, z, 1 - core)
    y_pair = y + 1 - 2 * yb
    x_peers = [None] + [place(turn(x, o), y, z, core) for o in (1, 2, 3)]
    y_peers = [None] + [place(x, turn(y, o), z, core) for o in (1, 2, 3)]
    z_peers = [None] + [place(x, y, turn(z, o), core) for o in (1, 2, 3)]
    big_pos, small_pos = (z, x), (x, z)
    big_peers, small_peers = (z_peers, x_peers), (x_peers, z_peers)
    pair_peers = (
        [place(turn(x, o), y_pair, z, core) for o in range(4)],
        [place(x, y_pair, turn(z, o), core) for o in range(4)],
    )
    HALVES = (0, 1)
    OFFSETS = (2, 1, 3)

    def send(src, dst, number, device):
        return pltpu.make_async_remote_copy(
            src_ref=src,
            dst_ref=dst,
            send_sem=send_sem,
            recv_sem=recv_sem.at[number],
            device_id=device,
            device_id_type=MESH,
        )

    def own_block(buf):
        big, small = block_at(yb, z, x)
        return buf.at[0, yb, core, big, small]

    enc_copy = pltpu.make_async_copy(enc, encv, local_sem.at[0])
    dec_copy = pltpu.make_async_copy(dec, decv, local_sem.at[1])
    tok_copy = pltpu.make_async_copy(tok, own_block(g), local_sem.at[2])
    tgt_copy = pltpu.make_async_copy(tgt_in, tgt, local_sem.at[3])
    bias_copy = pltpu.make_async_copy(bias_in, bias, local_sem.at[4])
    tok_copy.start()
    enc_copy.start()
    dec_copy.start()
    tgt_copy.start()
    bias_copy.start()

    barrier = pltpu.get_barrier_semaphore()
    for device in (
        partner,
        *x_peers[1:],
        *y_peers[1:],
        *z_peers[1:],
        *pair_peers[0][1:],
        *pair_peers[1][1:],
    ):
        pl.semaphore_signal(barrier, inc=1, device_id=device, device_id_type=MESH)
    tok_copy.wait()
    pl.semaphore_wait(barrier, 16)

    class Gather:
        def __init__(self, buf, t, numbers, offsets=(OFFSETS, OFFSETS)):
            self.buf, self.t, self.numbers = buf, t, numbers
            self.offsets = offsets

        def piece(self, half):
            return self.buf.at[self.t, half, core, big_pos[half], small_pos[half]]

        def chunk(self, half, i):
            return self.buf.at[self.t, half, core, i]

        def small_copy(self, half, o):
            ref = self.piece(half)
            return send(ref, ref, self.numbers["small"][half], small_peers[half][o])

        def pair_copy(self, half, o):
            ref = self.piece(half)
            return send(ref, ref, self.numbers["small"][half], pair_peers[half][o])

        def all_small(self, half, count=3):
            ref = self.buf.at[self.t, half, core, 0, 0:count]
            return send(ref, ref, self.numbers["small"][half], partner)

        def all_joint(self, half):
            return send(final_in, final_in, self.numbers["small"][half], partner)

        def joint(self, mine, other):
            for o in (2, 1, 3, 0):
                self.pair_copy(mine, o).start()
                if o > 0:
                    self.small_copy(mine, o).start()
            if EARLY:
                self.early(mine)

        def big_copy(self, half, o):
            ref = self.chunk(half, big_pos[half])
            return send(ref, ref, self.numbers["big"][half][o - 1], big_peers[half][o])

        def piece_copy(self, half, o, i):
            ref = self.buf.at[self.t, half, core, big_pos[half], i]
            return send(ref, ref, self.numbers["big"][half][o - 1], big_peers[half][o])

        def early(self, half):
            for o in self.offsets[half]:
                self.piece_copy(half, o, small_pos[half]).start()

        def shared_copy(self, half, o):
            ref = self.chunk(half, turn(big_pos[half], 4 - o))
            return send(ref, ref, self.numbers["shared"], partner)

        def all_shared(self, of_core):
            ref = self.buf.at[self.t, :, of_core]
            return send(ref, ref, self.numbers["shared"], partner)

        def small(self, half):
            for o in OFFSETS:
                self.small_copy(half, o).start()

        def big(self, half, count=3, early=False):
            self.all_small(half, count).wait_recv()
            for o in self.offsets[half]:
                if not early:
                    self.big_copy(half, o).start()
                for d in OFFSETS if early else ():
                    self.piece_copy(half, o, turn(small_pos[half], d)).start()
            self.shared_copy(half, 0).start()

        def share(self, half):
            for o in self.offsets[half]:
                self.big_copy(half, o).wait_recv()
                self.shared_copy(half, o).start()

        def done(self):
            self.all_shared(1 - core).wait_recv()

        def drain(self, joint):
            if joint:
                by_half(lambda mine, other: self.all_joint(mine).wait_send())
            for half in HALVES:
                if not joint:
                    self.all_small(half).wait_send()
                for o in self.offsets[half]:
                    self.big_copy(half, o).wait_send()
            self.all_shared(core).wait_send()

    def by_half(fn):
        @pl.when(yb == 0)
        def _():
            fn(0, 1)

        @pl.when(yb == 1)
        def _():
            fn(1, 0)

    tokens = Gather(g, 0, K_GATHER[0])
    by_half(tokens.joint)

    def big_hops(gather):
        def run(mine, other):
            gather.big(mine, 3, EARLY)
            gather.big(other, 4)

        return run

    by_half(big_hops(tokens))

    def share_hops(gather):
        def run(mine, other):
            gather.share(mine)
            gather.share(other)

        return run

    by_half(share_hops(tokens))
    enc_copy.wait()
    bias_copy.wait()

    def encode_part(from_core, n):
        cols = pl.ds(pl.multiple_of(n * 256, 256), 256)
        weights = jnp.concatenate([encv[rows, cols] for rows in core_shards(from_core)], 0)
        return cols, jnp.dot(
            core_columns(g, (0,), from_core), weights, preferred_element_type=F32
        )

    @pl.loop(0, 4, unroll=4)
    def _(n):
        cols, value = encode_part(core, n)
        pre[:, cols] = value + bias[:, cols]

    tokens.done()

    @pl.loop(0, 4, unroll=4)
    def _(n):
        cols, value = encode_part(1 - core, n)
        act = pre[:, cols] + value
        pre[:, cols] = act
        feat[:, cols] = jnp.maximum(act, 0.0).astype(BF16)

    dec_copy.wait()

    def decode(t, to_core, half):
        firsts = [
            pl.multiple_of((half * 4 + z_high * 2 + to_core) * 256, 256) for z_high in range(2)
        ]
        weights = jnp.concatenate([decv[t, :, pl.ds(first, 256)] for first in firsts], 1)
        value = jnp.dot(feat[...], weights, preferred_element_type=F32).astype(BF16)
        for z_high in range(2):
            for to_x in range(4):
                for z_low in range(2):
                    big, small = block_at(half, z_high * 2 + z_low, to_x)
                    at = (to_x * 2 + z_low) * ROWS
                    p[t, half, to_core, big, small] = value[
                        at : at + ROWS, z_high * 256 : z_high * 256 + 256
                    ]

    def part_copy(t, half):
        return send(p.at[t, half, 1 - core], rc.at[t, half], K_PART[t][half], partner)

    def part_add(t, half):
        part_copy(t, half).wait_recv()

        @pl.loop(0, 4)
        def _(b):
            p[t, half, core, b] = (
                p[t, half, core, b].astype(F32) + rc[t, half, b].astype(F32)
            ).astype(BF16)

    LOW, HIGH = pl.ds(0, 2), pl.ds(2, 2)

    def chunk_sum(t, half, o, part):
        return p.at[t, half, core, turn(big_pos[half], o), part]

    def turn_copies(t, half):
        return [
            send(
                chunk_sum(t, half, 2, part),
                turn_in.at[t, half, i],
                K_TURN[t][half],
                big_peers[half][o],
            )
            for i, (part, o) in enumerate(((LOW, 1), (HIGH, 3)))
        ]

    def direct_copies(t, half):
        return [
            send(
                chunk_sum(t, half, o, part), big_in.at[t, half, i], K_BIG[t][half], big_peers[half][o]
            )
            for i, part, o in ((0, LOW, 3), (2, HIGH, 1))
        ]

    def summed_copies(t, half):
        return [
            send(
                chunk_sum(t, half, o, part), big_in.at[t, half, i], K_BIG[t][half], big_peers[half][o]
            )
            for i, part, o in ((1, LOW, 1), (3, HIGH, 3))
        ]

    def all_turns(t, half):
        return send(turn_in.at[t, half], turn_in.at[t, half], K_TURN[t][half], partner)

    def all_big_sums(t, half):
        return send(big_in.at[t, half], big_in.at[t, half], K_BIG[t][half], partner)

    def big_start(t, half):
        for copy in (*turn_copies(t, half), *direct_copies(t, half)):
            copy.start()

    def big_mid(t, half):
        all_turns(t, half).wait_recv()
        for i, (part, o) in enumerate(((LOW, 1), (HIGH, 3))):
            ref = chunk_sum(t, half, o, part)
            ref[...] = (ref[...].astype(F32) + turn_in[t, half, i].astype(F32)).astype(BF16)
            summed_copies(t, half)[i].start()

    def big_sum(t, half):
        all_big_sums(t, half).wait_recv()
        for i in range(4):
            first = i // 2 * 2
            r1[t, half, i] = (
                p[t, half, core, big_pos[half], i].astype(F32)
                + big_in[t, half, first, i % 2].astype(F32)
                + big_in[t, half, first + 1, i % 2].astype(F32)
            ).astype(BF16)

    def small_sum_copy(half, o):
        return send(
            r1.at[1, half, turn(small_pos[half], o)],
            small_in.at[half, o - 1],
            K_SMALL[half],
            small_peers[half][o],
        )

    def all_small_sums(half):
        return send(r1.at[1, half, 0:3], small_in.at[half], K_SMALL[half], partner)

    def final_copy(half, o, pair):
        return send(
            r1.at[0, half, turn(small_pos[half], o)],
            final_in.at[3 + o if pair else o - 1],
            K_FINAL,
            (pair_peers if pair else small_peers)[half][o],
        )

    def final_mine(mine, other):
        for o in OFFSETS:
            final_copy(mine, o, False).start()

    def final_other(mine, other):
        for o in (2, 1, 3, 0):
            final_copy(other, o, True).start()

    all_finals = send(final_in, final_in, K_FINAL, partner)

    def decode_slot(t, between=None):
        for half in HALVES:
            decode(t, 1 - core, half)
            part_copy(t, half).start()
        for half in HALVES:
            decode(t, core, half)
            part_add(t, half)
            if between is None:
                big_start(t, half)
        if between is not None:
            between()
            for half in HALVES:
                big_start(t, half)

    def small_sum(half):
        all_small_sums(half).wait_recv()
        value = r1[1, half, small_pos[half]].astype(F32)
        for o in OFFSETS:
            value = value + small_in[half, o - 1].astype(F32)
        r2[half] = value.astype(BF16)

    def cross_send(half, from_y):
        return send(
            r2.at[half],
            cross_in.at[from_y],
            K_CROSS[from_y],
            place(x, 2 + half, z, core),
        )

    @pl.when(first_layer)
    def _():
        decode_slot(1)

    def first_turns():
        @pl.when(first_layer)
        def _():
            for half in HALVES:
                big_mid(1, half)

    decode_slot(0, first_turns)

    @pl.loop(0, 4)
    def _(n):
        cols = pl.ds(pl.multiple_of(n * 256, 256), 256)
        ft[cols, :] = feat[:, cols].T

    ft_store = pltpu.make_async_copy(ft, ft_out, local_sem.at[0])
    ft_store.start()

    for half in HALVES:

        @pl.loop(0, 4)
        def _(m):
            z_high, to_core = lax.div(m, 2), lax.rem(m, 2)
            block = column_block(g, (0,), half, z_high, to_core)
            rows = pl.ds(pl.multiple_of((half * 4 + m) * 256, 256), 256)
            gt[rows, :] = block.T

    gt_store = pltpu.make_async_copy(gt, gt_out, local_sem.at[1])
    gt_store.start()

    @pl.when(first_layer)
    def _():
        for half in HALVES:
            big_sum(1, half)
            for o in OFFSETS:
                small_sum_copy(half, o).start()

    for half in HALVES:
        big_mid(0, half)

    @pl.when(first_layer)
    def _():
        for half in HALVES:
            small_sum(half)
            for from_y in (0, 1):

                @pl.when(yb == from_y)
                def _():
                    cross_send(half, from_y).start()

    def last_sums(mine, other):
        big_sum(0, other)
        final_other(mine, other)
        big_sum(0, mine)
        final_mine(mine, other)

    by_half(last_sums)

    s0 = Gather(s, 0, K_GATHER[0])
    s1 = Gather(
        s, 1, K_GATHER[1], [(1, 3) if half in PASS else OFFSETS for half in HALVES]
    )

    def back_copy(to_y, half):
        big, small = block_at(half, z, x)
        return send(
            own_block(s),
            s.at[1, half, core, big, small],
            K_BACK[half],
            place(x, to_y, z, core),
        )

    def pass_copy(half):
        opposite = turn(big_pos[half], 2)
        return send(
            s.at[0, half, core, opposite],
            s.at[1, half, core, opposite],
            K_PASS[half],
            place(x, 3 - y, z, core),
        )

    tgt_copy.wait()
    all_finals.wait_recv()
    total = r1[0, yb, block_at(yb, z, x)[1]].astype(F32) - tgt[...].astype(F32)
    for i in range(7):
        total = total + final_in[i].astype(F32)
    rerr[...] = total

    @pl.when(second_layer)
    def _():
        for from_y in (0, 1):
            cross_send(0, from_y).wait_recv()
        rerr[...] = rerr[...] + cross_in[0].astype(F32) + cross_in[1].astype(F32)

    error = rerr[...]
    own_s = own_block(s)
    own_s[...] = (LOSS_SCALE / TOK * error).astype(BF16)

    @pl.when(second_layer)
    def _():
        for half in HALVES:

            @pl.when(yb == half)
            def _():
                for to_y in (0, 1):
                    back_copy(to_y, half).start()

    by_half(s0.joint)
    rerr_copy = pltpu.make_async_copy(rerr, rerr_out, local_sem.at[11])
    rerr_copy.start()

    square = error * error
    tile = jnp.zeros((8, 128), F32)
    for i in range(8):
        for j in range(2):
            tile = tile + square[i * 8 : i * 8 + 8, j * 128 : j * 128 + 128]

    def square_copy(stage, o):
        peers = ([None, partner], y_peers, x_peers, z_peers)[stage]
        pos = (core, y, x, z)[stage]
        return send(
            squares_own.at[stage], squares_in.at[stage, pos], K_SQUARE[stage], peers[o]
        )

    def square_offsets(stage):
        return (1, 2, 3) if stage > 0 else (1,)

    def all_squares(stage):
        ref = squares_in.at[stage, 0 : len(square_offsets(stage))]
        return send(ref, ref, K_SQUARE[stage], partner)

    def squares_start(stage, value):
        squares_own[stage] = value
        squares_in[stage, (core, y, x, z)[stage]] = value
        for o in square_offsets(stage):
            square_copy(stage, o).start()

    def squares_end(stage):
        all_squares(stage).wait_recv()
        value = squares_in[stage, 0]
        for i in range(1, 4 if stage > 0 else 2):
            value = value + squares_in[stage, i]
        return value

    squares_start(0, tile)

    def feature_grad(t, n):
        rows = pl.ds(pl.multiple_of(n * 256, 256), 256)
        return rows, lax.dot_general(
            all_columns(s, (t,)),
            decv[t, rows, :],
            (((1,), (1,)), ((), ())),
            preferred_element_type=F32,
        )

    def feature_grad_part(t, from_core, n):
        rows = pl.ds(pl.multiple_of(n * 256, 256), 256)
        weights = jnp.concatenate(
            [decv[t, rows, cols] for cols in core_shards(from_core)], 1
        )
        return rows, lax.dot_general(
            core_columns(s, (t,), from_core),
            weights,
            (((1,), (1,)), ((), ())),
            preferred_element_type=F32,
        )

    def pg_copy(n):
        cols = pl.ds(pl.multiple_of(n * 256, 256), 256)
        return pltpu.make_async_copy(pg.at[:, cols], pg_out.at[:, cols], local_sem.at[7 + n])

    def grad_first(t):
        @pl.loop(0, 4, unroll=4)
        def _(n):
            cols, value = feature_grad(t, n)
            fg[:, cols] = value

    def grad_half(t, from_core, more):
        @pl.loop(0, 4, unroll=4)
        def _(n):
            cols, value = feature_grad_part(t, from_core, n)
            fg[:, cols] = fg[:, cols] + value if more else value

    def grad_last(t, from_core):
        @pl.loop(0, 4, unroll=4)
        def _(n):
            cols, value = feature_grad_part(t, from_core, n)
            grad = jnp.where(pre[:, cols] > 0.0, fg[:, cols] + value, 0.0).astype(BF16)
            pg[:, cols] = grad
            bg[:, cols] = jnp.sum(grad.astype(F32), 0, keepdims=True)
            pg_copy(n).start()

    @pl.when(first_layer)
    def _():
        for half in HALVES:
            back_copy(0, half).wait_recv()
            s1.small(half)
            if EARLY1:
                s1.early(half)

    squares_start(1, squares_end(0))
    for t in ORDER:
        if t == 0:
            by_half(big_hops(s0))
        else:

            @pl.when(first_layer)
            def _():
                for half in HALVES:
                    s1.big(half, 3, EARLY1)

    stores = [
        pltpu.make_async_copy(s.at[t], s_out.at[t], local_sem.at[5 + t]) for t in (0, 1)
    ]

    def share_slot(t):
        if t == 0:
            for half in HALVES:
                s0.share(half)
        else:
            for half in HALVES:
                s1.share(half)
            for half in PASS:
                pass_copy(half).wait_recv()
                s1.shared_copy(half, 2).start()

    def done_slot(t):
        (s0, s1)[t].done()
        stores[t].start()

    @pl.when(second_layer)
    def _():
        for half in HALVES:
            s0.big_copy(half, 2).wait_recv()
            if half in PASS:
                pass_copy(half).start()
            s0.shared_copy(half, 2).start()
        for half in HALVES:
            for o in (1, 3):
                s0.big_copy(half, o).wait_recv()
                s0.shared_copy(half, o).start()

    @pl.when(first_layer)
    def _():
        share_slot(ORDER[0])
        done_slot(ORDER[0])

    squares_start(2, squares_end(1))
    @pl.when(first_layer)
    def _():
        grad_first(ORDER[0])

    @pl.when(first_layer)
    def _():
        share_slot(ORDER[1])

    squares_start(3, squares_end(2))

    @pl.when(first_layer)
    def _():
        grad_half(ORDER[1], core, True)

    @pl.when(second_layer)
    def _():
        grad_half(0, core, False)


    @pl.when(first_layer)
    def _():
        done_slot(ORDER[1])

    @pl.when(second_layer)
    def _():
        done_slot(0)

    @pl.when(first_layer)
    def _():
        grad_last(ORDER[1], 1 - core)

    @pl.when(second_layer)
    def _():
        grad_last(0, 1 - core)

    bg_copy = pltpu.make_async_copy(bg, bg_out, local_sem.at[13])
    bg_copy.start()
    squares_own[4] = squares_end(3)
    squares_copy = pltpu.make_async_copy(squares_own.at[4], squares_out, local_sem.at[12])
    squares_copy.start()

    def drain_sums(t):
        for half in HALVES:
            part_copy(t, half).wait_send()
            all_turns(t, half).wait_send()
            all_big_sums(t, half).wait_send()

    tokens.drain(True)
    drain_sums(0)
    all_finals.wait_send()
    s0.drain(True)
    for stage in range(4):
        all_squares(stage).wait_send()

    @pl.when(first_layer)
    def _():
        drain_sums(1)
        s1.drain(False)
        for half in HALVES:
            all_small_sums(half).wait_send()
            for from_y in (0, 1):

                @pl.when(yb == from_y)
                def _():
                    cross_send(half, from_y).wait_send()

        stores[1].wait()

    @pl.when(second_layer)
    def _():
        for half in HALVES:

            @pl.when(yb == half)
            def _():
                for to_y in (0, 1):
                    back_copy(to_y, half).wait_send()

            if half in PASS:
                pass_copy(half).wait_send()

    stores[0].wait()
    rerr_copy.wait()
    squares_copy.wait()
    bg_copy.wait()
    ft_store.wait()
    gt_store.wait()
    for n in range(4):
        pg_copy(n).wait()


def weight_grads_kernel(
    gt_in, ft_in, s_in, pg_in, rerr_in, squares_in, bg_in,
    dec_grad, enc_grad, rerr_out, mean_out, bg_out,
    gt, ft, s, pg, rerr, squares, mean, bg, dec_out, enc_out,
    first_sem, in_sem, dec_sem, enc_sem, small_sem,
):
    y = lax.div(lax.axis_index("layer"), 4)
    first_layer = y < 2
    second_layer = y >= 2
    ft_copies = [
        pltpu.make_async_copy(
            ft_in.at[pl.ds(i * 256, 256)], ft.at[pl.ds(i * 256, 256)], first_sem.at[i]
        )
        for i in range(4)
    ]
    s_copies = [
        [
            pltpu.make_async_copy(s_in.at[t, half], s.at[t, half], in_sem.at[1 + 2 * t + half])
            for half in (0, 1)
        ]
        for t in (0, 1)
    ]
    pg_copy = pltpu.make_async_copy(pg_in, pg, in_sem.at[5])
    gt_copy = pltpu.make_async_copy(gt_in, gt, in_sem.at[6])
    first_s_copies = [
        pltpu.make_async_copy(s_in.at[0, 0, c], s.at[0, 0, c], first_sem.at[4 + c])
        for c in (0, 1)
    ]
    for copy in (*ft_copies, *first_s_copies, s_copies[0][1]):
        copy.start()

    small_in = [
        pltpu.make_async_copy(src, dst, small_sem.at[i])
        for i, (src, dst) in enumerate(((rerr_in, rerr), (squares_in, squares), (bg_in, bg)))
    ]
    small_out = [
        pltpu.make_async_copy(src, dst, small_sem.at[3 + i])
        for i, (src, dst) in enumerate(((rerr, rerr_out), (mean, mean_out), (bg, bg_out)))
    ]

    def dec_copy(t, m):
        cols = pl.ds(pl.multiple_of(m * 256, 256), 256)
        return pltpu.make_async_copy(
            dec_out.at[t, m], dec_grad.at[t, :, cols], dec_sem.at[t, m]
        )

    def dec_half(t, half):
        if (t, half) != (0, 0):
            s_copies[t][half].wait()

        @pl.loop(0, 4, unroll=4)
        def _(i):
            m = half * 4 + i
            block = column_block(s, (t,), half, lax.div(i, 2), lax.rem(i, 2))
            dec_out[t, m] = jnp.dot(
                ft[...], block, preferred_element_type=F32
            ).astype(BF16)
            dec_copy(t, m).start()

    for copy in (*ft_copies, *first_s_copies):
        copy.wait()

    @pl.when(first_layer)
    def _():
        for copy in s_copies[1]:
            copy.start()

    gt_copy.start()
    pg_copy.start()
    for copy in small_in:
        copy.start()
    dec_half(0, 0)
    dec_half(0, 1)

    @pl.when(first_layer)
    def _():
        dec_half(1, 0)
        dec_half(1, 1)

    @pl.when(second_layer)
    def _():
        @pl.loop(0, 8)
        def _(m):
            dec_out[1, m] = jnp.zeros((SHARD, 256), BF16)
            dec_copy(1, m).start()

    for copy in small_in:
        copy.wait()
    mean[...] = jnp.sum(squares[...], keepdims=True) / (LAYERS * TOK * D)
    for copy in small_out:
        copy.start()
    pg_copy.wait()
    gt_copy.wait()

    def enc_copy(n):
        rows = pl.ds(pl.multiple_of(n * 256, 256), 256)
        return pltpu.make_async_copy(
            enc_out.at[rows, :], enc_grad.at[rows, :], enc_sem.at[n]
        )

    @pl.loop(0, 8, unroll=4)
    def _(n):
        rows = pl.ds(pl.multiple_of(n * 256, 256), 256)
        enc_out[rows, :] = jnp.dot(
            gt[rows, :], pg[...], preferred_element_type=F32
        ).astype(BF16)
        enc_copy(n).start()

    for t in (0, 1):
        for m in range(8):
            dec_copy(t, m).wait()
    for n in range(8):
        enc_copy(n).wait()
    for copy in small_out:
        copy.wait()


def on_device(tokens_in, targets, enc_weight, enc_bias, dec_weight):
    anywhere = pl.BlockSpec(memory_space=pl.ANY)
    shape = jax.ShapeDtypeStruct
    blocks = (2, 2, 4, 4, ROWS, COLS)
    rerr, squares, gt, ft, s, pg, bg = pl.pallas_call(
        step_kernel,
        out_shape=(
            shape((ROWS, COLS), F32),
            shape((8, 128), F32),
            shape((D, TOK), BF16),
            shape((SHARD, TOK), BF16),
            shape((2, *blocks), BF16),
            shape((TOK, SHARD), BF16),
            shape((1, SHARD), F32),
        ),
        in_specs=[anywhere] * 5,
        out_specs=[anywhere] * 7,
        scratch_shapes=[
            pltpu.VMEM((ROWS, COLS), BF16),
            pltpu.VMEM((1, SHARD), F32),
            pltpu.VMEM((ROWS, COLS), F32),
            pltpu.VMEM((1, SHARD), F32),
            pltpu.VMEM((D, SHARD), BF16),
            pltpu.VMEM((2, SHARD, D), BF16),
            pltpu.VMEM((1, *blocks), BF16),
            pltpu.VMEM((TOK, SHARD), F32),
            pltpu.VMEM((TOK, SHARD), BF16),
            pltpu.VMEM((2, *blocks), BF16),
            pltpu.VMEM((2, 2, 4, 4, ROWS, COLS), BF16),
            pltpu.VMEM((2, 2, 2, 2, ROWS, COLS), BF16),
            pltpu.VMEM((2, 2, 4, 2, ROWS, COLS), BF16),
            pltpu.VMEM((2, 2, 4, ROWS, COLS), BF16),
            pltpu.VMEM((2, 3, ROWS, COLS), BF16),
            pltpu.VMEM((2, ROWS, COLS), BF16),
            pltpu.VMEM((7, ROWS, COLS), BF16),
            pltpu.VMEM((2, ROWS, COLS), BF16),
            pltpu.VMEM((2, *blocks), BF16),
            pltpu.VMEM((TOK, SHARD), F32),
            pltpu.VMEM((D, TOK), BF16),
            pltpu.VMEM((SHARD, TOK), BF16),
            pltpu.VMEM((TOK, SHARD), BF16),
            pltpu.VMEM((4, 4, 8, 128), F32),
            pltpu.VMEM((5, 8, 128), F32),
            pltpu.SemaphoreType.DMA,
            pltpu.SemaphoreType.DMA((K_COUNT,)),
            pltpu.SemaphoreType.DMA((14,)),
        ],
        compiler_params=pltpu.CompilerParams(
            collective_id=0, has_side_effects=True, vmem_limit_bytes=60 * 2**20
        ),
        name="step",
    )(tokens_in, targets, enc_weight, enc_bias.reshape(1, SHARD), dec_weight)

    dec_grad, enc_grad, rerr, mean, bg = pl.pallas_call(
        weight_grads_kernel,
        out_shape=(
            shape((2, SHARD, D), BF16),
            shape((D, SHARD), BF16),
            shape((ROWS, COLS), F32),
            shape((1, 1), F32),
            shape((1, SHARD), F32),
        ),
        in_specs=[anywhere] * 7,
        out_specs=[anywhere] * 5,
        scratch_shapes=[
            pltpu.VMEM((D, TOK), BF16),
            pltpu.VMEM((SHARD, TOK), BF16),
            pltpu.VMEM((2, *blocks), BF16),
            pltpu.VMEM((TOK, SHARD), BF16),
            pltpu.VMEM((ROWS, COLS), F32),
            pltpu.VMEM((8, 128), F32),
            pltpu.VMEM((1, 1), F32),
            pltpu.VMEM((1, SHARD), F32),
            pltpu.VMEM((2, 8, SHARD, 256), BF16),
            pltpu.VMEM((D, SHARD), BF16),
            pltpu.SemaphoreType.DMA((6,)),
            pltpu.SemaphoreType.DMA((7,)),
            pltpu.SemaphoreType.DMA((2, 8)),
            pltpu.SemaphoreType.DMA((8,)),
            pltpu.SemaphoreType.DMA((6,)),
        ],
        compiler_params=pltpu.CompilerParams(vmem_limit_bytes=60 * 2**20),
        name="weight_grads",
    )(gt, ft, s, pg, rerr, squares, bg)
    return (rerr, mean.reshape(()), enc_grad, bg.reshape(SHARD), dec_grad)


def solution(mesh):
    placed = (
        P("feat", "layer"),
        P("feat", "layer"),
        P(None, ("layer", "feat")),
        P(("layer", "feat")),
        P(None, ("layer", "feat"), None),
    )
    return jax.shard_map(
        on_device,
        mesh=mesh,
        in_specs=placed,
        out_specs=(
            P("feat", "layer"),
            P(),
            P(None, ("layer", "feat")),
            P(("layer", "feat")),
            P(None, ("layer", "feat"), None),
        ),
        check_vma=False,
    )
```
